32 devices in a mesh: ctx: 4 (over z), fsdp: 8 (over y, x, core).
Axes of the slice: x: 2, y: 2, z: 4, core: 2. Of those that a mesh axis runs over, the one named last changes fastest.
Arguments:
- tokens: bfloat16 [8, 1024, 1024], P('fsdp', 'ctx'), may hold values from -10 to 10
- segment_ids: int32 [8, 1024], P('fsdp', 'ctx'), may hold values from 0 to 7, never falling along the last dimension, each value on 1 to 512 neighbouring positions
- cotangent: bfloat16 [8, 1024, 1024], P('fsdp', 'ctx'), may hold values from -6 to 6
- query_weight: bfloat16 [1024, 1024], P('fsdp'), may hold values from -0.1875 to 0.1875
- query_bias: bfloat16 [1024], P('fsdp'), may hold values from -3 to 3
- key_weight: bfloat16 [1024, 1024], P('fsdp'), may hold values from -0.1875 to 0.1875
- value_weight: bfloat16 [1024, 1024], P('fsdp'), may hold values from -0.1875 to 0.1875
- value_bias: bfloat16 [1024], P('fsdp'), may hold values from -3 to 3
- out_weight: bfloat16 [1024, 1024], P('fsdp'), may hold values from -0.75 to 0.75
- out_bias: bfloat16 [1024], P('fsdp'), may hold values from -3 to 3
- attn_gain: bfloat16 [1024], P('fsdp'), may hold values from 0.25 to 1.75
- attn_shift: bfloat16 [1024], P('fsdp'), may hold values from -2 to 2
- up_weight: bfloat16 [1024, 4096], P('fsdp'), may hold values from -0.1875 to 0.1875
- up_bias: bfloat16 [4096], P('fsdp'), may hold values from -3 to 3
- down_weight: bfloat16 [4096, 1024], P('fsdp'), may hold values from -0.09375 to 0.09375
- down_bias: bfloat16 [1024], P('fsdp'), may hold values from -3 to 3
- mlp_gain: bfloat16 [1024], P('fsdp'), may hold values from 0.25 to 1.75
- mlp_shift: bfloat16 [1024], P('fsdp'), may hold values from -2 to 2
Outputs:
- output: bfloat16 [8, 1024, 1024], P('fsdp', 'ctx')
- input_grad: float32 [8, 1024, 1024], P('fsdp', 'ctx')
- grad_query_weight: float32 [1024, 1024], P('fsdp')
- grad_query_bias: float32 [1024], P('fsdp')
- grad_key_weight: float32 [1024, 1024], P('fsdp')
- grad_value_weight: float32 [1024, 1024], P('fsdp')
- grad_value_bias: float32 [1024], P('fsdp')
- grad_out_weight: float32 [1024, 1024], P('fsdp')
- grad_out_bias: float32 [1024], P('fsdp')
- grad_attn_gain: float32 [1024], P('fsdp')
- grad_attn_shift: float32 [1024], P('fsdp')
- grad_up_weight: float32 [1024, 4096], P('fsdp')
- grad_up_bias: float32 [4096], P('fsdp')
- grad_down_weight: float32 [4096, 1024], P('fsdp')
- grad_down_bias: float32 [1024], P('fsdp')
- grad_mlp_gain: float32 [1024], P('fsdp')
- grad_mlp_shift: float32 [1024], P('fsdp')
- rms_stream: float32 [], replicated
- rms_attn: float32 [], replicated
- rms_mlp: float32 [], replicated
The draws below stay inside these ranges and needn't reach their ends.
Inputs may be any that keep to these rules, and one draw needn't show every extreme that they name: `segment_ids`: each of the 8 sequences holds segments 0 to 7 in order, each of 1 to 512 tokens, one of exactly 512; tokens of segment 8 - 1 are padding.
All inputs are finite; a program needn't handle non-finite values.
Results may differ from the reference program's by a relative error of at most 0.019.
The reference program's roundings to bfloat16 on the way count: a program that leaves them out, or rounds other values in their place, can miss the bound.
Values may be sent and summed in bfloat16 or wider, within the bound.
No kernel may reach another device: no remote copies, remote signals or barrier semaphores. Data moves between devices by JAX's collectives and lax.ppermute only.
A program may use at most 192 MiB of HBM per device.

```python
import math
import jax
import jax.numpy as jnp
import numpy as np
from jax import lax

D = 1024
HEADS = 16
HEAD_DIM = 64
FF = 4096
SEQ_LEN = 1024
SEGS = 8
MOST = 512
NSEQ = 8


def draw_tokens(key, part):
    key_value_pairs = jax.random.fold_in(key, 0)
    position = jnp.arange(SEQ_LEN, dtype=jnp.float32) / (SEQ_LEN - 1)
    growth = jnp.sqrt(1.0 + 3.0 * position)[None, :, None]
    values_drawn = jnp.clip(jax.random.normal(key_value_pairs, (NSEQ, SEQ_LEN, D), jnp.float32), -4.5, 4.5)
    return (values_drawn * growth).astype(jnp.bfloat16)


def shard_levels(rng, extent, cuts, least, high):
    def one(axis_at, blocks):
        steps = jax.random.uniform(jax.random.fold_in(jax.random.fold_in(rng, 6), axis_at), (blocks,), jnp.float32, least / len(cuts), high / len(cuts))
        return jnp.repeat(jnp.exp(steps), extent[axis_at] // blocks).reshape((-1,) + (1,) * (len(extent) - axis_at - 1))

    factor_of = one(*cuts[0])
    for cut in cuts[1:]:
        factor_of = factor_of * one(*cut)
    return factor_of


def length_profile(amount, total, bound, slope):
    loads = [(1 << 20) // math.isqrt(rank ** slope) + 1 for rank in range(2, amount + 1)]
    rest, holding = total - bound - (amount - 1), [1] * (amount - 1)
    while rest > 0:
        free = [i for i in range(amount - 1) if holding[i] < bound]
        mass, budget = sum([loads[i] for i in free]), rest
        for i in free:
            addition = min(bound - holding[i], max(1, budget * loads[i] // mass), rest)
            holding[i] = holding[i] + addition
            rest = rest - addition
    return np.array([bound] + holding)


def uneven(key, number_of, total, limit, lean):
    if number_of == 2:
        one = jax.random.randint(key, (), max(1, total - limit), min(limit, total - 1) + 1)
        return jnp.stack([one, total - one])
    sizes = jnp.asarray(length_profile(number_of, total, limit, lean), jnp.int32)
    twos = (number_of - 1) // 2
    donor, sink = sizes[1:1 + 2 * twos:2], sizes[2:2 + 2 * twos:2]
    room = jnp.minimum(donor - 1, limit - sink)
    shifted = jax.random.randint(jax.random.fold_in(key, 1), (twos,), 0, 1 << 20) % (room + 1)
    sizes = sizes.at[1:1 + 2 * twos:2].set(donor - shifted).at[2:2 + 2 * twos:2].set(sink + shifted)
    return sizes[jax.random.permutation(jax.random.fold_in(key, 2), number_of)]


def bell_draw(stream_key, dims, width, reach, pieces=(), kind=jnp.bfloat16):
    drawn = width * jax.random.normal(stream_key, dims, jnp.float32)
    if pieces:
        drawn = drawn * shard_levels(stream_key, dims, pieces, -0.22, 0.18)
    return jnp.clip(drawn, -reach, reach).astype(kind)


def setup_inputs(seed: int = 0) -> dict:
    key_list = jax.random.split(jax.random.key(seed), 19)
    tokens = draw_tokens(jax.random.fold_in(key_list[18], 71), 0)
    segment_ids = jax.vmap(lambda own: jnp.searchsorted(jnp.cumsum(uneven(own, SEGS, SEQ_LEN, MOST, 2)), jnp.arange(SEQ_LEN), side="right"))(jax.random.split(key_list[1], NSEQ)).reshape((NSEQ, SEQ_LEN)).astype(jnp.int32)
    cotangent = bell_draw(key_list[2], (NSEQ, SEQ_LEN, D), 1.0, 6.0, ((0, 8), (1, 4)))
    query_weight = bell_draw(key_list[3], (D, D), D ** -0.5, 0.1875, ((0, 8),))
    query_bias = bell_draw(key_list[4], (D,), 0.5, 3.0, ((0, 8),))
    key_weight = bell_draw(key_list[5], (D, D), D ** -0.5, 0.1875, ((0, 8),))
    value_weight = bell_draw(key_list[6], (D, D), D ** -0.5, 0.1875, ((0, 8),))
    value_bias = bell_draw(key_list[7], (D,), 0.5, 3.0, ((0, 8),))
    out_weight = bell_draw(key_list[8], (D, D), (D // 16) ** -0.5, 0.75, ((0, 8),))
    out_bias = bell_draw(key_list[9], (D,), 0.5, 3.0, ((0, 8),))
    attn_gain = jnp.clip(1.0 + 0.15 * jax.random.normal(key_list[10], (D,), jnp.float32), 0.25, 1.75).astype(jnp.bfloat16)
    attn_shift = bell_draw(key_list[11], (D,), 0.3, 2.0, ((0, 8),))
    up_weight = bell_draw(key_list[12], (D, FF), D ** -0.5, 0.1875, ((0, 8),))
    up_bias = bell_draw(key_list[13], (FF,), 0.5, 3.0, ((0, 8),))
    down_weight = bell_draw(key_list[14], (FF, D), FF ** -0.5, 0.09375, ((0, 8),))
    down_bias = bell_draw(key_list[15], (D,), 0.5, 3.0, ((0, 8),))
    mlp_gain = jnp.clip(1.0 + 0.15 * jax.random.normal(key_list[16], (D,), jnp.float32), 0.25, 1.75).astype(jnp.bfloat16)
    mlp_shift = bell_draw(key_list[17], (D,), 0.3, 2.0, ((0, 8),))
    return dict(tokens=tokens, segment_ids=segment_ids, cotangent=cotangent, query_weight=query_weight, query_bias=query_bias, key_weight=key_weight, value_weight=value_weight, value_bias=value_bias, out_weight=out_weight, out_bias=out_bias, attn_gain=attn_gain, attn_shift=attn_shift, up_weight=up_weight, up_bias=up_bias, down_weight=down_weight, down_bias=down_bias, mlp_gain=mlp_gain, mlp_shift=mlp_shift)


HIGHEST = lax.Precision.HIGHEST

@jax.custom_vjp
def low(v):
    return lax.optimization_barrier(v.astype(jnp.bfloat16)).astype(jnp.float32)

@jax.custom_vjp
def low_back(v):
    return v

def low_keep(v):
    return (low(v), None)

def low_pass(kept, grad):
    return (grad,)

def back_keep(v):
    return (v, None)

def back_low(kept, grad):
    return (low(grad),)
low.defvjp(low_keep, low_pass)
low_back.defvjp(back_keep, back_low)

def project(layer_activations, weight_matrix):
    return jnp.einsum('gld,de->gle', layer_activations, weight_matrix, precision=HIGHEST)

def normalize(hidden, gain_vector, shift_vector):
    centre = hidden - lax.optimization_barrier(jnp.mean(hidden, axis=-1, keepdims=True))
    variance = lax.optimization_barrier(jnp.mean(centre * centre, axis=-1, keepdims=True))
    return centre * lax.rsqrt(variance + 1e-05) * gain_vector + shift_vector

def attend_one(packed):
    queries, keys_in, values, labels = packed
    scores = jnp.einsum('qhd,khd->hqk', queries, keys_in, precision=HIGHEST) * HEAD_DIM ** (-0.5)
    same_segment = labels[:, None] == labels[None, :]
    scores = low_back(jnp.where(same_segment[None], scores, -1000000000.0))
    probabilities = jax.nn.softmax(scores, axis=-1)
    return jnp.einsum('hqk,khd->qhd', low(probabilities), values, precision=HIGHEST)

def layer(parameters, tokens_in, labels):
    query_weight, query_bias, key_weight, value_weight, value_bias, out_weight, out_bias, attn_gain, attn_shift, up_weight, up_bias, down_weight, down_bias, mlp_gain, mlp_shift = parameters
    groups, length, width_all = tokens_in.shape
    queries = low_back(low(project(tokens_in, query_weight) + query_bias))
    keys_in = low_back(low(project(tokens_in, key_weight)))
    values = low_back(low(project(tokens_in, value_weight) + value_bias))
    split_shape = (groups, length, HEADS, HEAD_DIM)
    mixed = lax.map(jax.checkpoint(attend_one), (queries.reshape(split_shape), keys_in.reshape(split_shape), values.reshape(split_shape), labels))
    mixed = low_back(low(mixed.reshape(groups, length, width_all)))
    attn_branch = low_back(project(mixed, out_weight) + out_bias)
    normed = normalize(tokens_in + attn_branch, attn_gain, attn_shift)
    gate_pre = low_back(project(low(normed), up_weight) + up_bias)
    hidden = low(jax.nn.gelu(gate_pre, approximate=False))
    mlp_branch = low_back(project(hidden, down_weight) + down_bias)
    return (normalize(normed + mlp_branch, mlp_gain, mlp_shift), (attn_branch, mlp_branch))

def reference(tokens, segment_ids, cotangent, query_weight, query_bias, key_weight, value_weight, value_bias, out_weight, out_bias, attn_gain, attn_shift, up_weight, up_bias, down_weight, down_bias, mlp_gain, mlp_shift):
    parameters = tuple((member.astype(jnp.float32) for member in (query_weight, query_bias, key_weight, value_weight, value_bias, out_weight, out_bias, attn_gain, attn_shift, up_weight, up_bias, down_weight, down_bias, mlp_gain, mlp_shift)))
    blocks_count = NSEQ // 4
    token_blocks = tokens.astype(jnp.float32).reshape(blocks_count, 4, SEQ_LEN, D)
    label_blocks = segment_ids.reshape(blocks_count, 4, SEQ_LEN)
    valid_blocks = (label_blocks != SEGS - 1).astype(jnp.float32)
    cot_blocks = cotangent.astype(jnp.float32).reshape(blocks_count, 4, SEQ_LEN, D) * valid_blocks[..., None]

    def block_step(running, packed):
        gradient_sums, square_sums = running
        block_tokens, block_labels, block_valid, block_cot = packed

        def forward(params_in, tokens_in):
            return layer(params_in, tokens_in, block_labels)
        outputs, pullback, branches = jax.vjp(forward, parameters, block_tokens, has_aux=True)
        grad_params, grad_tokens = pullback(block_cot)
        gradient_sums = jax.tree.map(jnp.add, gradient_sums, grad_params)
        weighted = block_valid[..., None]
        square_sums = square_sums + jnp.stack([jnp.sum(weighted * block_tokens * block_tokens), jnp.sum(weighted * branches[0] * branches[0]), jnp.sum(weighted * branches[1] * branches[1])])
        return ((gradient_sums, square_sums), (outputs.astype(jnp.bfloat16), grad_tokens))
    initial = (tuple((jnp.zeros_like(member) for member in parameters)), jnp.zeros((3,), jnp.float32))
    (gradient_sums, square_sums), (outputs, grad_tokens) = lax.scan(block_step, initial, (token_blocks, label_blocks, valid_blocks, cot_blocks))
    counted = jnp.sum(valid_blocks) * D
    root_means = jnp.sqrt(square_sums / counted)
    return (outputs.reshape(NSEQ, SEQ_LEN, D), grad_tokens.reshape(NSEQ, SEQ_LEN, D), gradient_sums[0], gradient_sums[1], gradient_sums[2], gradient_sums[3], gradient_sums[4], gradient_sums[5], gradient_sums[6], gradient_sums[7], gradient_sums[8], gradient_sums[9], gradient_sums[10], gradient_sums[11], gradient_sums[12], gradient_sums[13], gradient_sums[14], root_means[0], root_means[1], root_means[2])
```

```python
from functools import partial

import jax
import jax.numpy as jnp
from jax import lax
from jax.experimental import pallas as pl
from jax.experimental.pallas import tpu as pltpu
from jax.sharding import PartitionSpec as P

HEADS = 16
HEAD_DIM = 64
SEGS = 8
EPSILON = 1e-05
MASKED = -1000000000.0
SCALE = HEAD_DIM ** (-0.5)
BF = jnp.bfloat16
F32 = jnp.float32

CHUNK = 256
HERE = 4
WIDE = HERE * HEAD_DIM
SHARDS = 8
ROWS = 128
PARAMS = pltpu.CompilerParams(vmem_limit_bytes=60 * 1024 * 1024)


def dot(a, b, dims=((1,), (0,))):
    return lax.dot_general(a, b, (dims, ((), ())), preferred_element_type=F32)


def vec(small_ref, row, start, size):
    return jnp.concatenate(
        [small_ref[f, row : row + 1, start : start + size].astype(F32) for f in range(SHARDS)],
        axis=1,
    )


def any_spec(shape):
    return pl.BlockSpec(shape, lambda *a: (0,) * len(shape))


def segment_setup(z, xs, segr, segc, ends):
    for k in range(4):
        a = lax.rem(z - k + 4, 4)
        row = xs[k][CHUNK : CHUNK + 16, 0:CHUNK].astype(F32)[0:1, :]
        segr[a] = jnp.broadcast_to(row, (8, CHUNK))
        segc[a] = jnp.transpose(jnp.broadcast_to(row, (128, CHUNK)))
        ends[0, a] = jnp.min(row).astype(jnp.int32)
        ends[1, a] = jnp.max(row).astype(jnp.int32)


def key_range(ends, i):
    low = jnp.int32(0)
    high = jnp.int32(4)
    for j in range(4):
        low = low + (ends[1, j] < ends[0, i]).astype(jnp.int32)
        high = high - (ends[0, j] > ends[1, i]).astype(jnp.int32)
    return low, high


def attn_fwd_kernel(
    sc, x0, x1, x2, x3, w, m0, m1, m2, m3, mixf, lse, qkv, segr, segc, ends
):
    z = sc[0]
    xs = (x0, x1, x2, x3)
    segment_setup(z, xs, segr, segc, ends)
    weight = w[:, 0:ROWS, :].reshape(SHARDS * ROWS, 3 * WIDE)
    first = w[2 * z, ROWS : ROWS + 16, :].astype(F32)
    second = w[2 * z + 1, ROWS : ROWS + 16, :].astype(F32)
    qb = jnp.concatenate([first[0:1, 0:128], second[0:1, 0:128]], axis=1)
    vb = jnp.concatenate([first[0:1, 128:256], second[0:1, 128:256]], axis=1)
    for k in range(4):
        a = pl.multiple_of(lax.rem(z - k + 4, 4) * CHUNK, CHUNK)
        prod = dot(xs[k][0:CHUNK, :], weight)
        q = ((prod[:, 0:WIDE] + qb).astype(BF).astype(F32) * SCALE).astype(BF)
        kk = prod[:, WIDE : 2 * WIDE].astype(BF)
        v = (prod[:, 2 * WIDE :] + vb).astype(BF)
        for n, part in enumerate((q, kk, v)):
            for h in range(HERE):
                qkv[n * HERE + h, pl.ds(a, CHUNK), :] = part[:, h * HEAD_DIM : (h + 1) * HEAD_DIM]

    def q_chunk(i, carry):
        rows = pl.ds(pl.multiple_of(i * CHUNK, CHUNK), CHUNK)
        low, high = key_range(ends, i)
        col = segc[i]
        col2 = jnp.concatenate([col, col], axis=1)
        qs = [qkv[h, rows, :] for h in range(HERE)]

        def key_chunk(j, state):
            keys = pl.ds(pl.multiple_of(j * CHUNK, CHUNK), CHUNK)
            mask = col2 == segr[j][0:1, :]
            new = []
            for h in range(HERE):
                m, l, acc = state[h]
                s = dot(qs[h], qkv[HERE + h, keys, :], ((1,), (1,)))
                s = jnp.where(mask, s, MASKED)
                m_new = jnp.maximum(m, jnp.max(s, axis=1, keepdims=True))
                p = jnp.exp(s - m_new)
                fix = jnp.exp(m - m_new)
                l = l * fix + jnp.sum(p, axis=1, keepdims=True)
                acc = acc * fix + dot(p.astype(BF), qkv[2 * HERE + h, keys, :])
                new.append((m_new, l, acc))
            return tuple(new)

        init = tuple(
            (
                jnp.full((CHUNK, 1), MASKED, F32),
                jnp.zeros((CHUNK, 1), F32),
                jnp.zeros((CHUNK, HEAD_DIM), F32),
            )
            for _ in range(HERE)
        )
        state = lax.fori_loop(low, high, key_chunk, init)
        lane = lax.broadcasted_iota(jnp.int32, (CHUNK, 128), 1)
        logs = jnp.zeros((CHUNK, 128), F32)
        for h in range(HERE):
            m, l, acc = state[h]
            mixf[rows, h * HEAD_DIM : (h + 1) * HEAD_DIM] = acc / l
            logs = jnp.where(lane == h, m + jnp.log(l), logs)
        lse[rows, :] = logs
        return carry

    lax.fori_loop(0, 4, q_chunk, 0)
    for k, out in enumerate((m0, m1, m2, m3)):
        a = pl.multiple_of(lax.rem(z - k + 4, 4) * CHUNK, CHUNK)
        out[...] = mixf[pl.ds(a, CHUNK), :].astype(BF)


SMEM_SPEC = pl.BlockSpec(memory_space=pltpu.SMEM)
VMEM_SPEC = pl.BlockSpec(memory_space=pltpu.VMEM)


def attn_fwd(scalars, xs, pack):
    shape = jax.ShapeDtypeStruct
    return pl.pallas_call(
        attn_fwd_kernel,
        name="attn_fwd",
        out_shape=(shape((CHUNK, WIDE), BF),) * 4
        + (
            shape((4 * CHUNK, WIDE), F32),
            shape((4 * CHUNK, 128), F32),
            shape((3 * HERE, 4 * CHUNK, HEAD_DIM), BF),
        ),
        in_specs=[SMEM_SPEC] + [VMEM_SPEC] * 5,
        out_specs=(VMEM_SPEC,) * 7,
        scratch_shapes=[
            pltpu.VMEM((4, 8, CHUNK), F32),
            pltpu.VMEM((4, CHUNK, 128), F32),
            pltpu.SMEM((2, 4), jnp.int32),
        ],
        compiler_params=PARAMS,
    )(scalars, *xs, pack)


def normalise(h):
    centre = h - jnp.mean(h, axis=-1, keepdims=True)
    inverse = lax.rsqrt(jnp.mean(centre * centre, axis=-1, keepdims=True) + EPSILON)
    return centre * inverse, inverse


def norm_pullback(upstream, scaled, inverse, gain):
    e = upstream * gain
    return inverse * (
        e
        - jnp.mean(e, axis=-1, keepdims=True)
        - scaled * jnp.mean(e * scaled, axis=-1, keepdims=True)
    )


def out_kernel(sc, tok, r0, r1, r2, r3, w, small, valid, normed, low, scaled, inv, mixed, stats):
    z = sc[0]
    acc = jnp.zeros((CHUNK, 1024), F32)
    for k, r in enumerate((r0, r1, r2, r3)):
        a = lax.rem(z + k, 4)
        rows = w[pl.ds(2 * a, 2)].reshape(WIDE, 1024)
        acc = acc + dot(r[...], rows)
        mixed[:, pl.ds(pl.multiple_of(a * WIDE, WIDE), WIDE)] = r[...]
    branch = acc + vec(small, 0, 256, 128)
    x = tok[...].astype(F32)
    n, inverse = normalise(x + branch)
    y = n * vec(small, 0, 384, 128) + vec(small, 0, 512, 128)
    normed[...] = y
    low[...] = y.astype(BF)
    scaled[...] = n
    inv[...] = jnp.broadcast_to(inverse, (CHUNK, 128))
    ok = valid[...]
    lane = lax.broadcasted_iota(jnp.int32, (8, 128), 1)
    stats[...] = jnp.where(
        lane == 0,
        jnp.sum(ok * x * x),
        jnp.where(lane == 1, jnp.sum(ok * branch * branch), jnp.where(lane == 3, jnp.sum(ok), 0.0)),
    )


def out_project(scalars, tok, parts, big, pack, valid):
    shape = jax.ShapeDtypeStruct
    full = lambda *s: any_spec(s)
    return pl.pallas_call(
        out_kernel,
        name="out_project",
        grid=(1,),
        out_shape=(
            shape((CHUNK, 1024), F32),
            shape((CHUNK, 1024), BF),
            shape((CHUNK, 1024), F32),
            shape((CHUNK, 128), F32),
            shape((CHUNK, 1024), BF),
            shape((8, 128), F32),
        ),
        in_specs=[SMEM_SPEC, full(CHUNK, 1024)]
        + [full(CHUNK, WIDE)] * 4
        + [
            pl.BlockSpec((SHARDS, ROWS, 1024), lambda j: (0, 8, 0)),
            pl.BlockSpec((SHARDS, 16, 768), lambda j: (0, 8, 0)),
            full(CHUNK, 1),
        ],
        out_specs=(
            full(CHUNK, 1024),
            full(CHUNK, 1024),
            full(CHUNK, 1024),
            full(CHUNK, 128),
            full(CHUNK, 1024),
            full(8, 128),
        ),
        compiler_params=PARAMS,
    )(scalars, tok, *parts, big, pack, valid)


def mlp_fwd_kernel(
    normed, low, up, down, small, cot, valid, hidden, slope, out, gh2, gm, sums, stats, acc
):
    j = pl.program_id(0)
    gate = dot(low[...], up[...].reshape(SHARDS * ROWS, 512))
    gate = gate + small[j, 1:2, 256:768].astype(F32)
    cdf = 0.5 * (1.0 + lax.erf(gate * (2.0 ** -0.5)))
    h = (gate * cdf).astype(BF)
    hidden[...] = h
    slope[...] = cdf + gate * (jnp.exp(-0.5 * gate * gate) * 0.3989422804014327)
    part = dot(h, down[...].reshape(512, 1024))

    @pl.when(j == 0)
    def _():
        acc[...] = part

    @pl.when(j > 0)
    def _():
        acc[...] += part

    @pl.when(j == SHARDS - 1)
    def _():
        branch = acc[...] + vec(small, 0, 640, 128)
        n, inverse = normalise(normed[...] + branch)
        gain = vec(small, 1, 0, 128)
        out[...] = (n * gain + vec(small, 1, 128, 128)).astype(BF)
        ok = valid[...]
        u = cot[...].astype(F32) * ok
        g = norm_pullback(u, n, inverse, gain)
        gh2[...] = g
        g_low = g.astype(BF)
        gm[...] = g_low
        sums[0:1, :] = jnp.sum(u * n, axis=0, keepdims=True)
        sums[1:2, :] = jnp.sum(u, axis=0, keepdims=True)
        sums[2:3, :] = jnp.sum(g_low.astype(F32), axis=0, keepdims=True)
        sums[3:8, :] = jnp.zeros((5, 1024), F32)
        lane = lax.broadcasted_iota(jnp.int32, (8, 128), 1)
        stats[...] = jnp.where(lane == 2, jnp.sum(ok * branch * branch), 0.0)


def mlp_fwd(normed, low, big, pack, cot, valid):
    shape = jax.ShapeDtypeStruct
    full = lambda *s: any_spec(s)
    return pl.pallas_call(
        mlp_fwd_kernel,
        name="mlp_fwd",
        grid=(SHARDS,),
        out_shape=(
            shape((CHUNK, 4096), BF),
            shape((CHUNK, 4096), F32),
            shape((CHUNK, 1024), BF),
            shape((CHUNK, 1024), F32),
            shape((CHUNK, 1024), BF),
            shape((8, 1024), F32),
            shape((8, 128), F32),
        ),
        in_specs=[
            full(CHUNK, 1024),
            full(CHUNK, 1024),
            pl.BlockSpec((SHARDS, ROWS, 512), lambda j: (0, 4 + j // 2, j % 2)),
            pl.BlockSpec((1, 512, 1024), lambda j: (j, 0, 0)),
            pl.BlockSpec((SHARDS, 16, 768), lambda j: (0, 8, 0)),
            full(CHUNK, 1024),
            full(CHUNK, 1),
        ],
        out_specs=(
            pl.BlockSpec((CHUNK, 512), lambda j: (0, j)),
            pl.BlockSpec((CHUNK, 512), lambda j: (0, j)),
            full(CHUNK, 1024),
            full(CHUNK, 1024),
            full(CHUNK, 1024),
            full(8, 1024),
            full(8, 128),
        ),
        scratch_shapes=[pltpu.VMEM((CHUNK, 1024), F32)],
        compiler_params=PARAMS,
    )(normed, low, big, big, pack, cot, valid)


ORDER = (3, 1, 2, 0)


def step_shard(j, sc):
    half = j // 2
    rel = jnp.where(half == 0, 3, jnp.where(half == 3, 0, half))
    return 2 * jnp.bitwise_xor(sc[1], rel) + jnp.bitwise_xor(sc[2], 1 - j % 2)


def step_rel(j):
    half = j // 2
    return jnp.where(half == 0, 3, jnp.where(half == 3, 0, half))


def mlp_bwd_kernel(
    sc,
    gm,
    hidden,
    slope,
    up,
    down,
    low,
    gh2,
    scaled,
    inv,
    small,
    mixed,
    wout,
    gd_keep,
    gd_send,
    gu_keep,
    gu_send,
    go_keep,
    go_send,
    gh1,
    g0,
    g1,
    g2,
    g3,
    sums,
    ub,
    acc,
    low_t,
):
    j = pl.program_id(0)
    f = step_shard(j, sc)
    chip, core, z = sc[1], sc[2], sc[0]

    @pl.when(j == 0)
    def _():
        low_t[...] = jnp.transpose(low[...])

    grad = gm[...]
    dh = dot(grad, down[...].reshape(512, 1024), ((1,), (1,)))
    gg = dh * slope[...]
    gg_low = gg.astype(BF)
    ub[pl.ds(f, 1)] = jnp.sum(gg_low.astype(F32), axis=0, keepdims=True).reshape(1, 1, 512)
    gd = dot(hidden[...], grad, ((0,), (0,))).astype(BF)

    @pl.when(j % 2 == 0)
    def _():
        gd_send[...] = gd.reshape(1, 512, 1024)

    @pl.when(j % 2 == 1)
    def _():
        gd_keep[...] = gd.reshape(1, 512, 1024)

    for r in range(4):
        rows = 2 * jnp.bitwise_xor(chip, r)
        at = pl.multiple_of((rows + core) * ROWS, ROWS)
        gu_keep[r] = dot(low_t[pl.ds(at, ROWS), :], gg_low).astype(BF)
        at = pl.multiple_of((rows + 1 - core) * ROWS, ROWS)
        gu_send[r] = dot(low_t[pl.ds(at, ROWS), :], gg_low).astype(BF)
    part = dot(gg_low, up[...].reshape(SHARDS * ROWS, 512), ((1,), (1,)))

    @pl.when(j == 0)
    def _():
        acc[...] = part

    @pl.when(j > 0)
    def _():
        acc[...] += part

    @pl.when(j == SHARDS - 1)
    def _():
        u = gh2[...] + acc[...]
        n = scaled[...]
        g = norm_pullback(u, n, inv[:, 0:1], vec(small, 0, 384, 128))
        gh1[...] = g
        g_low = g.astype(BF)
        sums[0:1, :] = jnp.sum(u * n, axis=0, keepdims=True)
        sums[1:2, :] = jnp.sum(u, axis=0, keepdims=True)
        sums[2:3, :] = jnp.sum(g_low.astype(F32), axis=0, keepdims=True)
        sums[3:8, :] = jnp.zeros((5, 1024), F32)
        go = dot(mixed[...], g_low, ((0,), (0,)))
        acc_o = go.astype(BF).reshape(SHARDS, ROWS, 1024)
        low_t[...] = jnp.zeros_like(low_t)
        for f_at in range(SHARDS):
            rel = jnp.bitwise_xor(chip, f_at // 2)

            @pl.when(core == f_at % 2)
            def _():
                go_keep[rel] = acc_o[f_at]

            @pl.when(core != f_at % 2)
            def _():
                go_send[rel] = acc_o[f_at]

        for k, out in enumerate((g0, g1, g2, g3)):
            a = lax.rem(z + k, 4)
            rows = wout[pl.ds(2 * a, 2)].reshape(WIDE, 1024)
            out[...] = dot(g_low, rows, ((1,), (1,))).astype(BF)


def mlp_bwd(scalars, gm, hidden, slope, big, low, gh2, scaled, inv, pack, mixed):
    shape = jax.ShapeDtypeStruct
    full = lambda *s: pl.BlockSpec(s, lambda j, sc: (0,) * len(s))
    keep_down = pl.BlockSpec((1, 512, 1024), lambda j, sc: (step_rel(j), 0, 0))

    def up_at(j, sc):
        f = step_shard(j, sc)
        return (0, f // 2, f % 2)

    keep_up = pl.BlockSpec((4, ROWS, 512), up_at)
    return pl.pallas_call(
        mlp_bwd_kernel,
        name="mlp_bwd",
        grid_spec=pltpu.PrefetchScalarGridSpec(
            num_scalar_prefetch=1,
            grid=(SHARDS,),
            in_specs=[
                full(CHUNK, 1024),
                pl.BlockSpec((CHUNK, 512), lambda j, sc: (0, step_shard(j, sc))),
                pl.BlockSpec((CHUNK, 512), lambda j, sc: (0, step_shard(j, sc))),
                pl.BlockSpec(
                    (SHARDS, ROWS, 512),
                    lambda j, sc: (0, 4 + step_shard(j, sc) // 2, step_shard(j, sc) % 2),
                ),
                pl.BlockSpec((1, 512, 1024), lambda j, sc: (step_shard(j, sc), 0, 0)),
                full(CHUNK, 1024),
                full(CHUNK, 1024),
                full(CHUNK, 1024),
                full(CHUNK, 128),
                pl.BlockSpec((SHARDS, 16, 768), lambda j, sc: (0, 8, 0)),
                full(CHUNK, 1024),
                pl.BlockSpec((SHARDS, ROWS, 1024), lambda j, sc: (0, 8, 0)),
            ],
            out_specs=(
                keep_down,
                keep_down,
                keep_up,
                keep_up,
                full(4, ROWS, 1024),
                full(4, ROWS, 1024),
                full(CHUNK, 1024),
            )
            + (full(CHUNK, WIDE),) * 4
            + (full(8, 1024), full(SHARDS, 1, 512)),
            scratch_shapes=[pltpu.VMEM((CHUNK, 1024), F32), pltpu.VMEM((1024, CHUNK), BF)],
        ),
        out_shape=(
            shape((4, 512, 1024), BF),
            shape((4, 512, 1024), BF),
            shape((4, 512, 1024), BF),
            shape((4, 512, 1024), BF),
            shape((4, ROWS, 1024), BF),
            shape((4, ROWS, 1024), BF),
            shape((CHUNK, 1024), F32),
        )
        + (shape((CHUNK, WIDE), BF),) * 4
        + (shape((8, 1024), F32), shape((SHARDS, 1, 512), F32)),
        compiler_params=PARAMS,
    )(scalars, gm, hidden, slope, big, big, low, gh2, scaled, inv, pack, mixed, big)


def attn_bwd_kernel(
    sc,
    x0,
    x1,
    x2,
    x3,
    w,
    qkv,
    mixf,
    lse,
    g0,
    g1,
    g2,
    g3,
    own,
    s1,
    s2,
    s3,
    gw_keep,
    gw_send,
    sums,
    segr,
    segc,
    ends,
    gs,
    dq,
    dk,
    dv,
    delta,
    dall,
    gw,
):
    z, chip, core = sc[0], sc[1], sc[2]
    xs = (x0, x1, x2, x3)
    segment_setup(z, xs, segr, segc, ends)
    dk[...] = jnp.zeros_like(dk)
    dv[...] = jnp.zeros_like(dv)
    lane = lax.broadcasted_iota(jnp.int32, (CHUNK, 128), 1)
    for k, g in enumerate((g0, g1, g2, g3)):
        rows = pl.ds(pl.multiple_of(lax.rem(z - k + 4, 4) * CHUNK, CHUNK), CHUNK)
        prod = g[...].astype(F32) * mixf[rows, :]
        d = jnp.zeros((CHUNK, 128), F32)
        for h in range(HERE):
            at = slice(h * HEAD_DIM, (h + 1) * HEAD_DIM)
            gs[h, rows, :] = g[:, at]
            d = jnp.where(lane == h, jnp.sum(prod[:, at], axis=1, keepdims=True), d)
        delta[rows, :] = d

    def q_chunk(i, carry):
        rows = pl.ds(pl.multiple_of(i * CHUNK, CHUNK), CHUNK)
        low, high = key_range(ends, i)
        col = segc[i]
        col2 = jnp.concatenate([col, col], axis=1)
        logs = lse[rows, :]
        deltas = delta[rows, :]
        dq[...] = jnp.zeros_like(dq)

        def key_chunk(j, inner):
            keys = pl.ds(pl.multiple_of(j * CHUNK, CHUNK), CHUNK)
            mask = col2 == segr[j][0:1, :]
            for h in range(HERE):
                q = qkv[h, rows, :]
                kk = qkv[HERE + h, keys, :]
                v = qkv[2 * HERE + h, keys, :]
                g = gs[h, rows, :]
                s = dot(q, kk, ((1,), (1,)))
                p = jnp.where(mask, jnp.exp(s - logs[:, h : h + 1]), 0.0)
                dp = dot(g, v, ((1,), (1,)))
                ds = (p * (dp - deltas[:, h : h + 1])).astype(BF)
                dv[h, keys, :] += dot(p.astype(BF), g, ((0,), (0,)))
                dk[h, keys, :] += dot(ds, q, ((0,), (0,)))
                dq[h] += dot(ds, kk)
            return inner

        lax.fori_loop(low, high, key_chunk, 0)
        for h in range(HERE):
            dall[rows, h * HEAD_DIM : (h + 1) * HEAD_DIM] = (dq[h] * SCALE).astype(BF)
        return carry

    lax.fori_loop(0, 4, q_chunk, 0)
    for h in range(HERE):
        at = WIDE + h * HEAD_DIM
        dall[:, at : at + HEAD_DIM] = dk[h].astype(BF)
        at = 2 * WIDE + h * HEAD_DIM
        dall[:, at : at + HEAD_DIM] = dv[h].astype(BF)
    sums[0:1, :] = jnp.sum(dall[:, 0:WIDE].astype(F32), axis=0, keepdims=True)
    sums[1:2, :] = jnp.sum(dall[:, 2 * WIDE :].astype(F32), axis=0, keepdims=True)
    sums[2:8, :] = jnp.zeros((6, WIDE), F32)
    weight = w[:, 0:ROWS, :].reshape(SHARDS * ROWS, 3 * WIDE)
    for k, out in enumerate((own, s1, s2, s3)):
        rows = pl.ds(pl.multiple_of(lax.rem(z - k + 4, 4) * CHUNK, CHUNK), CHUNK)
        d = dall[rows, :]
        out[...] = dot(d, weight, ((1,), (1,))).astype(out.dtype)
        part = dot(xs[k][0:CHUNK, :], d, ((0,), (0,)))
        if k == 0:
            gw[...] = part
        else:
            gw[...] += part
    for r in range(4):
        at = 2 * jnp.bitwise_xor(chip, r)
        gw_keep[r] = gw[pl.ds(pl.multiple_of((at + core) * ROWS, ROWS), ROWS), :].astype(BF)
        gw_send[r] = gw[pl.ds(pl.multiple_of((at + 1 - core) * ROWS, ROWS), ROWS), :].astype(BF)


def attn_bwd(scalars, xs, pack, qkv, mixf, lse, gs):
    shape = jax.ShapeDtypeStruct
    return pl.pallas_call(
        attn_bwd_kernel,
        name="attn_bwd",
        out_shape=(shape((CHUNK, 1024), F32),)
        + (shape((CHUNK, 1024), BF),) * 3
        + (shape((4, ROWS, 768), BF),) * 2
        + (shape((8, WIDE), F32),),
        in_specs=[SMEM_SPEC] + [VMEM_SPEC] * 12,
        out_specs=(VMEM_SPEC,) * 7,
        scratch_shapes=[
            pltpu.VMEM((4, 8, CHUNK), F32),
            pltpu.VMEM((4, CHUNK, 128), F32),
            pltpu.SMEM((2, 4), jnp.int32),
            pltpu.VMEM((HERE, 4 * CHUNK, HEAD_DIM), BF),
            pltpu.VMEM((HERE, CHUNK, HEAD_DIM), F32),
            pltpu.VMEM((HERE, 4 * CHUNK, HEAD_DIM), F32),
            pltpu.VMEM((HERE, 4 * CHUNK, HEAD_DIM), F32),
            pltpu.VMEM((4 * CHUNK, 128), F32),
            pltpu.VMEM((4 * CHUNK, 768), BF),
            pltpu.VMEM((1024, 768), F32),
        ],
        compiler_params=PARAMS,
    )(scalars, *xs, pack, qkv, mixf, lse, *gs)


def shift(x, k):
    n = lax.axis_size("ctx")
    return lax.ppermute(x, "ctx", [(i, (i + k) % n) for i in range(n)])


def swap(x, bits):
    return lax.ppermute(x, "fsdp", [(i, i ^ bits) for i in range(lax.axis_size("fsdp"))])


def gather_rows(x):
    full = lax.all_gather(x, "fsdp", axis=0, tiled=False)
    owners = full.shape[0]
    return full if owners == SHARDS else full


def add(*terms):
    total = terms[0].astype(F32)
    for term in terms[1:]:
        total = total + term.astype(F32)
    return total


def plane_sum(keep, send, direct):
    got = swap(send, 1)
    rows = keep.shape[1]
    part = lambda r, a, b: add(keep[r, a:b], got[r, a:b])
    if direct:
        far = swap(part(3, 0, rows).astype(BF), 6)
        along = swap(part(1, 0, rows).astype(BF), 2)
        across = swap(part(2, 0, rows).astype(BF), 4)
        return add(part(0, 0, rows), along, across, far)
    half = rows // 2
    from_x = swap(part(3, 0, half).astype(BF), 2)
    from_y = swap(part(3, half, rows).astype(BF), 4)
    to_y = jnp.concatenate([add(part(2, 0, half), from_x), part(2, half, rows)]).astype(BF)
    to_x = jnp.concatenate([part(1, 0, half), add(part(1, half, rows), from_y)]).astype(BF)
    return add(part(0, 0, rows), swap(to_x, 2), swap(to_y, 4))


def line_sum(x):
    index = lax.axis_index("ctx")
    mine = x.astype(BF)
    pair = add(mine, lax.ppermute(mine, "ctx", [(0, 1), (3, 2)])).astype(BF)
    whole = add(pair, lax.ppermute(pair, "ctx", [(1, 2), (2, 1)])).astype(BF)
    back = lax.ppermute(whole, "ctx", [(1, 0), (2, 3)])
    inner = (index == 1) | (index == 2)
    return jnp.where(inner, whole, back).astype(F32)


def everyone_sum(x):
    owners = lax.axis_size("fsdp")
    step = 1
    while step < owners:
        x = x + swap(x, step)
        step *= 2
    x = x + lax.ppermute(x, "ctx", [(0, 1), (1, 0), (2, 3), (3, 2)])
    return x + lax.ppermute(x, "ctx", [(0, 2), (2, 0), (1, 3), (3, 1)])


def per_device(
    tokens,
    segment_ids,
    cotangent,
    query_weight,
    query_bias,
    key_weight,
    value_weight,
    value_bias,
    out_weight,
    out_bias,
    attn_gain,
    attn_shift,
    up_weight,
    up_bias,
    down_weight,
    down_bias,
    mlp_gain,
    mlp_shift,
):
    owners = lax.axis_size("fsdp")
    plane = owners == SHARDS
    z = lax.axis_index("ctx")
    f = lax.axis_index("fsdp")
    if plane:
        chip, core = f // 2, f % 2
    else:
        chip, core = jnp.int32(0), jnp.int32(0)
    scalars = jnp.stack([z, chip, core, z]).astype(jnp.int32)
    tok = tokens[0]
    seg_row = jnp.pad(segment_ids.astype(BF), ((0, 15), (0, 1024 - CHUNK)))
    packed = jnp.concatenate([tok, seg_row])
    xs = [packed] + [shift(packed, k) for k in (1, 2, 3)]
    valid = (segment_ids[0] != SEGS - 1).astype(F32)[:, None]

    quarter = jnp.concatenate(
        [
            lax.dynamic_slice_in_dim(m, z * WIDE, WIDE, 1)
            for m in (query_weight, key_weight, value_weight)
        ],
        axis=1,
    )
    if plane:
        line0 = jnp.concatenate(
            [query_bias, value_bias, out_bias, attn_gain, attn_shift, down_bias]
        )
        line1 = jnp.concatenate([mlp_gain, mlp_shift, up_bias])
        lines = jnp.pad(jnp.stack([line0, line1]), ((0, 14), (0, 0)))
        pack = lax.all_gather(jnp.concatenate([quarter, lines]), "fsdp", axis=0)
        ups = [up_weight[:, 1024 * b : 1024 * (b + 1)] for b in range(4)]
        big = lax.all_gather(
            jnp.concatenate([down_weight] + ups + [out_weight]), "fsdp", axis=0
        )
    else:
        whole = lambda m: lax.all_gather(m, "fsdp", axis=0, tiled=True)
        split = lambda m: whole(m).reshape(SHARDS, -1)
        line0 = jnp.concatenate(
            [split(m) for m in (query_bias, value_bias, out_bias, attn_gain, attn_shift, down_bias)],
            axis=1,
        )
        line1 = jnp.concatenate([split(m) for m in (mlp_gain, mlp_shift, up_bias)], axis=1)
        lines = jnp.pad(jnp.stack([line0, line1], axis=1), ((0, 0), (0, 14), (0, 0)))
        pack = jnp.concatenate([whole(quarter).reshape(SHARDS, ROWS, 768), lines], axis=1)
        up = whole(up_weight).reshape(SHARDS, ROWS, 4, 1024).swapaxes(1, 2)
        big = jnp.concatenate(
            [
                whole(down_weight).reshape(SHARDS, 512, 1024),
                up.reshape(SHARDS, 512, 1024),
                whole(out_weight).reshape(SHARDS, ROWS, 1024),
            ],
            axis=1,
        )

    m0, m1, m2, m3, mixf, lse, qkv = attn_fwd(scalars, xs, pack)
    parts = [m0] + [shift(m, -k) for k, m in ((1, m1), (2, m2), (3, m3))]
    normed, low, scaled, inv, mixed, stats_a = out_project(scalars, tok, parts, big, pack, valid)
    hidden, slope, result, gh2, gm, sums_m, stats_m = mlp_fwd(
        normed, low, big, pack, cotangent[0], valid
    )
    (
        gd_keep,
        gd_send,
        gu_keep,
        gu_send,
        go_keep,
        go_send,
        gh1,
        g0,
        g1,
        g2,
        g3,
        sums_a,
        ub,
    ) = mlp_bwd(scalars, gm, hidden, slope, big, low, gh2, scaled, inv, pack, mixed)
    gs = [g0] + [shift(g, k) for k, g in ((1, g1), (2, g2), (3, g3))]
    own, s1, s2, s3, gw_keep, gw_send, sums_q = attn_bwd(scalars, xs, pack, qkv, mixf, lse, gs)
    input_grad = gh1 + add(own, *[shift(s, -k) for k, s in ((1, s1), (2, s2), (3, s3))])

    place = lambda row: lax.dynamic_update_slice(
        jnp.zeros((1, 1024), F32), row, (0, z * WIDE)
    )
    smalls = jnp.concatenate(
        [
            sums_m[0:3],
            sums_a[0:3],
            place(sums_q[0:1]),
            place(sums_q[1:2]),
            ub.reshape(4, 1024),
            jnp.pad(stats_a[0:1] + stats_m[0:1], ((0, 3), (0, 1024 - 128))),
        ]
    )
    if plane:
        smalls = everyone_sum(smalls)
    else:
        smalls = lax.psum(smalls, ("ctx", "fsdp"))
    size = 1024 // owners
    mine = lambda row: lax.dynamic_slice(smalls, (row, f * size), (1, size)).reshape(size)
    up_bias_grad = lax.dynamic_slice(
        smalls[8:12].reshape(4096), (f * (4096 // owners),), (4096 // owners,)
    )
    counted = smalls[12, 3] * 1024
    rms = [jnp.sqrt(smalls[12, n] / counted) for n in range(3)]

    if plane:
        down_own = plane_sum(gd_keep, gd_send, False)
        up_own = plane_sum(gu_keep, gu_send, False)
        out_own = plane_sum(go_keep, go_send, True)
        q_own = plane_sum(gw_keep, gw_send, True)
        grad_down = line_sum(down_own)
        rest = line_sum(jnp.concatenate([up_own, out_own]))
        grad_up = jnp.concatenate([rest[ROWS * b : ROWS * (b + 1)] for b in range(4)], axis=1)
        grad_out = rest[512:]
    else:
        both = lambda keep, send: jnp.stack([keep, send], axis=1)
        scatter = lambda m: lax.psum_scatter(m, "fsdp", scatter_dimension=0, tiled=True)
        down_own = scatter(both(gd_keep, gd_send).reshape(4096, 1024))
        up_own = scatter(
            both(gu_keep, gu_send)
            .reshape(SHARDS, 4, ROWS, 1024)
            .swapaxes(1, 2)
            .reshape(1024, 4096)
        )
        out_own = scatter(both(go_keep, go_send).reshape(1024, 1024))
        q_own = scatter(both(gw_keep, gw_send).reshape(1024, 768))
        grad_down, grad_up, grad_out = line_sum(down_own), line_sum(up_own), line_sum(out_own)
    q_low = q_own.astype(BF)
    pieces = [q_low] + [shift(q_low, k) for k in (1, 2, 3)]
    table = jnp.stack(pieces)
    table = jnp.take(table, (z - jnp.arange(4)) % 4, axis=0).astype(F32)
    cols = lambda n: jnp.concatenate(
        [table[a, :, n * WIDE : (n + 1) * WIDE] for a in range(4)], axis=1
    )
    return (
        result[None],
        input_grad[None],
        cols(0),
        mine(6),
        cols(1),
        cols(2),
        mine(7),
        grad_out,
        mine(5),
        mine(3),
        mine(4),
        grad_up,
        up_bias_grad,
        grad_down,
        mine(2),
        mine(0),
        mine(1),
        rms[0],
        rms[1],
        rms[2],
    )


def solution(mesh):
    matrix, vector = P("fsdp", None), P("fsdp")
    stream = P("fsdp", "ctx", None)
    placed = (
        stream,
        P("fsdp", "ctx"),
        stream,
        matrix,
        vector,
        matrix,
        matrix,
        vector,
        matrix,
        vector,
        vector,
        vector,
        matrix,
        vector,
        matrix,
        vector,
        vector,
        vector,
    )
    return jax.shard_map(
        per_device,
        mesh=mesh,
        in_specs=placed,
        out_specs=(
            stream,
            stream,
            matrix,
            vector,
            matrix,
            matrix,
            vector,
            matrix,
            vector,
            vector,
            vector,
            matrix,
            vector,
            matrix,
            vector,
            vector,
            vector,
            P(),
            P(),
            P(),
        ),
        check_vma=False,
    )
```

```python
from functools import partial

import jax
import jax.numpy as jnp
from jax import lax
from jax.experimental import pallas as pl
from jax.experimental.pallas import tpu as pltpu
from jax.sharding import PartitionSpec as P

HEADS = 16
HEAD_DIM = 64
SEGS = 8
EPSILON = 1e-05
MASKED = -1000000000.0
SCALE = HEAD_DIM ** (-0.5)
BF = jnp.bfloat16
F32 = jnp.float32

CHUNK = 256
HERE = 4
WIDE = HERE * HEAD_DIM
SHARDS = 8
ROWS = 128
PACK = 2 * ROWS + 16
PARAMS = pltpu.CompilerParams(vmem_limit_bytes=60 * 1024 * 1024)


SMEM_SPEC = pl.BlockSpec(memory_space=pltpu.SMEM)
VMEM_SPEC = pl.BlockSpec(memory_space=pltpu.VMEM)


def dot(a, b, dims=((1,), (0,))):
    return lax.dot_general(a, b, (dims, ((), ())), preferred_element_type=F32)


def vec(small_ref, row, start, size):
    return jnp.concatenate(
        [small_ref[f, row : row + 1, start : start + size].astype(F32) for f in range(SHARDS)],
        axis=1,
    )


def any_spec(shape):
    return pl.BlockSpec(shape, lambda *a: (0,) * len(shape))


def pack_kernel(sc, tok, seg, wq, wk, wv, wout, qb, vb, ob, ag, sh, db, mg, ms, ub, xp, pk):
    z = sc[0]
    cols = pl.ds(pl.multiple_of(z * WIDE, WIDE), WIDE)
    xp[0:CHUNK] = tok[...]
    xp[CHUNK:] = jnp.zeros((16, 1024), BF)
    xp[CHUNK : CHUNK + 1, 0:CHUNK] = seg[...].astype(F32).astype(BF)
    pk[0:ROWS] = wout[...]
    for n, w in enumerate((wq, wk, wv)):
        pk[ROWS : 2 * ROWS, WIDE * n : WIDE * n + WIDE] = w[:, cols]
    pk[ROWS : 2 * ROWS, 3 * WIDE :] = jnp.zeros((ROWS, 1024 - 3 * WIDE), BF)
    pk[2 * ROWS :] = jnp.zeros((16, 1024), BF)
    at = slice(2 * ROWS, 2 * ROWS + 1)
    for n, vector in enumerate((qb, vb, ob, ag, sh, db)):
        pk[at, 128 * n : 128 * n + 128] = vector[...]
    at = slice(2 * ROWS + 1, 2 * ROWS + 2)
    for n, vector in enumerate((mg, ms)):
        pk[at, 128 * n : 128 * n + 128] = vector[...]
    pk[at, 256:768] = ub[...]


def pack_inputs(scalars, tok, seg, weights, vectors):
    shape = jax.ShapeDtypeStruct
    return pl.pallas_call(
        pack_kernel,
        name="pack_inputs",
        in_specs=[SMEM_SPEC] + [VMEM_SPEC] * 15,
        out_specs=(VMEM_SPEC,) * 2,
        out_shape=(shape((CHUNK + 16, 1024), BF), shape((PACK, 1024), BF)),
        compiler_params=PARAMS,
    )(scalars, tok, seg, *weights, *[v[None] for v in vectors])


def segment_setup(rows, segc, ends):
    for a in range(4):
        row = rows[a][0:1, :]
        segc[a] = jnp.transpose(jnp.broadcast_to(row, (128, CHUNK)))
        ends[0, a] = jnp.min(row).astype(jnp.int32)
        ends[1, a] = jnp.max(row).astype(jnp.int32)


def key_range(ends, i):
    low = jnp.int32(0)
    high = jnp.int32(4)
    for j in range(4):
        low = low + (ends[1, j] < ends[0, i]).astype(jnp.int32)
        high = high - (ends[0, j] > ends[1, i]).astype(jnp.int32)
    return low, high


def attn_fwd_kernel(
    sc,
    x0,
    right,
    left,
    x2,
    far,
    w,
    small,
    m0,
    m1,
    m2,
    m3,
    mixf,
    lse,
    qkv,
    xall,
    segr,
    segc,
    ends,
):
    z = sc[0]

    def place(k, src):
        a = lax.rem(z - k + 4, 4)
        xall[a] = src[0:CHUNK, :]
        segr[a] = jnp.broadcast_to(
            src[CHUNK : CHUNK + 16, 0:CHUNK].astype(F32)[0:1, :], (8, CHUNK)
        )

    place(0, x0)
    place(2, x2)
    for k, usual, end in ((1, right, 0), (3, left, 3)):
        pl.when(z == end)(partial(place, k, far))
        pl.when(z != end)(partial(place, k, usual))
    segment_setup(segr, segc, ends)
    weight = w[...].reshape(SHARDS * ROWS, 3 * WIDE)
    first = small[2 * z].astype(F32)
    second = small[2 * z + 1].astype(F32)
    qb = jnp.concatenate([first[0:1, 0:128], second[0:1, 0:128]], axis=1)
    vb = jnp.concatenate([first[0:1, 128:256], second[0:1, 128:256]], axis=1)
    for n in range(4):
        a = n * CHUNK
        prod = dot(xall[n], weight)
        q = ((prod[:, 0:WIDE] + qb).astype(BF).astype(F32) * SCALE).astype(BF)
        kk = prod[:, WIDE : 2 * WIDE].astype(BF)
        v = (prod[:, 2 * WIDE :] + vb).astype(BF)
        for at, part in enumerate((q, kk, v)):
            for h in range(HERE):
                qkv[at * HERE + h, a : a + CHUNK, :] = part[:, h * HEAD_DIM : (h + 1) * HEAD_DIM]

    def q_chunk(i, carry):
        rows = pl.ds(pl.multiple_of(i * CHUNK, CHUNK), CHUNK)
        low, high = key_range(ends, i)
        col = segc[i]
        col2 = jnp.concatenate([col, col], axis=1)
        qs = [qkv[h, rows, :] for h in range(HERE)]

        def key_chunk(j, state):
            keys = pl.ds(pl.multiple_of(j * CHUNK, CHUNK), CHUNK)
            mask = col2 == segr[j][0:1, :]
            new = []
            for h in range(HERE):
                m, l, acc = state[h]
                s = dot(qs[h], qkv[HERE + h, keys, :], ((1,), (1,)))
                s = jnp.where(mask, s, MASKED)
                m_new = jnp.maximum(m, jnp.max(s, axis=1, keepdims=True))
                p = jnp.exp(s - m_new)
                fix = jnp.exp(m - m_new)
                l = l * fix + jnp.sum(p, axis=1, keepdims=True)
                acc = acc * fix + dot(p.astype(BF), qkv[2 * HERE + h, keys, :])
                new.append((m_new, l, acc))
            return tuple(new)

        init = tuple(
            (
                jnp.full((CHUNK, 1), MASKED, F32),
                jnp.zeros((CHUNK, 1), F32),
                jnp.zeros((CHUNK, HEAD_DIM), F32),
            )
            for _ in range(HERE)
        )
        state = lax.fori_loop(low, high, key_chunk, init)
        lane = lax.broadcasted_iota(jnp.int32, (CHUNK, 128), 1)
        logs = jnp.zeros((CHUNK, 128), F32)
        for h in range(HERE):
            m, l, acc = state[h]
            mixf[rows, h * HEAD_DIM : (h + 1) * HEAD_DIM] = acc / l
            logs = jnp.where(lane == h, m + jnp.log(l), logs)
        lse[rows, :] = logs
        return carry

    lax.fori_loop(0, 4, q_chunk, 0)
    for k, out in enumerate((m0, m1, m2, m3)):
        a = pl.multiple_of(lax.rem(z - k + 4, 4) * CHUNK, CHUNK)
        out[...] = mixf[pl.ds(a, CHUNK), :].astype(BF)


OUT_SPEC = pl.BlockSpec((SHARDS, ROWS, 1024), lambda *a: (0, 0, 0))
QKV_SPEC = pl.BlockSpec((SHARDS, ROWS, 3 * WIDE), lambda *a: (0, 1, 0))
SMALL_SPEC = pl.BlockSpec((SHARDS, 16, 3 * WIDE), lambda *a: (0, 2 * ROWS // 16, 0))


def attn_fwd(scalars, xs, pack):
    shape = jax.ShapeDtypeStruct
    return pl.pallas_call(
        attn_fwd_kernel,
        name="attn_fwd",
        out_shape=(shape((CHUNK, WIDE), BF),) * 4
        + (
            shape((4 * CHUNK, WIDE), F32),
            shape((4 * CHUNK, 128), F32),
            shape((3 * HERE, 4 * CHUNK, HEAD_DIM), BF),
            shape((4, CHUNK, 1024), BF),
            shape((4, 8, CHUNK), F32),
        ),
        grid=(1,),
        in_specs=[SMEM_SPEC] + [any_spec((CHUNK + 16, 1024))] * 5 + [QKV_SPEC, SMALL_SPEC],
        out_specs=(any_spec((CHUNK, WIDE)),) * 4
        + (
            any_spec((4 * CHUNK, WIDE)),
            any_spec((4 * CHUNK, 128)),
            any_spec((3 * HERE, 4 * CHUNK, HEAD_DIM)),
            any_spec((4, CHUNK, 1024)),
            any_spec((4, 8, CHUNK)),
        ),
        scratch_shapes=[
            pltpu.VMEM((4, CHUNK, 128), F32),
            pltpu.SMEM((2, 4), jnp.int32),
        ],
        compiler_params=PARAMS,
    )(scalars, *xs, pack, pack)


def normalise(h):
    centre = h - jnp.mean(h, axis=-1, keepdims=True)
    inverse = lax.rsqrt(jnp.mean(centre * centre, axis=-1, keepdims=True) + EPSILON)
    return centre * inverse, inverse


def norm_pullback(upstream, scaled, inverse, gain):
    e = upstream * gain
    return inverse * (
        e
        - jnp.mean(e, axis=-1, keepdims=True)
        - scaled * jnp.mean(e * scaled, axis=-1, keepdims=True)
    )


def relative(f, sc):
    return 2 * jnp.bitwise_xor(sc[1], f // 2) + jnp.bitwise_xor(sc[2], f % 2)


def out_kernel(sc, tok, r0, r1, r2, r3, w, small, valid, normed, low, low_rel, scaled, inv, mixed, stats):
    z = sc[0]
    acc = jnp.zeros((CHUNK, 1024), F32)
    for k, r in enumerate((r0, r1, r2, r3)):
        a = lax.rem(z + k, 4)
        rows = w[pl.ds(2 * a, 2)].reshape(WIDE, 1024)
        acc = acc + dot(r[...], rows)
        mixed[:, pl.ds(pl.multiple_of(a * WIDE, WIDE), WIDE)] = r[...]
    branch = acc + vec(small, 0, 256, 128)
    x = tok[...].astype(F32)
    n, inverse = normalise(x + branch)
    y = n * vec(small, 0, 384, 128) + vec(small, 0, 512, 128)
    normed[...] = y
    y_low = y.astype(BF)
    low[...] = y_low
    for f in range(SHARDS):
        at = relative(f, sc)
        low_rel[:, pl.ds(pl.multiple_of(at * ROWS, ROWS), ROWS)] = y_low[:, ROWS * f : ROWS * f + ROWS]
    scaled[...] = n
    inv[...] = jnp.broadcast_to(inverse, (CHUNK, 128))
    ok = valid[...]
    lane = lax.broadcasted_iota(jnp.int32, (8, 128), 1)
    stats[...] = jnp.where(
        lane == 0,
        jnp.sum(ok * x * x),
        jnp.where(lane == 1, jnp.sum(ok * branch * branch), jnp.where(lane == 3, jnp.sum(ok), 0.0)),
    )


def out_project(scalars, tok, parts, pack, valid):
    shape = jax.ShapeDtypeStruct
    full = lambda *s: any_spec(s)
    return pl.pallas_call(
        out_kernel,
        name="out_project",
        grid=(1,),
        out_shape=(
            shape((CHUNK, 1024), F32),
            shape((CHUNK, 1024), BF),
            shape((CHUNK, 1024), BF),
            shape((CHUNK, 1024), F32),
            shape((CHUNK, 128), F32),
            shape((CHUNK, 1024), BF),
            shape((8, 128), F32),
        ),
        in_specs=[SMEM_SPEC, full(CHUNK, 1024)]
        + [full(CHUNK, WIDE)] * 4
        + [OUT_SPEC, SMALL_SPEC, full(CHUNK, 1)],
        out_specs=(
            full(CHUNK, 1024),
            full(CHUNK, 1024),
            full(CHUNK, 1024),
            full(CHUNK, 1024),
            full(CHUNK, 128),
            full(CHUNK, 1024),
            full(8, 128),
        ),
        compiler_params=PARAMS,
    )(scalars, tok, *parts, pack, pack, valid)


def mlp_fwd_kernel(normed, low, low_rel, mixed, *refs):
    ups = refs[0:SHARDS]
    down, small, cot, valid, acts, slope, out, gh2, sums, stats, acc = refs[SHARDS:]
    j = pl.program_id(0)
    gate = dot(low_rel[...], jnp.concatenate([u[...] for u in ups]))
    gate = gate + small[j, 1:2, 256:768].astype(F32)
    cdf = 0.5 * (1.0 + lax.erf(gate * (2.0 ** -0.5)))
    h = (gate * cdf).astype(BF)
    for b in range(4):
        for half in range(2):

            @pl.when(j == 2 * b + half)
            def _():
                acts[b, :, 512 * half : 512 * half + 512] = h

    slope[...] = cdf + gate * (jnp.exp(-0.5 * gate * gate) * 0.3989422804014327)
    part = dot(h, down[...].reshape(512, 1024))

    @pl.when(j == 0)
    def _():
        acc[...] = part

    @pl.when(j > 0)
    def _():
        acc[...] += part

    @pl.when(j == SHARDS - 1)
    def _():
        branch = acc[...] + vec(small, 0, 640, 128)
        n, inverse = normalise(normed[...] + branch)
        gain = vec(small, 1, 0, 128)
        out[...] = (n * gain + vec(small, 1, 128, 128)).astype(BF)
        ok = valid[...]
        u = cot[...].astype(F32) * ok
        g = norm_pullback(u, n, inverse, gain)
        gh2[...] = g
        g_low = g.astype(BF)
        acts[4] = low[...]
        acts[5] = mixed[...]
        acts[6] = g_low
        sums[0:1, :] = jnp.sum(u * n, axis=0, keepdims=True)
        sums[1:2, :] = jnp.sum(u, axis=0, keepdims=True)
        sums[2:3, :] = jnp.sum(g_low.astype(F32), axis=0, keepdims=True)
        sums[3:8, :] = jnp.zeros((5, 1024), F32)
        lane = lax.broadcasted_iota(jnp.int32, (8, 128), 1)
        stats[...] = jnp.where(lane == 2, jnp.sum(ok * branch * branch), 0.0)


UP_SPECS = [pl.BlockSpec((ROWS, 512), lambda j: (0, j))] * SHARDS


def mlp_fwd(normed, low, low_rel, mixed, ups, down, pack, cot, valid):
    shape = jax.ShapeDtypeStruct
    full = lambda *s: any_spec(s)
    return pl.pallas_call(
        mlp_fwd_kernel,
        name="mlp_fwd",
        grid=(SHARDS,),
        out_shape=(
            shape((7, CHUNK, 1024), BF),
            shape((CHUNK, 4096), F32),
            shape((CHUNK, 1024), BF),
            shape((CHUNK, 1024), F32),
            shape((8, 1024), F32),
            shape((8, 128), F32),
        ),
        in_specs=[
            full(CHUNK, 1024),
            full(CHUNK, 1024),
            full(CHUNK, 1024),
            full(CHUNK, 1024),
        ]
        + UP_SPECS
        + [
            pl.BlockSpec((1, 512, 1024), lambda j: (j, 0, 0)),
            SMALL_SPEC,
            full(CHUNK, 1024),
            full(CHUNK, 1),
        ],
        out_specs=(
            full(7, CHUNK, 1024),
            pl.BlockSpec((CHUNK, 512), lambda j: (0, j)),
            full(CHUNK, 1024),
            full(CHUNK, 1024),
            full(8, 1024),
            full(8, 128),
        ),
        scratch_shapes=[pltpu.VMEM((CHUNK, 1024), F32)],
        compiler_params=PARAMS,
    )(normed, low, low_rel, mixed, *ups, down, pack, cot, valid)


def mlp_bwd_kernel(sc, gm, slope, *refs):
    ups = refs[0:SHARDS]
    down, gh2, scaled, inv, small, wout = refs[SHARDS : SHARDS + 6]
    grads, gh1, g0, g1, g2, g3, sums, ub, acc, total = refs[SHARDS + 6 :]
    j = pl.program_id(0)
    z = sc[0]
    dh = dot(gm[0], down[...].reshape(512, 1024), ((1,), (1,)))
    gg = (dh * slope[...]).astype(BF)
    ub[pl.ds(j, 1)] = jnp.sum(gg.astype(F32), axis=0, keepdims=True).reshape(1, 1, 512)
    for b in range(4):
        for half in range(2):

            @pl.when(j == 2 * b + half)
            def _():
                grads[b, :, 512 * half : 512 * half + 512] = gg

    part = dot(gg, jnp.concatenate([u[...] for u in ups]), ((1,), (1,)))

    @pl.when(j == 0)
    def _():
        acc[...] = part

    @pl.when(j > 0)
    def _():
        acc[...] += part

    @pl.when(j == SHARDS - 1)
    def _():
        for f in range(SHARDS):
            at = pl.ds(pl.multiple_of(relative(f, sc) * ROWS, ROWS), ROWS)
            total[:, ROWS * f : ROWS * f + ROWS] = acc[:, at]
        u = gh2[...] + total[...]
        n = scaled[...]
        g = norm_pullback(u, n, inv[:, 0:1], vec(small, 0, 384, 128))
        gh1[...] = g
        g_low = g.astype(BF)
        grads[4] = g_low
        sums[0:1, :] = jnp.sum(u * n, axis=0, keepdims=True)
        sums[1:2, :] = jnp.sum(u, axis=0, keepdims=True)
        sums[2:3, :] = jnp.sum(g_low.astype(F32), axis=0, keepdims=True)
        sums[3:8, :] = jnp.zeros((5, 1024), F32)
        for k, out in enumerate((g0, g1, g2, g3)):
            a = lax.rem(z + k, 4)
            rows = wout[pl.ds(2 * a, 2)].reshape(WIDE, 1024)
            out[...] = dot(g_low, rows, ((1,), (1,))).astype(BF)


def mlp_bwd(scalars, acts, slope, ups, down, gh2, scaled, inv, pack):
    shape = jax.ShapeDtypeStruct
    full = lambda *s: any_spec(s)
    return pl.pallas_call(
        mlp_bwd_kernel,
        name="mlp_bwd",
        grid=(SHARDS,),
        in_specs=[
            SMEM_SPEC,
            pl.BlockSpec((1, CHUNK, 1024), lambda j: (6, 0, 0)),
            pl.BlockSpec((CHUNK, 512), lambda j: (0, j)),
        ]
        + UP_SPECS
        + [
            pl.BlockSpec((1, 512, 1024), lambda j: (j, 0, 0)),
            full(CHUNK, 1024),
            full(CHUNK, 1024),
            full(CHUNK, 128),
            SMALL_SPEC,
            OUT_SPEC,
        ],
        out_specs=(full(5, CHUNK, 1024), full(CHUNK, 1024))
        + (full(CHUNK, WIDE),) * 4
        + (full(8, 1024), full(SHARDS, 1, 512)),
        scratch_shapes=[pltpu.VMEM((CHUNK, 1024), F32)] * 2,
        out_shape=(shape((5, CHUNK, 1024), BF), shape((CHUNK, 1024), F32))
        + (shape((CHUNK, WIDE), BF),) * 4
        + (shape((8, 1024), F32), shape((SHARDS, 1, 512), F32)),
        compiler_params=PARAMS,
    )(scalars, acts, slope, *ups, down, gh2, scaled, inv, pack, pack)


REST = 640


def step_shard(j, sc):
    rel = jnp.where(j == 0, 3, jnp.where(j >= 3, 0, j))
    return 2 * jnp.bitwise_xor(sc[1], rel) + sc[2]


def down_kernel(sc, ho, hp, lo, lp, d3, d1, d2, d0, right):
    s = pl.program_id(0)

    @pl.when(s == 0)
    def _():
        right[0:CHUNK] = lo[0]
        right[CHUNK:] = lp[0]

    left = jnp.concatenate([ho[0], hp[0]])
    res = dot(left, right[...], ((0,), (0,))).astype(BF)
    for n, out in enumerate((d3, d1, d2, d0)):

        @pl.when(s == n)
        def _():
            out[...] = res


def down_grads(scalars, acts, acts_p):
    shape = jax.ShapeDtypeStruct
    full = lambda *s: pl.BlockSpec(s, lambda j, sc: (0,) * len(s))

    def hid(j, sc):
        f = step_shard(j, sc)
        return (f // 2, 0, f % 2)

    hidden = pl.BlockSpec((1, CHUNK, 512), hid)
    grad = pl.BlockSpec((1, CHUNK, 1024), lambda j, sc: (6, 0, 0))
    return pl.pallas_call(
        down_kernel,
        name="down_grads",
        grid_spec=pltpu.PrefetchScalarGridSpec(
            num_scalar_prefetch=1,
            grid=(4,),
            in_specs=[hidden, hidden, grad, grad],
            out_specs=(full(512, 1024),) * 4,
            scratch_shapes=[pltpu.VMEM((2 * CHUNK, 1024), BF)],
        ),
        out_shape=(shape((512, 1024), BF),) * 4,
        compiler_params=PARAMS,
    )(scalars, acts, acts_p, acts, acts_p)


def rest_kernel(sc, lo, lp, go, gp, r3, r1, r2, r0, low_sel, mix_sel):
    s = pl.program_id(0)
    chip, core = sc[1], sc[2]

    @pl.when(s == 0)
    def _():
        for r in range(4):
            at = pl.multiple_of((2 * jnp.bitwise_xor(chip, r) + core) * ROWS, ROWS)
            to = slice(ROWS * r, ROWS * r + ROWS)
            low_sel[0:CHUNK, to] = lo[0, :, pl.ds(at, ROWS)]
            low_sel[CHUNK:, to] = lp[0, :, pl.ds(at, ROWS)]
            mix_sel[0:CHUNK, to] = lo[1, :, pl.ds(at, ROWS)]
            mix_sel[CHUNK:, to] = lp[1, :, pl.ds(at, ROWS)]

    @pl.when(s == 4)
    def _():
        low_sel[...] = mix_sel[...]

    right = jnp.concatenate([go[0], gp[0]])
    res = dot(low_sel[...], right, ((0,), (0,))).astype(BF)
    for b in range(5):

        @pl.when(s == b)
        def _():
            for r, out in enumerate((r0, r1, r2, r3)):
                out[ROWS * b : ROWS * b + ROWS] = res[ROWS * r : ROWS * r + ROWS]


def rest_grads(scalars, acts, acts_p, grads, grads_p):
    shape = jax.ShapeDtypeStruct
    full = lambda *s: pl.BlockSpec(s, lambda j, sc: (0,) * len(s))
    flat = pl.BlockSpec((pl.Element(2), pl.Element(CHUNK), pl.Element(1024)), lambda j, sc: (4, 0, 0))
    grad = pl.BlockSpec((1, CHUNK, 1024), lambda j, sc: (j, 0, 0))
    return pl.pallas_call(
        rest_kernel,
        name="rest_grads",
        grid_spec=pltpu.PrefetchScalarGridSpec(
            num_scalar_prefetch=1,
            grid=(5,),
            in_specs=[flat, flat, grad, grad],
            out_specs=(full(REST, 1024),) * 4,
            scratch_shapes=[pltpu.VMEM((2 * CHUNK, 512), BF)] * 2,
        ),
        out_shape=(shape((REST, 1024), BF),) * 4,
        compiler_params=PARAMS,
    )(scalars, acts, acts_p, grads, grads_p)


def attn_bwd_kernel(
    sc,
    xall,
    segr,
    w,
    qkv,
    mixf,
    lse,
    g0,
    g1,
    g2,
    g3,
    sums_m,
    sums_a,
    ubt,
    stats_a,
    stats_m,
    ig,
    gw_out,
    small,
    segc,
    ends,
    gs,
    dq,
    dk,
    dv,
    delta,
    dall,
    gw,
):
    z = sc[0]
    segment_setup(segr, segc, ends)
    dk[...] = jnp.zeros_like(dk)
    dv[...] = jnp.zeros_like(dv)
    lane = lax.broadcasted_iota(jnp.int32, (CHUNK, 128), 1)
    for k, g in enumerate((g0, g1, g2, g3)):
        rows = pl.ds(pl.multiple_of(lax.rem(z - k + 4, 4) * CHUNK, CHUNK), CHUNK)
        prod = g[...].astype(F32) * mixf[rows, :]
        d = jnp.zeros((CHUNK, 128), F32)
        for h in range(HERE):
            at = slice(h * HEAD_DIM, (h + 1) * HEAD_DIM)
            gs[h, rows, :] = g[:, at]
            d = jnp.where(lane == h, jnp.sum(prod[:, at], axis=1, keepdims=True), d)
        delta[rows, :] = d

    def q_chunk(i, carry):
        rows = pl.ds(pl.multiple_of(i * CHUNK, CHUNK), CHUNK)
        low, high = key_range(ends, i)
        col = segc[i]
        col2 = jnp.concatenate([col, col], axis=1)
        logs = lse[rows, :]
        deltas = delta[rows, :]
        dq[...] = jnp.zeros_like(dq)

        def key_chunk(j, inner):
            keys = pl.ds(pl.multiple_of(j * CHUNK, CHUNK), CHUNK)
            mask = col2 == segr[j][0:1, :]
            for h in range(HERE):
                q = qkv[h, rows, :]
                kk = qkv[HERE + h, keys, :]
                v = qkv[2 * HERE + h, keys, :]
                g = gs[h, rows, :]
                s = dot(q, kk, ((1,), (1,)))
                p = jnp.where(mask, jnp.exp(s - logs[:, h : h + 1]), 0.0)
                dp = dot(g, v, ((1,), (1,)))
                ds = (p * (dp - deltas[:, h : h + 1])).astype(BF)
                dv[h, keys, :] += dot(p.astype(BF), g, ((0,), (0,)))
                dk[h, keys, :] += dot(ds, q, ((0,), (0,)))
                dq[h] += dot(ds, kk)
            return inner

        lax.fori_loop(low, high, key_chunk, 0)
        for h in range(HERE):
            dall[rows, h * HEAD_DIM : (h + 1) * HEAD_DIM] = (dq[h] * SCALE).astype(BF)
        return carry

    lax.fori_loop(0, 4, q_chunk, 0)
    for h in range(HERE):
        at = WIDE + h * HEAD_DIM
        dall[:, at : at + HEAD_DIM] = dk[h].astype(BF)
        at = 2 * WIDE + h * HEAD_DIM
        dall[:, at : at + HEAD_DIM] = dv[h].astype(BF)
    here = pl.ds(pl.multiple_of(z * WIDE, WIDE), WIDE)
    small[...] = jnp.zeros_like(small)
    small[0:3, :] = sums_m[0:3, :]
    small[3:6, :] = sums_a[0:3, :]
    small[6:7, here] = jnp.sum(dall[:, 0:WIDE].astype(F32), axis=0, keepdims=True)
    small[7:8, here] = jnp.sum(dall[:, 2 * WIDE :].astype(F32), axis=0, keepdims=True)
    small[8:12, :] = ubt[...]
    every = lambda value: jnp.broadcast_to(value, (1, 1024))
    small[12:13, :] = every(stats_a[0:1, 0:1])
    small[13:14, :] = every(stats_a[0:1, 1:2])
    small[14:15, :] = every(stats_m[0:1, 2:3])
    count = stats_a[0:1, 3:4]
    high = jnp.floor(count * 0.0625)
    small[15:16, :] = every(high)
    small[16:17, :] = every(count - 16.0 * high)
    gw_out[:, 3 * WIDE :] = jnp.transpose(small[...]).astype(BF)
    weight = w[...].reshape(SHARDS * ROWS, 3 * WIDE)
    for k in range(4):
        rows = slice(CHUNK * k, CHUNK * k + CHUNK)
        d = dall[rows, :]
        ig[rows, :] = dot(d, weight, ((1,), (1,))).astype(BF)
        part = dot(xall[k], d, ((0,), (0,)))
        if k == 0:
            gw[...] = part
        else:
            gw[...] += part
    gw_out[:, 0 : 3 * WIDE] = gw[...].astype(BF)


def attn_bwd(scalars, xall, segr, pack, qkv, mixf, lse, gs, smalls):
    shape = jax.ShapeDtypeStruct
    return pl.pallas_call(
        attn_bwd_kernel,
        name="attn_bwd",
        out_shape=(shape((1024, 1024), BF), shape((1024, 3 * WIDE + 128), BF)),
        grid=(1,),
        in_specs=[SMEM_SPEC]
        + [
            any_spec((4, CHUNK, 1024)),
            any_spec((4, 8, CHUNK)),
            QKV_SPEC,
            any_spec((3 * HERE, 4 * CHUNK, HEAD_DIM)),
            any_spec((4 * CHUNK, WIDE)),
            any_spec((4 * CHUNK, 128)),
        ]
        + [any_spec((CHUNK, WIDE))] * 4
        + [any_spec((8, 1024)), any_spec((8, 1024)), any_spec((4, 1024))]
        + [any_spec((8, 128))] * 2,
        out_specs=(any_spec((1024, 1024)), any_spec((1024, 3 * WIDE + 128))),
        scratch_shapes=[
            pltpu.VMEM((128, 1024), F32),
            pltpu.VMEM((4, CHUNK, 128), F32),
            pltpu.SMEM((2, 4), jnp.int32),
            pltpu.VMEM((HERE, 4 * CHUNK, HEAD_DIM), BF),
            pltpu.VMEM((HERE, CHUNK, HEAD_DIM), F32),
            pltpu.VMEM((HERE, 4 * CHUNK, HEAD_DIM), F32),
            pltpu.VMEM((HERE, 4 * CHUNK, HEAD_DIM), F32),
            pltpu.VMEM((4 * CHUNK, 128), F32),
            pltpu.VMEM((4 * CHUNK, 768), BF),
            pltpu.VMEM((1024, 768), F32),
        ],
        compiler_params=PARAMS,
    )(scalars, xall, segr, pack, qkv, mixf, lse, *gs, *smalls)


def finish_kernel(sc, *refs):
    z = sc[0]
    pieces, (gq, gk, gv), vectors, ub, rms = refs[0:4], refs[4:7], refs[7:15], refs[15], refs[16:19]
    for k, piece in enumerate(pieces):
        cols = pl.ds(pl.multiple_of(lax.rem(z - k + 4, 4) * WIDE, WIDE), WIDE)
        for n, out in enumerate((gq, gk, gv)):
            out[:, cols] = piece[:, WIDE * n : WIDE * n + WIDE].astype(F32)
    extra = pieces[0][:, 3 * WIDE :].astype(F32)
    for piece in pieces[1:]:
        extra = extra + piece[:, 3 * WIDE :].astype(F32)
    extra = jnp.transpose(extra)
    for n, out in enumerate(vectors):
        out[...] = extra[n : n + 1, :]
    ub[...] = extra[8:12, :]
    counted = (16.0 * extra[15:16, 0:1] + extra[16:17, 0:1]) * 1024.0
    for n, out in enumerate(rms):
        out[...] = jnp.sqrt(extra[12 + n : 13 + n, 0:1] / counted)


def finish(scalars, pieces):
    shape = jax.ShapeDtypeStruct
    shapes = [(ROWS, 1024)] * 3 + [(1, ROWS)] * 8 + [(4, ROWS)] + [(1, 1)] * 3
    return pl.pallas_call(
        finish_kernel,
        name="finish",
        out_shape=tuple(shape(n, F32) for n in shapes),
        in_specs=[SMEM_SPEC] + [VMEM_SPEC] * 4,
        out_specs=(VMEM_SPEC,) * len(shapes),
        compiler_params=PARAMS,
    )(scalars, *pieces)


def line_gather(x):
    right = lax.ppermute(x, "ctx", [(0, 1), (1, 2), (2, 3)])
    left = lax.ppermute(x, "ctx", [(1, 0), (2, 1), (3, 2)])
    two = lax.ppermute(x, "ctx", [(0, 2), (1, 3), (2, 0), (3, 1)])
    return [x, right, left, two]


def line_forward(two):
    return lax.ppermute(two, "ctx", [(1, 0), (2, 3)])


def shift(x, k):
    n = lax.axis_size("ctx")
    return lax.ppermute(x, "ctx", [(i, (i + k) % n) for i in range(n)])


def swap(x, bits):
    return lax.ppermute(x, "fsdp", [(i, i ^ bits) for i in range(lax.axis_size("fsdp"))])


def add(*terms):
    total = terms[0].astype(F32)
    for term in terms[1:]:
        total = total + term.astype(F32)
    return total


def line_in(x):
    return lax.ppermute(x, "ctx", [(0, 1), (3, 2)])


def line_cross(x):
    return lax.ppermute(x, "ctx", [(1, 2), (2, 1)])


def line_out(x):
    return lax.ppermute(x, "ctx", [(1, 0), (2, 3)])


def line_sum(x):
    index = lax.axis_index("ctx")
    mine = x.astype(BF)
    pair = add(mine, line_in(mine)).astype(BF)
    whole = add(pair, line_cross(pair)).astype(BF)
    inner = (index == 1) | (index == 2)
    return jnp.where(inner, whole, line_out(whole)).astype(F32)


def per_device(
    tokens,
    segment_ids,
    cotangent,
    query_weight,
    query_bias,
    key_weight,
    value_weight,
    value_bias,
    out_weight,
    out_bias,
    attn_gain,
    attn_shift,
    up_weight,
    up_bias,
    down_weight,
    down_bias,
    mlp_gain,
    mlp_shift,
):
    owners = lax.axis_size("fsdp")
    plane = owners == SHARDS
    z = lax.axis_index("ctx")
    f = lax.axis_index("fsdp")
    if plane:
        chip, core = f // 2, f % 2
    else:
        chip, core = jnp.int32(0), jnp.int32(0)
    scalars = jnp.stack([z, chip, core, z]).astype(jnp.int32)
    tok = tokens[0]
    if plane:
        weights = (query_weight, key_weight, value_weight, out_weight)
        vectors = (query_bias, value_bias, out_bias, attn_gain, attn_shift, down_bias)
        vectors += (mlp_gain, mlp_shift, up_bias)
        packed, mine_pack = pack_inputs(scalars, tok, segment_ids, weights, vectors)
        pack = lax.all_gather(mine_pack, "fsdp", axis=0)
        xs = line_gather(packed)
        xs.append(line_forward(xs[3]))
        near_x, near_y = swap(up_weight, 2), swap(up_weight, 4)
        xs, near_x, near_y, after, pack = lax.optimization_barrier(
            (xs, near_x, near_y, down_weight, pack)
        )
        down = lax.all_gather(after, "fsdp", axis=0)
        half = up_weight.shape[1] // 2
        far = [swap(near_x[:, :half], 4), swap(near_y[:, half:], 2)]
    else:
        seg_row = jnp.pad(segment_ids.astype(BF), ((0, 15), (0, 1024 - CHUNK)))
        packed = jnp.concatenate([tok, seg_row])
        xs = line_gather(packed)
        xs.append(line_forward(xs[3]))
        quarter = jnp.concatenate(
            [
                lax.dynamic_slice_in_dim(m, z * WIDE, WIDE, 1)
                for m in (query_weight, key_weight, value_weight)
            ],
            axis=1,
        )
        whole = lambda m: lax.all_gather(m, "fsdp", axis=0, tiled=True)
        split = lambda m: whole(m).reshape(SHARDS, -1)
        line0 = jnp.concatenate(
            [split(m) for m in (query_bias, value_bias, out_bias, attn_gain, attn_shift, down_bias)],
            axis=1,
        )
        line1 = jnp.concatenate([split(m) for m in (mlp_gain, mlp_shift, up_bias)], axis=1)
        lines = jnp.pad(jnp.stack([line0, line1], axis=1), ((0, 0), (0, 14), (0, 0)))
        pack = jnp.concatenate([whole(quarter).reshape(SHARDS, ROWS, 768), lines], axis=1)
        out_rows = whole(out_weight).reshape(SHARDS, ROWS, 1024)
        wide = lambda m: jnp.pad(m, ((0, 0), (0, 0), (0, 1024 - m.shape[2])))
        pack = jnp.concatenate([out_rows, wide(pack)], axis=1)
        ups = list(whole(up_weight).reshape(SHARDS, ROWS, 4096))
        down = whole(down_weight).reshape(SHARDS, 512, 1024)
    valid = (segment_ids[0] != SEGS - 1).astype(F32)[:, None]

    m0, m1, m2, m3, mixf, lse, qkv, xall, segr = attn_fwd(scalars, xs, pack)
    parts = [m0] + [shift(m, -k) for k, m in ((1, m1), (2, m2), (3, m3))]
    if plane:
        far, m0 = lax.optimization_barrier((far, m0))
        far = jnp.concatenate(far, axis=1)
        ups = []
        for rows in (up_weight, near_x, near_y, far):
            ups += [rows, swap(rows, 1)]
    normed, low, low_rel, scaled, inv, mixed, stats_a = out_project(
        scalars, tok, parts, pack, valid
    )
    acts, slope, result, gh2, sums_m, stats_m = mlp_fwd(
        normed, low, low_rel, mixed, ups, down, pack, cotangent[0], valid
    )
    acts_p = swap(acts, 1)
    grads, gh1, g0, g1, g2, g3, sums_a, ub = mlp_bwd(
        scalars, acts, slope, ups, down, gh2, scaled, inv, pack
    )
    gs = [g0] + [shift(g, k) for k, g in ((1, g1), (2, g2), (3, g3))]
    grads_p = swap(grads, 1)
    d3, d1, d2, d0 = down_grads(scalars, acts, acts_p)
    if plane:
        d_far = swap(d3, 2)
    r3, r1, r2, r0 = rest_grads(scalars, acts, acts_p, grads, grads_p)
    gs, d1, r3, r1, r2, r0 = lax.optimization_barrier((gs, d1, r3, r1, r2, r0))
    if plane:
        r_far = swap(r3, 4)
        d_from_x, r_from_y = swap(d1, 2), swap(r2, 4)
    smalls = (sums_m, sums_a, ub.reshape(1024, 4).T, stats_a, stats_m)
    ig, gw = attn_bwd(scalars, xall, segr, pack, qkv, mixf, lse, gs, smalls)
    if plane:
        ig, gw, d_far, r_far, d_from_x = lax.optimization_barrier(
            (ig, gw, d_far, r_far, d_from_x)
        )
    gw_first = gw
    ig = lax.psum_scatter(ig, "ctx", scatter_dimension=0, tiled=True)
    ig, gw = lax.optimization_barrier((ig, gw))
    q_own = lax.psum_scatter(gw, "fsdp", scatter_dimension=0, tiled=True)
    input_grad = add(gh1, ig)
    q_low = q_own.astype(BF)

    if plane:
        cuts = ((0, 192, 0, 256), (192, 320, 256, 384), (320, 448, 384, 512), (448, 512, 512, 640))
        count = len(cuts)
        sent, pairs, wholes, parts = {}, {}, {}, {}
        q_pieces = None
        for wave in range(count + 3):
            out = {}
            if wave < count:
                a, b, c, d = cuts[wave]
                out["y"] = add(d2[a:b], d_far[a:b]).astype(BF)
                out["x"] = add(r1[c:d], r_far[c:d]).astype(BF)
            if 0 <= wave - 1 < count:
                a, b, c, d = cuts[wave - 1]
                from_y, from_x = sent.pop(wave - 1)
                total = [add(d0[a:b], d_from_x[a:b], from_y), add(r0[c:d], r_from_y[c:d], from_x)]
                out["one"] = jnp.concatenate(total).astype(BF)
            if 0 <= wave - 2 < count:
                out["two"] = pairs.pop(wave - 2)
            if 0 <= wave - 3 < count:
                out["three"] = wholes[wave - 3]
            if wave == 0:
                out["after"] = gw_first
            if wave == 2:
                out["after"] = ig
            if wave == 3:
                out["after"] = q_low
            if wave == count + 1:
                out["q"] = q_low
            out = lax.optimization_barrier(out)
            if "y" in out:
                sent[wave] = (swap(out["y"], 4), swap(out["x"], 2))
            if "one" in out:
                pairs[wave - 1] = add(out["one"], line_in(out["one"])).astype(BF)
            if "two" in out:
                wholes[wave - 2] = add(out["two"], line_cross(out["two"])).astype(BF)
            if "three" in out:
                inner = (z == 1) | (z == 2)
                back = line_out(out["three"])
                parts[wave - 3] = jnp.where(inner, out["three"], back).astype(F32)
            if "q" in out:
                q_pieces = [out["q"]] + [shift(out["q"], k) for k in (1, 2, 3)]
        parts_d = [parts[n][0 : cuts[n][1] - cuts[n][0]] for n in range(count)]
        parts_r = [parts[n][cuts[n][1] - cuts[n][0] :] for n in range(count)]
        parts_r = [parts_r[0][0:ROWS], parts_r[0][ROWS:]] + parts_r[1:]
        grad_down = jnp.concatenate(parts_d)
        grad_up = jnp.concatenate(parts_r[0:4], axis=1)
        grad_out = parts_r[4]
    else:
        other = scalars.at[2].set(1)
        sums_w = (d3, d1, d2, d0, r3, r1, r2, r0)
        second = down_grads(other, acts, acts_p) + rest_grads(other, acts, acts_p, grads, grads_p)
        rows_of = lambda t: ([t[3], t[1], t[2], t[0]], [t[7], t[5], t[6], t[4]])
        down_0, rest_0 = rows_of(sums_w)
        down_1, rest_1 = rows_of(second)
        down_all = 0.5 * jnp.stack([m.astype(F32) for p in zip(down_0, down_1) for m in p])
        rest_all = 0.5 * jnp.stack([m.astype(F32) for p in zip(rest_0, rest_1) for m in p])
        scatter = lambda m: lax.psum_scatter(
            m.astype(BF), "fsdp", scatter_dimension=0, tiled=True
        )
        grad_down = line_sum(scatter(down_all.reshape(4096, 1024)))
        grad_up = line_sum(
            scatter(
                rest_all[:, 0:512]
                .reshape(SHARDS, 4, ROWS, 1024)
                .swapaxes(1, 2)
                .reshape(1024, 4096)
            )
        )
        grad_out = line_sum(scatter(rest_all[:, 512:].reshape(1024, 1024)))
        q_pieces = [q_low] + [shift(q_low, k) for k in (1, 2, 3)]
    if plane:
        done = finish(scalars, q_pieces)
        grad_q, grad_k, grad_v = done[0:3]
        vectors = [v.reshape(-1) for v in done[3:11]]
        up_bias_grad = done[11].T.reshape(-1)
        rms = [v.reshape(()) for v in done[12:15]]
    else:
        table = jnp.take(jnp.stack(q_pieces), (z - jnp.arange(4)) % 4, axis=0)
        extra = add(*q_pieces)[:, 3 * WIDE :]
        cols = lambda n: jnp.concatenate(
            [table[a, :, n * WIDE : (n + 1) * WIDE].astype(F32) for a in range(4)], axis=1
        )
        grad_q, grad_k, grad_v = cols(0), cols(1), cols(2)
        vectors = [extra[:, n] for n in range(8)]
        up_bias_grad = extra[:, 8:12].reshape(-1)
        counted = (16.0 * extra[0, 15] + extra[0, 16]) * 1024
        rms = [jnp.sqrt(extra[0, 12 + n] / counted) for n in range(3)]
    return (
        result[None],
        input_grad[None],
        grad_q,
        vectors[6],
        grad_k,
        grad_v,
        vectors[7],
        grad_out,
        vectors[5],
        vectors[3],
        vectors[4],
        grad_up,
        up_bias_grad,
        grad_down,
        vectors[2],
        vectors[0],
        vectors[1],
        rms[0],
        rms[1],
        rms[2],
    )


def solution(mesh):
    matrix, vector = P("fsdp", None), P("fsdp")
    stream = P("fsdp", "ctx", None)
    placed = (
        stream,
        P("fsdp", "ctx"),
        stream,
        matrix,
        vector,
        matrix,
        matrix,
        vector,
        matrix,
        vector,
        vector,
        vector,
        matrix,
        vector,
        matrix,
        vector,
        vector,
        vector,
    )
    return jax.shard_map(
        per_device,
        mesh=mesh,
        in_specs=placed,
        out_specs=(
            stream,
            stream,
            matrix,
            vector,
            matrix,
            matrix,
            vector,
            matrix,
            vector,
            vector,
            vector,
            matrix,
            vector,
            matrix,
            vector,
            vector,
            vector,
            P(),
            P(),
            P(),
        ),
        check_vma=False,
    )
```

```python
from functools import partial

import jax
import jax.numpy as jnp
from jax import lax
from jax.experimental import pallas as pl
from jax.experimental.pallas import tpu as pltpu
from jax.sharding import PartitionSpec as P

HEADS = 16
HEAD_DIM = 64
SEGS = 8
EPSILON = 1e-05
MASKED = -1000000000.0
SCALE = HEAD_DIM ** (-0.5)
BF = jnp.bfloat16
F32 = jnp.float32

CHUNK = 256
HERE = 4
WIDE = HERE * HEAD_DIM
SHARDS = 8
ROWS = 128
PACK = 2 * ROWS + 16
PARAMS = pltpu.CompilerParams(vmem_limit_bytes=60 * 1024 * 1024)


SMEM_SPEC = pl.BlockSpec(memory_space=pltpu.SMEM)
VMEM_SPEC = pl.BlockSpec(memory_space=pltpu.VMEM)


def dot(a, b, dims=((1,), (0,))):
    return lax.dot_general(a, b, (dims, ((), ())), preferred_element_type=F32)


def vec(small_ref, row, start, size):
    return jnp.concatenate(
        [small_ref[f, row : row + 1, start : start + size].astype(F32) for f in range(SHARDS)],
        axis=1,
    )


def any_spec(shape):
    return pl.BlockSpec(shape, lambda *a: (0,) * len(shape))


def pack_kernel(sc, tok, seg, wq, wk, wv, wout, qb, vb, ob, ag, sh, db, mg, ms, ub, xp, pk):
    z = sc[0]
    cols = pl.ds(pl.multiple_of(z * WIDE, WIDE), WIDE)
    xp[0:CHUNK] = tok[...]
    xp[CHUNK:] = jnp.zeros((16, 1024), BF)
    xp[CHUNK : CHUNK + 1, 0:CHUNK] = seg[...].astype(F32).astype(BF)
    pk[0:ROWS] = wout[...]
    for n, w in enumerate((wq, wk, wv)):
        pk[ROWS : 2 * ROWS, WIDE * n : WIDE * n + WIDE] = w[:, cols]
    pk[ROWS : 2 * ROWS, 3 * WIDE :] = jnp.zeros((ROWS, 1024 - 3 * WIDE), BF)
    pk[2 * ROWS :] = jnp.zeros((16, 1024), BF)
    at = slice(2 * ROWS, 2 * ROWS + 1)
    for n, vector in enumerate((qb, vb, ob, ag, sh, db)):
        pk[at, 128 * n : 128 * n + 128] = vector[...]
    at = slice(2 * ROWS + 1, 2 * ROWS + 2)
    for n, vector in enumerate((mg, ms)):
        pk[at, 128 * n : 128 * n + 128] = vector[...]
    pk[at, 256:768] = ub[...]


def pack_inputs(scalars, tok, seg, weights, vectors):
    shape = jax.ShapeDtypeStruct
    return pl.pallas_call(
        pack_kernel,
        name="pack_inputs",
        in_specs=[SMEM_SPEC] + [VMEM_SPEC] * 15,
        out_specs=(VMEM_SPEC,) * 2,
        out_shape=(shape((CHUNK + 16, 1024), BF), shape((PACK, 1024), BF)),
        compiler_params=PARAMS,
    )(scalars, tok, seg, *weights, *[v[None] for v in vectors])


def segment_setup(rows, segc, ends):
    for a in range(4):
        row = rows[a][0:1, :]
        segc[a] = jnp.transpose(jnp.broadcast_to(row, (128, CHUNK)))
        ends[0, a] = jnp.min(row).astype(jnp.int32)
        ends[1, a] = jnp.max(row).astype(jnp.int32)


def key_range(ends, i):
    low = jnp.int32(0)
    high = jnp.int32(4)
    for j in range(4):
        low = low + (ends[1, j] < ends[0, i]).astype(jnp.int32)
        high = high - (ends[0, j] > ends[1, i]).astype(jnp.int32)
    return low, high


def one_head(x, h):
    pair = x[:, 128 * (h // 2) : 128 * (h // 2) + 128]
    lane = lax.broadcasted_iota(jnp.int32, pair.shape, 1)
    return jnp.where((lane < HEAD_DIM) == (h % 2 == 0), pair, jnp.zeros_like(pair))


def attn_fwd_kernel(
    sc,
    x0,
    right,
    left,
    x2,
    far,
    w,
    small,
    m0,
    m1,
    m2,
    m3,
    mixt,
    lse,
    qm,
    kv,
    kt,
    xall,
    segr,
    vt,
    acc,
    scores,
    probs,
    segc,
    ends,
):
    z = sc[0]

    def place(k, src):
        a = lax.rem(z - k + 4, 4)
        xall[a] = src[0:CHUNK, :]
        segr[a] = jnp.broadcast_to(
            src[CHUNK : CHUNK + 16, 0:CHUNK].astype(F32)[0:1, :], (8, CHUNK)
        )

    place(0, x0)
    place(2, x2)
    for k, usual, end in ((1, right, 0), (3, left, 3)):
        pl.when(z == end)(partial(place, k, far))
        pl.when(z != end)(partial(place, k, usual))
    segment_setup(segr, segc, ends)
    weight = w[...].reshape(SHARDS * ROWS, 3 * WIDE)
    first = small[2 * z].astype(F32)
    second = small[2 * z + 1].astype(F32)
    qb = jnp.concatenate([first[0:1, 0:128], second[0:1, 0:128]], axis=1)
    vb = jnp.concatenate([first[0:1, 128:256], second[0:1, 128:256]], axis=1)
    for n in range(4):
        at = slice(n * CHUNK, (n + 1) * CHUNK)
        prod = dot(xall[n], weight)
        q = ((prod[:, 0:WIDE] + qb).astype(BF).astype(F32) * SCALE).astype(BF)
        kk = prod[:, WIDE : 2 * WIDE].astype(BF)
        v = (prod[:, 2 * WIDE :] + vb).astype(BF)
        for h in range(HERE):
            qm[h, at, :] = one_head(q, h)
        kv[at, 0:WIDE] = kk
        kv[at, WIDE:] = v
        kt[:, at] = jnp.transpose(kk)
        vt[:, at] = jnp.transpose(v)

    def q_chunk(i, carry):
        rows = pl.ds(pl.multiple_of(i * CHUNK, CHUNK), CHUNK)
        low, high = key_range(ends, i)
        row = segr[i][0:1, :]

        acc[...] = jnp.zeros_like(acc)

        def key_chunk(j, state):
            keys = pl.ds(pl.multiple_of(j * CHUNK, CHUNK), CHUNK)
            col = segc[j]
            mask = jnp.concatenate([col, col], axis=1) == row
            new, fixes = [], []
            for h in range(HERE):
                pair = slice(128 * (h // 2), 128 * (h // 2) + 128)
                s = dot(kv[keys, pair], qm[h, rows, :], ((1,), (1,)))
                s = jnp.where(mask, s, MASKED)
                scores[h] = s
                new.append(jnp.maximum(state[h][0], jnp.max(s, axis=0, keepdims=True)))
            out = []
            for h in range(HERE):
                m, l = state[h]
                total = jnp.zeros((1, CHUNK), F32)
                for t in range(4):
                    tile = slice(64 * t, 64 * t + 64)
                    p = jnp.exp(scores[h, tile, :] - new[h])
                    total = total + jnp.sum(p, axis=0, keepdims=True)
                    probs[h, tile, :] = p.astype(BF)
                fixes.append(jnp.exp(m - new[h]))
                out.append((new[h], l * fixes[h] + total))
            for h in range(HERE):
                head = slice(h * HEAD_DIM, (h + 1) * HEAD_DIM)
                acc[head, :] = acc[head, :] * fixes[h] + dot(vt[head, keys], probs[h])
            return tuple(out)

        init = tuple(
            (jnp.full((1, CHUNK), MASKED, F32), jnp.zeros((1, CHUNK), F32)) for _ in range(HERE)
        )
        state = lax.fori_loop(low, high, key_chunk, init)
        for h in range(HERE):
            m, l = state[h]
            head = slice(h * HEAD_DIM, (h + 1) * HEAD_DIM)
            mixt[head, rows] = acc[head, :] / l
            lse[h : h + 1, rows] = m + jnp.log(l)
        return carry

    lax.fori_loop(0, 4, q_chunk, 0)
    for k, out in enumerate((m0, m1, m2, m3)):
        a = pl.multiple_of(lax.rem(z - k + 4, 4) * CHUNK, CHUNK)
        out[...] = jnp.transpose(mixt[:, pl.ds(a, CHUNK)].astype(BF))


OUT_SPEC = pl.BlockSpec((SHARDS, ROWS, 1024), lambda *a: (0, 0, 0))
QKV_SPEC = pl.BlockSpec((SHARDS, ROWS, 3 * WIDE), lambda *a: (0, 1, 0))
SMALL_SPEC = pl.BlockSpec((SHARDS, 16, 3 * WIDE), lambda *a: (0, 2 * ROWS // 16, 0))


def attn_fwd(scalars, xs, pack):
    shape = jax.ShapeDtypeStruct
    return pl.pallas_call(
        attn_fwd_kernel,
        name="attn_fwd",
        out_shape=(shape((CHUNK, WIDE), BF),) * 4
        + (
            shape((WIDE, 4 * CHUNK), F32),
            shape((8, 4 * CHUNK), F32),
            shape((HERE, 4 * CHUNK, 128), BF),
            shape((4 * CHUNK, 2 * WIDE), BF),
            shape((WIDE, 4 * CHUNK), BF),
            shape((4, CHUNK, 1024), BF),
            shape((4, 8, CHUNK), F32),
        ),
        grid=(1,),
        in_specs=[SMEM_SPEC] + [any_spec((CHUNK + 16, 1024))] * 5 + [QKV_SPEC, SMALL_SPEC],
        out_specs=(any_spec((CHUNK, WIDE)),) * 4
        + (
            any_spec((WIDE, 4 * CHUNK)),
            any_spec((8, 4 * CHUNK)),
            any_spec((HERE, 4 * CHUNK, 128)),
            any_spec((4 * CHUNK, 2 * WIDE)),
            any_spec((WIDE, 4 * CHUNK)),
            any_spec((4, CHUNK, 1024)),
            any_spec((4, 8, CHUNK)),
        ),
        scratch_shapes=[
            pltpu.VMEM((WIDE, 4 * CHUNK), BF),
            pltpu.VMEM((WIDE, CHUNK), F32),
            pltpu.VMEM((HERE, CHUNK, CHUNK), F32),
            pltpu.VMEM((HERE, CHUNK, CHUNK), BF),
            pltpu.VMEM((4, CHUNK, 128), F32),
            pltpu.SMEM((2, 4), jnp.int32),
        ],
        compiler_params=PARAMS,
    )(scalars, *xs, pack, pack)


def normalise(h):
    centre = h - jnp.mean(h, axis=-1, keepdims=True)
    inverse = lax.rsqrt(jnp.mean(centre * centre, axis=-1, keepdims=True) + EPSILON)
    return centre * inverse, inverse


def norm_pullback(upstream, scaled, inverse, gain):
    e = upstream * gain
    return inverse * (
        e
        - jnp.mean(e, axis=-1, keepdims=True)
        - scaled * jnp.mean(e * scaled, axis=-1, keepdims=True)
    )


def relative(f, sc):
    return 2 * jnp.bitwise_xor(sc[1], f // 2) + jnp.bitwise_xor(sc[2], f % 2)


TILE = 16


def eight(x):
    return jnp.sum(x.reshape(TILE // 8, 8, x.shape[1]), axis=0)


def out_kernel(
    sc, tok, r0, r1, r2, r3, w, small, valid, normed, low, low_rel, scaled, inv, mixed, stats, acc
):
    z = sc[0]
    for k, r in enumerate((r0, r1, r2, r3)):
        a = lax.rem(z + k, 4)
        mixed[:, pl.ds(pl.multiple_of(a * WIDE, WIDE), WIDE)] = r[...]
    acc[...] = dot(mixed[...], w[...].reshape(1024, 1024))
    bias, gain, shift_by = vec(small, 0, 256, 128), vec(small, 0, 384, 128), vec(small, 0, 512, 128)

    def tile(t, carry):
        rows = pl.ds(pl.multiple_of(t * TILE, TILE), TILE)
        branch = acc[rows, :] + bias
        x = tok[rows, :].astype(F32)
        n, inverse = normalise(x + branch)
        y = n * gain + shift_by
        normed[rows, :] = y
        low[rows, :] = y.astype(BF)
        scaled[rows, :] = n
        inv[rows, :] = jnp.broadcast_to(inverse, (TILE, 128))
        ok = valid[rows, :]
        return carry[0] + eight(ok * x * x), carry[1] + eight(ok * branch * branch)

    zero = jnp.zeros((8, 1024), F32)
    stream, branch = lax.fori_loop(0, CHUNK // TILE, tile, (zero, zero), unroll=4)
    for f in range(SHARDS):
        at = pl.multiple_of(relative(f, sc) * ROWS, ROWS)
        low_rel[:, pl.ds(at, ROWS)] = low[:, ROWS * f : ROWS * f + ROWS]
    lane = lax.broadcasted_iota(jnp.int32, (8, 128), 1)
    stats[...] = jnp.where(
        lane == 0,
        jnp.sum(stream),
        jnp.where(
            lane == 1, jnp.sum(branch), jnp.where(lane == 3, jnp.sum(valid[...]), 0.0)
        ),
    )


def out_project(scalars, tok, parts, pack, valid):
    shape = jax.ShapeDtypeStruct
    full = lambda *s: any_spec(s)
    return pl.pallas_call(
        out_kernel,
        name="out_project",
        grid=(1,),
        out_shape=(
            shape((CHUNK, 1024), F32),
            shape((CHUNK, 1024), BF),
            shape((CHUNK, 1024), BF),
            shape((CHUNK, 1024), F32),
            shape((CHUNK, 128), F32),
            shape((CHUNK, 1024), BF),
            shape((8, 128), F32),
        ),
        in_specs=[SMEM_SPEC, full(CHUNK, 1024)]
        + [full(CHUNK, WIDE)] * 4
        + [OUT_SPEC, SMALL_SPEC, full(CHUNK, 1)],
        out_specs=(
            full(CHUNK, 1024),
            full(CHUNK, 1024),
            full(CHUNK, 1024),
            full(CHUNK, 1024),
            full(CHUNK, 128),
            full(CHUNK, 1024),
            full(8, 128),
        ),
        scratch_shapes=[pltpu.VMEM((CHUNK, 1024), F32)],
        compiler_params=PARAMS,
    )(scalars, tok, *parts, pack, pack, valid)


UP_SPECS = [pl.BlockSpec((ROWS, 512), lambda j: (0, j))] * SHARDS


def gate_kernel(low, low_rel, mixed, *refs):
    ups = refs[0:SHARDS]
    small, acts, slope, pre = refs[SHARDS:]
    j = pl.program_id(0)
    pre[...] = dot(low_rel[...], jnp.concatenate([u[...] for u in ups]))
    bias = small[j, 1:2, 256:768].astype(F32)
    cols = pl.ds(pl.multiple_of((j % 2) * 512, 512), 512)
    for t in range(CHUNK // TILE):
        rows = slice(TILE * t, TILE * t + TILE)
        gate = pre[rows, :] + bias
        cdf = 0.5 * (1.0 + lax.erf(gate * (2.0 ** -0.5)))
        acts[j // 2, rows, cols] = (gate * cdf).astype(BF)
        slope[rows, :] = cdf + gate * (jnp.exp(-0.5 * gate * gate) * 0.3989422804014327)

    @pl.when(j == 0)
    def _():
        acts[4] = low[...]
        acts[5] = mixed[...]


def mlp_gate(low, low_rel, mixed, ups, pack):
    shape = jax.ShapeDtypeStruct
    full = lambda *s: any_spec(s)
    return pl.pallas_call(
        gate_kernel,
        name="mlp_gate",
        grid=(SHARDS,),
        out_shape=(shape((6, CHUNK, 1024), BF), shape((CHUNK, 4096), F32)),
        in_specs=[full(CHUNK, 1024)] * 3 + UP_SPECS + [SMALL_SPEC],
        out_specs=(full(6, CHUNK, 1024), pl.BlockSpec((CHUNK, 512), lambda j: (0, j))),
        scratch_shapes=[pltpu.VMEM((CHUNK, 512), F32)],
        compiler_params=PARAMS,
    )(low, low_rel, mixed, *ups, pack)


def mlp_tail_kernel(sc, acts, down_cols, down_rows, slope, small, valid, inv, *refs):
    far = refs[0 : SHARDS + 4]
    (
        out,
        grads,
        gh1,
        g0,
        g1,
        g2,
        g3,
        sums_m,
        stats,
        sums_a,
        ub,
        acc,
        gh2,
        gm,
        gg_all,
        pre,
        total,
        held,
        normed,
        cot,
        scaled,
        wout,
        sems,
    ) = refs[SHARDS + 4 :]
    s = pl.program_id(0)
    z = sc[0]
    targets = [normed, cot, scaled, wout] + [held.at[n] for n in range(SHARDS)]
    sources = [far[0], far[1], far[2], far[3].at[:, 0:ROWS, :]] + list(far[4:])
    copies = [
        pltpu.make_async_copy(src, dst, sems.at[n])
        for n, (src, dst) in enumerate(zip(sources, targets))
    ]
    zero = jnp.zeros((8, 1024), F32)

    def tiles(body, count):
        totals = lax.fori_loop(0, CHUNK // TILE, body, (zero,) * count, unroll=4)
        return [jnp.sum(t, axis=0, keepdims=True) for t in totals]

    @pl.when(s == 0)
    def _():
        for copy in copies:
            copy.start()

    @pl.when(s < 4)
    def _():
        hidden = jnp.concatenate([acts[b] for b in range(4)], axis=1)
        cols = pl.ds(pl.multiple_of(jnp.minimum(s, 3) * 256, 256), 256)
        acc[:, cols] = dot(hidden, down_cols[...].reshape(4096, 256))

    @pl.when(s == 3)
    def _():
        for copy in copies[0:2]:
            copy.wait()
        bias, gain, shift_by = vec(small, 0, 640, 128), vec(small, 1, 0, 128), vec(small, 1, 128, 128)

        def tile(t, carry):
            rows = pl.ds(pl.multiple_of(t * TILE, TILE), TILE)
            branch = acc[rows, :] + bias
            unit, inverse = normalise(normed[rows, :] + branch)
            out[rows, :] = (unit * gain + shift_by).astype(BF)
            ok = valid[rows, :]
            u = cot[rows, :].astype(F32) * ok
            g = norm_pullback(u, unit, inverse, gain)
            gh2[rows, :] = g
            g_low = g.astype(BF)
            gm[rows, :] = g_low
            terms = (u * unit, u, g_low.astype(F32), ok * branch * branch)
            return tuple(c + eight(v) for c, v in zip(carry, terms))

        totals = tiles(tile, 4)
        sums_m[...] = jnp.zeros_like(sums_m)
        for at in range(3):
            sums_m[at : at + 1, :] = totals[at]
        lane = lax.broadcasted_iota(jnp.int32, (8, 128), 1)
        stats[...] = jnp.where(lane == 2, jnp.sum(totals[3]), 0.0)

    @pl.when((s >= 4) & (s < 12))
    def _():
        j = jnp.clip(s - 4, 0, SHARDS - 1)
        pre[...] = dot(gm[...], down_rows[...].reshape(512, 1024), ((1,), (1,)))
        cols = pl.ds(pl.multiple_of((j % 2) * 512, 512), 512)
        total_ub = jnp.zeros((8, 512), F32)
        for t in range(CHUNK // TILE):
            rows = slice(TILE * t, TILE * t + TILE)
            gg = (pre[rows, :] * slope[rows, :]).astype(BF)
            gg_all[j // 2, rows, cols] = gg
            grads[0, rows, cols] = gg
            total_ub = total_ub + eight(gg.astype(F32))
        ub[pl.ds(j, 1)] = jnp.sum(total_ub, axis=0, keepdims=True).reshape(1, 1, 512)

    @pl.when(s == 12)
    def _():
        grads[0] = gm[...]
        for copy in copies[2:]:
            copy.wait()

    @pl.when(s >= 12)
    def _():
        j = jnp.clip(s - 12, 0, 3)
        rows = held[pl.ds(2 * j, 2)].reshape(2 * ROWS, 4096)
        gg = jnp.concatenate([gg_all[b] for b in range(4)], axis=1)
        part = dot(gg, rows, ((1,), (1,)))
        pair = jnp.bitwise_xor(sc[1], j)
        for t in range(2):
            f = 2 * pair + jnp.bitwise_xor(sc[2], t)
            to = pl.ds(pl.multiple_of(f * ROWS, ROWS), ROWS)
            total[:, to] = part[:, ROWS * t : ROWS * t + ROWS]

    @pl.when(s == 15)
    def _():
        gain = vec(small, 0, 384, 128)

        def tile(t, carry):
            rows = pl.ds(pl.multiple_of(t * TILE, TILE), TILE)
            u = gh2[rows, :] + total[rows, :]
            n = scaled[rows, :]
            g = norm_pullback(u, n, inv[rows, 0:1], gain)
            gh1[rows, :] = g
            g_low = g.astype(BF)
            grads[0, rows, :] = g_low
            terms = (u * n, u, g_low.astype(F32))
            return tuple(c + eight(v) for c, v in zip(carry, terms))

        totals = tiles(tile, 3)
        sums_a[...] = jnp.zeros_like(sums_a)
        for at in range(3):
            sums_a[at : at + 1, :] = totals[at]
        g_low = grads[0]
        for k, g_out in enumerate((g0, g1, g2, g3)):
            a = lax.rem(z + k, 4)
            rows = wout[pl.ds(2 * a, 2)].reshape(WIDE, 1024)
            g_out[...] = dot(g_low, rows, ((1,), (1,))).astype(BF)


def mlp_tail(scalars, acts, slope, ups, down, normed, scaled, inv, pack, cot, valid):
    shape = jax.ShapeDtypeStruct
    full = lambda *s: any_spec(s)
    block = lambda s: jnp.clip(s - 4, 0, SHARDS - 1)

    def grads_at(s):
        return (jnp.where(s < 12, block(s) // 2, jnp.where(s < 15, 5, 4)), 0, 0)

    return pl.pallas_call(
        mlp_tail_kernel,
        name="mlp_tail",
        grid=(16,),
        in_specs=[
            SMEM_SPEC,
            full(4, CHUNK, 1024),
            pl.BlockSpec((SHARDS, 512, 256), lambda s: (0, 0, jnp.minimum(s, 3))),
            pl.BlockSpec((1, 512, 1024), lambda s: (block(s), 0, 0)),
            pl.BlockSpec((CHUNK, 512), lambda s: (0, block(s))),
            SMALL_SPEC,
            full(CHUNK, 1),
            full(CHUNK, 128),
        ]
        + [pl.BlockSpec(memory_space=pl.ANY)] * (SHARDS + 4),
        out_specs=(
            full(CHUNK, 1024),
            pl.BlockSpec((1, CHUNK, 1024), grads_at),
            full(CHUNK, 1024),
        )
        + (full(CHUNK, WIDE),) * 4
        + (full(8, 1024), full(8, 128), full(8, 1024), full(SHARDS, 1, 512)),
        out_shape=(
            shape((CHUNK, 1024), BF),
            shape((6, CHUNK, 1024), BF),
            shape((CHUNK, 1024), F32),
        )
        + (shape((CHUNK, WIDE), BF),) * 4
        + (
            shape((8, 1024), F32),
            shape((8, 128), F32),
            shape((8, 1024), F32),
            shape((SHARDS, 1, 512), F32),
        ),
        scratch_shapes=[
            pltpu.VMEM((CHUNK, 1024), F32),
            pltpu.VMEM((CHUNK, 1024), F32),
            pltpu.VMEM((CHUNK, 1024), BF),
            pltpu.VMEM((4, CHUNK, 1024), BF),
            pltpu.VMEM((CHUNK, 512), F32),
            pltpu.VMEM((CHUNK, 1024), F32),
            pltpu.VMEM((SHARDS, ROWS, 4096), BF),
            pltpu.VMEM((CHUNK, 1024), F32),
            pltpu.VMEM((CHUNK, 1024), BF),
            pltpu.VMEM((CHUNK, 1024), F32),
            pltpu.VMEM((SHARDS, ROWS, 1024), BF),
            pltpu.SemaphoreType.DMA((SHARDS + 4,)),
        ],
        compiler_params=PARAMS,
    )(scalars, acts, down, down, slope, pack, valid, inv, normed, cot, scaled, pack, *ups)


REST = 640


def step_shard(j, sc):
    rel = jnp.where(j == 0, 3, jnp.where(j >= 3, 0, j))
    return 2 * jnp.bitwise_xor(sc[1], rel) + sc[2]


def product(left, right, res):
    for n in range(4):
        cols = slice(256 * n, 256 * n + 256)
        res[:, cols] = dot(left[...], right[:, cols]).astype(BF)


def down_kernel(sc, ho, hp, go, gp, d3, d1, d2, d0, left, right, res):
    s = pl.program_id(0)

    @pl.when(s == 0)
    def _():
        right[0:CHUNK] = go[0]
        right[CHUNK:] = gp[0]

    left[:, 0:CHUNK] = jnp.transpose(ho[0])
    left[:, CHUNK:] = jnp.transpose(hp[0])
    product(left, right, res)
    for n, out in enumerate((d3, d1, d2, d0)):

        @pl.when(s == n)
        def _():
            out[...] = res[...]


def down_grads(scalars, acts, acts_p, grads, grads_p):
    shape = jax.ShapeDtypeStruct
    full = lambda *s: pl.BlockSpec(s, lambda j, sc: (0,) * len(s))

    def hid(j, sc):
        f = step_shard(j, sc)
        return (f // 2, 0, f % 2)

    hidden = pl.BlockSpec((1, CHUNK, 512), hid)
    grad = pl.BlockSpec((1, CHUNK, 1024), lambda j, sc: (5, 0, 0))
    return pl.pallas_call(
        down_kernel,
        name="down_grads",
        grid_spec=pltpu.PrefetchScalarGridSpec(
            num_scalar_prefetch=1,
            grid=(4,),
            in_specs=[hidden, hidden, grad, grad],
            out_specs=(full(512, 1024),) * 4,
            scratch_shapes=[
                pltpu.VMEM((512, 2 * CHUNK), BF),
                pltpu.VMEM((2 * CHUNK, 1024), BF),
                pltpu.VMEM((512, 1024), BF),
            ],
        ),
        out_shape=(shape((512, 1024), BF),) * 4,
        compiler_params=PARAMS,
    )(scalars, acts, acts_p, grads, grads_p)


def rest_kernel(sc, lo, lp, go, gp, r3, r1, r2, r0, low_sel, mix_sel, right, res):
    s = pl.program_id(0)
    chip, core = sc[1], sc[2]

    @pl.when(s == 0)
    def _():
        for r in range(4):
            at = pl.multiple_of((2 * jnp.bitwise_xor(chip, r) + core) * ROWS, ROWS)
            to = slice(ROWS * r, ROWS * r + ROWS)
            for n, out in enumerate((low_sel, mix_sel)):
                out[to, 0:CHUNK] = jnp.transpose(lo[n, :, pl.ds(at, ROWS)])
                out[to, CHUNK:] = jnp.transpose(lp[n, :, pl.ds(at, ROWS)])

    @pl.when(s == 4)
    def _():
        low_sel[...] = mix_sel[...]

    right[0:CHUNK] = go[0]
    right[CHUNK:] = gp[0]
    product(low_sel, right, res)
    for r, out in enumerate((r0, r1, r2, r3)):
        out[...] = res[ROWS * r : ROWS * r + ROWS, :]


def rest_grads(scalars, acts, acts_p, grads, grads_p):
    shape = jax.ShapeDtypeStruct
    full = lambda *s: pl.BlockSpec(s, lambda j, sc: (0,) * len(s))
    flat = pl.BlockSpec((pl.Element(2), pl.Element(CHUNK), pl.Element(1024)), lambda j, sc: (4, 0, 0))
    grad = pl.BlockSpec((1, CHUNK, 1024), lambda j, sc: (j, 0, 0))
    return pl.pallas_call(
        rest_kernel,
        name="rest_grads",
        grid_spec=pltpu.PrefetchScalarGridSpec(
            num_scalar_prefetch=1,
            grid=(5,),
            in_specs=[flat, flat, grad, grad],
            out_specs=(pl.BlockSpec((ROWS, 1024), lambda j, sc: (j, 0)),) * 4,
            scratch_shapes=[
                pltpu.VMEM((512, 2 * CHUNK), BF),
                pltpu.VMEM((512, 2 * CHUNK), BF),
                pltpu.VMEM((2 * CHUNK, 1024), BF),
                pltpu.VMEM((512, 1024), BF),
            ],
        ),
        out_shape=(shape((REST, 1024), BF),) * 4,
        compiler_params=PARAMS,
    )(scalars, acts, acts_p, grads, grads_p)


def attn_bwd_kernel(
    sc,
    xall,
    segr,
    w,
    qm,
    kv,
    kt,
    mixt,
    lse,
    g0,
    g1,
    g2,
    g3,
    sums_m,
    sums_a,
    ubt,
    stats_a,
    stats_m,
    ig,
    gw_out,
    small,
    segc,
    ends,
    gs,
    dq,
    dqt,
    dk,
    dv,
    delta,
    dall,
    gw,
    scores,
    slopes,
    probs,
    pulls,
):
    z = sc[0]
    segment_setup(segr, segc, ends)
    dk[...] = jnp.zeros_like(dk)
    dv[...] = jnp.zeros_like(dv)
    for k, g in enumerate((g0, g1, g2, g3)):
        rows = pl.ds(pl.multiple_of(lax.rem(z - k + 4, 4) * CHUNK, CHUNK), CHUNK)
        turned = jnp.transpose(g[...])
        for h in range(HERE):
            head = slice(h * HEAD_DIM, (h + 1) * HEAD_DIM)
            gs[h, rows, :] = one_head(g[...], h)
            prod = turned[head, :].astype(F32) * mixt[head, rows]
            delta[h : h + 1, rows] = jnp.sum(prod, axis=0, keepdims=True)

    def q_chunk(i, carry):
        rows = pl.ds(pl.multiple_of(i * CHUNK, CHUNK), CHUNK)
        low, high = key_range(ends, i)
        row = segr[i][0:1, :]
        dqt[...] = jnp.zeros_like(dqt)

        def key_chunk(j, inner):
            keys = pl.ds(pl.multiple_of(j * CHUNK, CHUNK), CHUNK)
            col = segc[j]
            mask = jnp.concatenate([col, col], axis=1) == row
            for h in range(HERE):
                low_lane = 128 * (h // 2)
                pair = slice(low_lane, low_lane + 128)
                scores[h] = dot(kv[keys, pair], qm[h, rows, :], ((1,), (1,)))
                wide = slice(WIDE + low_lane, WIDE + low_lane + 128)
                slopes[h] = dot(kv[keys, wide], gs[h, rows, :], ((1,), (1,)))
            for h in range(HERE):
                log, shift_by = lse[h : h + 1, rows], delta[h : h + 1, rows]
                for t in range(4):
                    tile = slice(64 * t, 64 * t + 64)
                    p = jnp.where(mask[tile, :], jnp.exp(scores[h, tile, :] - log), 0.0)
                    probs[h, tile, :] = p.astype(BF)
                    pulls[h, tile, :] = (p * (slopes[h, tile, :] - shift_by)).astype(BF)
            for h in range(HERE):
                head = slice(h * HEAD_DIM, (h + 1) * HEAD_DIM)
                pair = slice(128 * (h // 2), 128 * (h // 2) + 128)
                dv[keys, pair] += dot(probs[h], gs[h, rows, :])
                dk[keys, pair] += dot(pulls[h], qm[h, rows, :])
                dqt[head, :] += dot(kt[head, keys], pulls[h])
            return inner

        lax.fori_loop(low, high, key_chunk, 0)
        dq[...] = (dqt[...] * SCALE).astype(BF)
        dall[rows, 0:WIDE] = jnp.transpose(dq[...])
        return carry

    lax.fori_loop(0, 4, q_chunk, 0)
    dall[:, WIDE : 2 * WIDE] = dk[...].astype(BF)
    dall[:, 2 * WIDE :] = dv[...].astype(BF)
    here = pl.ds(pl.multiple_of(z * WIDE, WIDE), WIDE)
    small[...] = jnp.zeros_like(small)
    small[0:3, :] = sums_m[0:3, :]
    small[3:6, :] = sums_a[0:3, :]
    small[6:7, here] = jnp.sum(dall[:, 0:WIDE].astype(F32), axis=0, keepdims=True)
    small[7:8, here] = jnp.sum(dall[:, 2 * WIDE :].astype(F32), axis=0, keepdims=True)
    small[8:12, :] = ubt[...]
    every = lambda value: jnp.broadcast_to(value, (1, 1024))
    small[12:13, :] = every(stats_a[0:1, 0:1])
    small[13:14, :] = every(stats_a[0:1, 1:2])
    small[14:15, :] = every(stats_m[0:1, 2:3])
    count = stats_a[0:1, 3:4]
    high = jnp.floor(count * 0.0625)
    small[15:16, :] = every(high)
    small[16:17, :] = every(count - 16.0 * high)
    gw_out[:, 3 * WIDE :] = jnp.transpose(small[...]).astype(BF)
    weight = w[...].reshape(SHARDS * ROWS, 3 * WIDE)
    for k in range(4):
        rows = slice(CHUNK * k, CHUNK * k + CHUNK)
        d = dall[rows, :]
        ig[rows, :] = dot(d, weight, ((1,), (1,))).astype(BF)
        part = dot(xall[k], d, ((0,), (0,)))
        if k == 0:
            gw[...] = part
        else:
            gw[...] += part
    gw_out[:, 0 : 3 * WIDE] = gw[...].astype(BF)


def attn_bwd(scalars, xall, segr, pack, qm, kv, kt, mixt, lse, gs, smalls):
    shape = jax.ShapeDtypeStruct
    return pl.pallas_call(
        attn_bwd_kernel,
        name="attn_bwd",
        out_shape=(shape((1024, 1024), BF), shape((1024, 3 * WIDE + 128), BF)),
        grid=(1,),
        in_specs=[SMEM_SPEC]
        + [
            any_spec((4, CHUNK, 1024)),
            any_spec((4, 8, CHUNK)),
            QKV_SPEC,
            any_spec((HERE, 4 * CHUNK, 128)),
            any_spec((4 * CHUNK, 2 * WIDE)),
            any_spec((WIDE, 4 * CHUNK)),
            any_spec((WIDE, 4 * CHUNK)),
            any_spec((8, 4 * CHUNK)),
        ]
        + [any_spec((CHUNK, WIDE))] * 4
        + [any_spec((8, 1024)), any_spec((8, 1024)), any_spec((4, 1024))]
        + [any_spec((8, 128))] * 2,
        out_specs=(any_spec((1024, 1024)), any_spec((1024, 3 * WIDE + 128))),
        scratch_shapes=[
            pltpu.VMEM((128, 1024), F32),
            pltpu.VMEM((4, CHUNK, 128), F32),
            pltpu.SMEM((2, 4), jnp.int32),
            pltpu.VMEM((HERE, 4 * CHUNK, 128), BF),
            pltpu.VMEM((WIDE, CHUNK), BF),
            pltpu.VMEM((WIDE, CHUNK), F32),
            pltpu.VMEM((4 * CHUNK, WIDE), F32),
            pltpu.VMEM((4 * CHUNK, WIDE), F32),
            pltpu.VMEM((8, 4 * CHUNK), F32),
            pltpu.VMEM((4 * CHUNK, 768), BF),
            pltpu.VMEM((1024, 768), F32),
            pltpu.VMEM((HERE, CHUNK, CHUNK), F32),
            pltpu.VMEM((HERE, CHUNK, CHUNK), F32),
            pltpu.VMEM((HERE, CHUNK, CHUNK), BF),
            pltpu.VMEM((HERE, CHUNK, CHUNK), BF),
        ],
        compiler_params=PARAMS,
    )(scalars, xall, segr, pack, qm, kv, kt, mixt, lse, *gs, *smalls)


def finish_kernel(sc, *refs):
    z = sc[0]
    pieces, (gq, gk, gv), vectors, ub, rms = refs[0:4], refs[4:7], refs[7:15], refs[15], refs[16:19]
    for k, piece in enumerate(pieces):
        cols = pl.ds(pl.multiple_of(lax.rem(z - k + 4, 4) * WIDE, WIDE), WIDE)
        for n, out in enumerate((gq, gk, gv)):
            out[:, cols] = piece[:, WIDE * n : WIDE * n + WIDE].astype(F32)
    extra = pieces[0][:, 3 * WIDE :].astype(F32)
    for piece in pieces[1:]:
        extra = extra + piece[:, 3 * WIDE :].astype(F32)
    extra = jnp.transpose(extra)
    for n, out in enumerate(vectors):
        out[...] = extra[n : n + 1, :]
    ub[...] = extra[8:12, :]
    counted = (16.0 * extra[15:16, 0:1] + extra[16:17, 0:1]) * 1024.0
    for n, out in enumerate(rms):
        out[...] = jnp.sqrt(extra[12 + n : 13 + n, 0:1] / counted)


def finish(scalars, pieces):
    shape = jax.ShapeDtypeStruct
    shapes = [(ROWS, 1024)] * 3 + [(1, ROWS)] * 8 + [(4, ROWS)] + [(1, 1)] * 3
    return pl.pallas_call(
        finish_kernel,
        name="finish",
        out_shape=tuple(shape(n, F32) for n in shapes),
        in_specs=[SMEM_SPEC] + [VMEM_SPEC] * 4,
        out_specs=(VMEM_SPEC,) * len(shapes),
        compiler_params=PARAMS,
    )(scalars, *pieces)


def line_gather(x):
    right = lax.ppermute(x, "ctx", [(0, 1), (1, 2), (2, 3)])
    left = lax.ppermute(x, "ctx", [(1, 0), (2, 1), (3, 2)])
    two = lax.ppermute(x, "ctx", [(0, 2), (1, 3), (2, 0), (3, 1)])
    return [x, right, left, two]


def line_forward(two):
    return lax.ppermute(two, "ctx", [(1, 0), (2, 3)])


def shift(x, k):
    n = lax.axis_size("ctx")
    return lax.ppermute(x, "ctx", [(i, (i + k) % n) for i in range(n)])


def swap(x, bits):
    return lax.ppermute(x, "fsdp", [(i, i ^ bits) for i in range(lax.axis_size("fsdp"))])


def add(*terms):
    total = terms[0].astype(F32)
    for term in terms[1:]:
        total = total + term.astype(F32)
    return total


def neighbour(x, bits):
    return lax.ppermute(x, "ctx", [(i, i ^ bits) for i in range(4)])


def half_sum(terms, which):
    half = terms[0].shape[0] // 2
    return add(*[lax.dynamic_slice_in_dim(t, which * half, half, 0) for t in terms])


class LineSum:
    def __init__(self, *terms):
        self.terms = terms
        self.odd = lax.axis_index("ctx") % 2

    def first(self):
        return half_sum(self.terms, 1 - self.odd).astype(BF)

    def second(self, got):
        self.pair = add(half_sum(self.terms, self.odd), got).astype(BF)
        return self.pair

    def third(self, got):
        self.whole = add(self.pair, got).astype(BF)
        return self.whole

    def result(self, got):
        even = self.odd == 0
        low = jnp.where(even, self.whole, got)
        return jnp.concatenate([low, jnp.where(even, got, self.whole)]).astype(F32)


def line_sum(*terms):
    parts = LineSum(*terms)
    got = neighbour(parts.first(), 1)
    got = neighbour(parts.second(got), 2)
    return parts.result(neighbour(parts.third(got), 1))


def per_device(
    tokens,
    segment_ids,
    cotangent,
    query_weight,
    query_bias,
    key_weight,
    value_weight,
    value_bias,
    out_weight,
    out_bias,
    attn_gain,
    attn_shift,
    up_weight,
    up_bias,
    down_weight,
    down_bias,
    mlp_gain,
    mlp_shift,
):
    owners = lax.axis_size("fsdp")
    plane = owners == SHARDS
    z = lax.axis_index("ctx")
    f = lax.axis_index("fsdp")
    if plane:
        chip, core = f // 2, f % 2
    else:
        chip, core = jnp.int32(0), jnp.int32(0)
    scalars = jnp.stack([z, chip, core, z]).astype(jnp.int32)
    tok = tokens[0]
    if plane:
        weights = (query_weight, key_weight, value_weight, out_weight)
        vectors = (query_bias, value_bias, out_bias, attn_gain, attn_shift, down_bias)
        vectors += (mlp_gain, mlp_shift, up_bias)
        packed, mine_pack = pack_inputs(scalars, tok, segment_ids, weights, vectors)
        pack = lax.all_gather(mine_pack, "fsdp", axis=0)
        xs = line_gather(packed)
        xs.append(line_forward(xs[3]))
        near_x, near_y = swap(up_weight, 2), swap(up_weight, 4)
        xs, near_x, near_y, after, pack = lax.optimization_barrier(
            (xs, near_x, near_y, down_weight, pack)
        )
        down = lax.all_gather(after, "fsdp", axis=0)
        half = up_weight.shape[1] // 2
        far = [swap(near_x[:, :half], 4), swap(near_y[:, half:], 2)]
    else:
        seg_row = jnp.pad(segment_ids.astype(BF), ((0, 15), (0, 1024 - CHUNK)))
        packed = jnp.concatenate([tok, seg_row])
        xs = line_gather(packed)
        xs.append(line_forward(xs[3]))
        quarter = jnp.concatenate(
            [
                lax.dynamic_slice_in_dim(m, z * WIDE, WIDE, 1)
                for m in (query_weight, key_weight, value_weight)
            ],
            axis=1,
        )
        whole = lambda m: lax.all_gather(m, "fsdp", axis=0, tiled=True)
        split = lambda m: whole(m).reshape(SHARDS, -1)
        line0 = jnp.concatenate(
            [split(m) for m in (query_bias, value_bias, out_bias, attn_gain, attn_shift, down_bias)],
            axis=1,
        )
        line1 = jnp.concatenate([split(m) for m in (mlp_gain, mlp_shift, up_bias)], axis=1)
        lines = jnp.pad(jnp.stack([line0, line1], axis=1), ((0, 0), (0, 14), (0, 0)))
        pack = jnp.concatenate([whole(quarter).reshape(SHARDS, ROWS, 768), lines], axis=1)
        out_rows = whole(out_weight).reshape(SHARDS, ROWS, 1024)
        wide = lambda m: jnp.pad(m, ((0, 0), (0, 0), (0, 1024 - m.shape[2])))
        pack = jnp.concatenate([out_rows, wide(pack)], axis=1)
        ups = list(whole(up_weight).reshape(SHARDS, ROWS, 4096))
        down = whole(down_weight).reshape(SHARDS, 512, 1024)
    valid = (segment_ids[0] != SEGS - 1).astype(F32)[:, None]

    m0, m1, m2, m3, mixt, lse, qm, kv, kt, xall, segr = attn_fwd(scalars, xs, pack)
    parts = [m0] + [shift(m, -k) for k, m in ((1, m1), (2, m2), (3, m3))]
    if plane:
        ups = [up_weight, swap(up_weight, 1)]
        parts, near_x, near_y, far = lax.optimization_barrier((parts, near_x, near_y, far))
        for rows in (near_x, near_y, jnp.concatenate(far, axis=1)):
            ups += [rows, swap(rows, 1)]
    normed, low, low_rel, scaled, inv, mixed, stats_a = out_project(
        scalars, tok, parts, pack, valid
    )
    acts, slope = mlp_gate(low, low_rel, mixed, ups, pack)
    acts_p = swap(acts, 1)
    result, grads, gh1, g0, g1, g2, g3, sums_m, stats_m, sums_a, ub = mlp_tail(
        scalars, acts, slope, ups, down, normed, scaled, inv, pack, cotangent[0], valid
    )
    gs = [g0] + [shift(g, k) for k, g in ((1, g1), (2, g2), (3, g3))]
    grads_p = swap(grads, 1)
    d3, d1, d2, d0 = down_grads(scalars, acts, acts_p, grads, grads_p)
    if plane:
        d_far = swap(d3, 2)
    r3, r1, r2, r0 = rest_grads(scalars, acts, acts_p, grads, grads_p)
    gs, r3, r1, r2, r0 = lax.optimization_barrier((gs, r3, r1, r2, r0))
    if plane:
        r_far = swap(r3, 4)
    smalls = (sums_m, sums_a, ub.reshape(1024, 4).T, stats_a, stats_m)
    ig, gw = attn_bwd(scalars, xall, segr, pack, qm, kv, kt, mixt, lse, gs, smalls)
    tie = lax.optimization_barrier
    if plane:
        ig, gw, d_far, r_far = tie((ig, gw, d_far, r_far))
    ig = lax.psum_scatter(ig, "ctx", scatter_dimension=0, tiled=True)
    if plane:
        to_y, to_x = add(d2, d_far).astype(BF), add(r1, r_far).astype(BF)
        to_y, to_x, d1, r2 = tie((to_y, to_x, d1, r2))
        r_from_x, r_from_y = swap(to_x, 2), swap(r2, 4)
        d_from_x, d_from_y = swap(d1, 2), swap(to_y, 4)
        r_sum = LineSum(r0, r_from_x, r_from_y)
        got_r = neighbour(r_sum.first(), 1)
        ig, gw, _ = tie((ig, gw, got_r))
    q_own = lax.psum_scatter(gw, "fsdp", scatter_dimension=0, tiled=True)
    q_low = q_own.astype(BF)

    if plane:
        r_second = r_sum.second(got_r)
        got_r = neighbour(r_second, 2)
        d_from_x, d_from_y, _ = tie((d_from_x, d_from_y, r_second))
        d_sum = LineSum(d0, d_from_x, d_from_y)
        got = neighbour(d_sum.first(), 1)
        r_third = r_sum.third(got_r)
        got_r = neighbour(r_third, 1)
        got, _ = tie((got, r_third))
        d_second = d_sum.second(got)
        got = neighbour(d_second, 2)
        q_low, _ = tie((q_low, d_second))
        q_pieces = [q_low] + [shift(q_low, k) for k in (1, 2, 3)]
        rest = r_sum.result(got_r)
        grad_down = d_sum.result(neighbour(d_sum.third(got), 1))
        input_grad = add(gh1, ig)
        grad_up = jnp.concatenate([rest[ROWS * b : ROWS * b + ROWS] for b in range(4)], axis=1)
        grad_out = rest[4 * ROWS :]
    else:
        other = scalars.at[2].set(1)
        sums_w = (d3, d1, d2, d0, r3, r1, r2, r0)
        second = down_grads(other, acts, acts_p, grads, grads_p)
        second += rest_grads(other, acts, acts_p, grads, grads_p)
        rows_of = lambda t: ([t[3], t[1], t[2], t[0]], [t[7], t[5], t[6], t[4]])
        down_0, rest_0 = rows_of(sums_w)
        down_1, rest_1 = rows_of(second)
        down_all = 0.5 * jnp.stack([m.astype(F32) for p in zip(down_0, down_1) for m in p])
        rest_all = 0.5 * jnp.stack([m.astype(F32) for p in zip(rest_0, rest_1) for m in p])
        scatter = lambda m: lax.psum_scatter(
            m.astype(BF), "fsdp", scatter_dimension=0, tiled=True
        )
        grad_down = line_sum(scatter(down_all.reshape(4096, 1024)))
        grad_up = line_sum(
            scatter(
                rest_all[:, 0:512]
                .reshape(SHARDS, 4, ROWS, 1024)
                .swapaxes(1, 2)
                .reshape(1024, 4096)
            )
        )
        grad_out = line_sum(scatter(rest_all[:, 512:].reshape(1024, 1024)))
        q_pieces = [q_low] + [shift(q_low, k) for k in (1, 2, 3)]
        input_grad = add(gh1, ig)
    if plane:
        done = finish(scalars, q_pieces)
        grad_q, grad_k, grad_v = done[0:3]
        vectors = [v.reshape(-1) for v in done[3:11]]
        up_bias_grad = done[11].T.reshape(-1)
        rms = [v.reshape(()) for v in done[12:15]]
    else:
        table = jnp.take(jnp.stack(q_pieces), (z - jnp.arange(4)) % 4, axis=0)
        extra = add(*q_pieces)[:, 3 * WIDE :]
        cols = lambda n: jnp.concatenate(
            [table[a, :, n * WIDE : (n + 1) * WIDE].astype(F32) for a in range(4)], axis=1
        )
        grad_q, grad_k, grad_v = cols(0), cols(1), cols(2)
        vectors = [extra[:, n] for n in range(8)]
        up_bias_grad = extra[:, 8:12].reshape(-1)
        counted = (16.0 * extra[0, 15] + extra[0, 16]) * 1024
        rms = [jnp.sqrt(extra[0, 12 + n] / counted) for n in range(3)]
    return (
        result[None],
        input_grad[None],
        grad_q,
        vectors[6],
        grad_k,
        grad_v,
        vectors[7],
        grad_out,
        vectors[5],
        vectors[3],
        vectors[4],
        grad_up,
        up_bias_grad,
        grad_down,
        vectors[2],
        vectors[0],
        vectors[1],
        rms[0],
        rms[1],
        rms[2],
    )


def solution(mesh):
    matrix, vector = P("fsdp", None), P("fsdp")
    stream = P("fsdp", "ctx", None)
    placed = (
        stream,
        P("fsdp", "ctx"),
        stream,
        matrix,
        vector,
        matrix,
        matrix,
        vector,
        matrix,
        vector,
        vector,
        vector,
        matrix,
        vector,
        matrix,
        vector,
        vector,
        vector,
    )
    return jax.shard_map(
        per_device,
        mesh=mesh,
        in_specs=placed,
        out_specs=(
            stream,
            stream,
            matrix,
            vector,
            matrix,
            matrix,
            vector,
            matrix,
            vector,
            vector,
            vector,
            matrix,
            vector,
            matrix,
            vector,
            vector,
            vector,
            P(),
            P(),
            P(),
        ),
        check_vma=False,
    )
```

```python
from functools import partial

import jax
import jax.numpy as jnp
from jax import lax
from jax.experimental import pallas as pl
from jax.experimental.pallas import tpu as pltpu
from jax.sharding import PartitionSpec as P

HEADS = 16
HEAD_DIM = 64
SEGS = 8
EPSILON = 1e-05
MASKED = -1000000000.0
SCALE = HEAD_DIM ** (-0.5)
BF = jnp.bfloat16
F32 = jnp.float32

CHUNK = 256
HERE = 4
WIDE = HERE * HEAD_DIM
SHARDS = 8
ROWS = 128
PACK = 2 * ROWS + 16
PARAMS = pltpu.CompilerParams(vmem_limit_bytes=60 * 1024 * 1024)


SMEM_SPEC = pl.BlockSpec(memory_space=pltpu.SMEM)
VMEM_SPEC = pl.BlockSpec(memory_space=pltpu.VMEM)


def dot(a, b, dims=((1,), (0,))):
    return lax.dot_general(a, b, (dims, ((), ())), preferred_element_type=F32)


def vec(small_ref, row, start, size):
    return jnp.concatenate(
        [small_ref[f, row : row + 1, start : start + size].astype(F32) for f in range(SHARDS)],
        axis=1,
    )


def any_spec(shape):
    return pl.BlockSpec(shape, lambda *a: (0,) * len(shape))


def pack_kernel(sc, tok, seg, wq, wk, wv, wout, qb, vb, ob, ag, sh, db, mg, ms, ub, xp, pk):
    z = sc[0]
    cols = pl.ds(pl.multiple_of(z * WIDE, WIDE), WIDE)
    xp[0:CHUNK] = tok[...]
    xp[CHUNK:] = jnp.zeros((16, 1024), BF)
    xp[CHUNK : CHUNK + 1, 0:CHUNK] = seg[...].astype(F32).astype(BF)
    pk[0:ROWS] = wout[...]
    for n, w in enumerate((wq, wk, wv)):
        pk[ROWS : 2 * ROWS, WIDE * n : WIDE * n + WIDE] = w[:, cols]
    pk[ROWS : 2 * ROWS, 3 * WIDE :] = jnp.zeros((ROWS, 1024 - 3 * WIDE), BF)
    pk[2 * ROWS :] = jnp.zeros((16, 1024), BF)
    at = slice(2 * ROWS, 2 * ROWS + 1)
    for n, vector in enumerate((qb, vb, ob, ag, sh, db)):
        pk[at, 128 * n : 128 * n + 128] = vector[...]
    at = slice(2 * ROWS + 1, 2 * ROWS + 2)
    for n, vector in enumerate((mg, ms)):
        pk[at, 128 * n : 128 * n + 128] = vector[...]
    for n in range(4):
        pk[at, 256 + 128 * n : 384 + 128 * n] = ub[n : n + 1, :]


def pack_inputs(scalars, tok, seg, weights, vectors):
    shape = jax.ShapeDtypeStruct
    return pl.pallas_call(
        pack_kernel,
        name="pack_inputs",
        in_specs=[SMEM_SPEC] + [VMEM_SPEC] * 15,
        out_specs=(VMEM_SPEC,) * 2,
        out_shape=(shape((CHUNK + 16, 1024), BF), shape((PACK, 1024), BF)),
        compiler_params=PARAMS,
    )(scalars, tok, seg, *weights, *[v.reshape(-1, 128) for v in vectors])


def segment_setup(rows, segc, ends):
    for a in range(4):
        row = rows[a][0:1, :]
        segc[a] = jnp.transpose(jnp.broadcast_to(row, (128, CHUNK)))
        ends[0, a] = jnp.min(row).astype(jnp.int32)
        ends[1, a] = jnp.max(row).astype(jnp.int32)


def key_range(ends, i):
    low = jnp.int32(0)
    high = jnp.int32(4)
    for j in range(4):
        low = low + (ends[1, j] < ends[0, i]).astype(jnp.int32)
        high = high - (ends[0, j] > ends[1, i]).astype(jnp.int32)
    return low, high


def one_head(x, h):
    pair = x[:, 128 * (h // 2) : 128 * (h // 2) + 128]
    lane = lax.broadcasted_iota(jnp.int32, pair.shape, 1)
    return jnp.where((lane < HEAD_DIM) == (h % 2 == 0), pair, jnp.zeros_like(pair))


def attn_fwd_kernel(
    sc,
    x0,
    right,
    left,
    x2,
    far,
    w,
    small,
    m0,
    m1,
    m2,
    m3,
    mixt,
    lse,
    qm,
    kv,
    kt,
    xall,
    segr,
    valid,
    vt,
    acc,
    scores,
    probs,
    segc,
    ends,
):
    z = sc[0]

    def place(k, src):
        a = lax.rem(z - k + 4, 4)
        xall[a] = src[0:CHUNK, :]
        segr[a] = jnp.broadcast_to(
            src[CHUNK : CHUNK + 16, 0:CHUNK].astype(F32)[0:1, :], (8, CHUNK)
        )

    place(0, x0)
    place(2, x2)
    for k, usual, end in ((1, right, 0), (3, left, 3)):
        pl.when(z == end)(partial(place, k, far))
        pl.when(z != end)(partial(place, k, usual))
    segment_setup(segr, segc, ends)
    valid[...] = (segc[z] != SEGS - 1).astype(F32)
    weight = w[...].reshape(SHARDS * ROWS, 3 * WIDE)
    first = small[2 * z].astype(F32)
    second = small[2 * z + 1].astype(F32)
    qb = jnp.concatenate([first[0:1, 0:128], second[0:1, 0:128]], axis=1)
    vb = jnp.concatenate([first[0:1, 128:256], second[0:1, 128:256]], axis=1)
    for n in range(4):
        at = slice(n * CHUNK, (n + 1) * CHUNK)
        prod = dot(xall[n], weight)
        q = ((prod[:, 0:WIDE] + qb).astype(BF).astype(F32) * SCALE).astype(BF)
        kk = prod[:, WIDE : 2 * WIDE].astype(BF)
        v = (prod[:, 2 * WIDE :] + vb).astype(BF)
        for h in range(HERE):
            qm[h, at, :] = one_head(q, h)
        kv[at, 0:WIDE] = kk
        kv[at, WIDE:] = v
        kt[:, at] = jnp.transpose(kk)
        vt[:, at] = jnp.transpose(v)

    def q_chunk(i, carry):
        rows = pl.ds(pl.multiple_of(i * CHUNK, CHUNK), CHUNK)
        low, high = key_range(ends, i)
        row = segr[i][0:1, :]

        acc[...] = jnp.zeros_like(acc)

        def key_chunk(j, state):
            keys = pl.ds(pl.multiple_of(j * CHUNK, CHUNK), CHUNK)
            col = segc[j]
            mask = jnp.concatenate([col, col], axis=1) == row
            new, fixes = [], []
            for h in range(HERE):
                pair = slice(128 * (h // 2), 128 * (h // 2) + 128)
                s = dot(kv[keys, pair], qm[h, rows, :], ((1,), (1,)))
                s = jnp.where(mask, s, MASKED)
                scores[h] = s
                new.append(jnp.maximum(state[h][0], jnp.max(s, axis=0, keepdims=True)))
            out = []
            for h in range(HERE):
                m, l = state[h]
                total = jnp.zeros((1, CHUNK), F32)
                for t in range(4):
                    tile = slice(64 * t, 64 * t + 64)
                    p = jnp.exp(scores[h, tile, :] - new[h])
                    total = total + jnp.sum(p, axis=0, keepdims=True)
                    probs[h, tile, :] = p.astype(BF)
                fixes.append(jnp.exp(m - new[h]))
                out.append((new[h], l * fixes[h] + total))
            for h in range(HERE):
                head = slice(h * HEAD_DIM, (h + 1) * HEAD_DIM)
                acc[head, :] = acc[head, :] * fixes[h] + dot(vt[head, keys], probs[h])
            return tuple(out)

        init = tuple(
            (jnp.full((1, CHUNK), MASKED, F32), jnp.zeros((1, CHUNK), F32)) for _ in range(HERE)
        )
        state = lax.fori_loop(low, high, key_chunk, init)
        for h in range(HERE):
            m, l = state[h]
            head = slice(h * HEAD_DIM, (h + 1) * HEAD_DIM)
            mixt[head, rows] = acc[head, :] / l
            lse[h : h + 1, rows] = m + jnp.log(l)
        return carry

    lax.fori_loop(0, 4, q_chunk, 0)
    for k, out in enumerate((m0, m1, m2, m3)):
        a = pl.multiple_of(lax.rem(z - k + 4, 4) * CHUNK, CHUNK)
        out[...] = jnp.transpose(mixt[:, pl.ds(a, CHUNK)].astype(BF))


OUT_SPEC = pl.BlockSpec((SHARDS, ROWS, 1024), lambda *a: (0, 0, 0))
QKV_SPEC = pl.BlockSpec((SHARDS, ROWS, 3 * WIDE), lambda *a: (0, 1, 0))
SMALL_SPEC = pl.BlockSpec((SHARDS, 16, 3 * WIDE), lambda *a: (0, 2 * ROWS // 16, 0))


def attn_fwd(scalars, xs, pack):
    shape = jax.ShapeDtypeStruct
    return pl.pallas_call(
        attn_fwd_kernel,
        name="attn_fwd",
        out_shape=(shape((CHUNK, WIDE), BF),) * 4
        + (
            shape((WIDE, 4 * CHUNK), F32),
            shape((8, 4 * CHUNK), F32),
            shape((HERE, 4 * CHUNK, 128), BF),
            shape((4 * CHUNK, 2 * WIDE), BF),
            shape((WIDE, 4 * CHUNK), BF),
            shape((4, CHUNK, 1024), BF),
            shape((4, 8, CHUNK), F32),
            shape((CHUNK, 128), F32),
        ),
        grid=(1,),
        in_specs=[SMEM_SPEC] + [any_spec((CHUNK + 16, 1024))] * 5 + [QKV_SPEC, SMALL_SPEC],
        out_specs=(any_spec((CHUNK, WIDE)),) * 4
        + (
            any_spec((WIDE, 4 * CHUNK)),
            any_spec((8, 4 * CHUNK)),
            any_spec((HERE, 4 * CHUNK, 128)),
            any_spec((4 * CHUNK, 2 * WIDE)),
            any_spec((WIDE, 4 * CHUNK)),
            any_spec((4, CHUNK, 1024)),
            any_spec((4, 8, CHUNK)),
            any_spec((CHUNK, 128)),
        ),
        scratch_shapes=[
            pltpu.VMEM((WIDE, 4 * CHUNK), BF),
            pltpu.VMEM((WIDE, CHUNK), F32),
            pltpu.VMEM((HERE, CHUNK, CHUNK), F32),
            pltpu.VMEM((HERE, CHUNK, CHUNK), BF),
            pltpu.VMEM((4, CHUNK, 128), F32),
            pltpu.SMEM((2, 4), jnp.int32),
        ],
        compiler_params=PARAMS,
    )(scalars, *xs, pack, pack)


def normalise(h):
    centre = h - jnp.mean(h, axis=-1, keepdims=True)
    inverse = lax.rsqrt(jnp.mean(centre * centre, axis=-1, keepdims=True) + EPSILON)
    return centre * inverse, inverse


def norm_pullback(upstream, scaled, inverse, gain):
    e = upstream * gain
    return inverse * (
        e
        - jnp.mean(e, axis=-1, keepdims=True)
        - scaled * jnp.mean(e * scaled, axis=-1, keepdims=True)
    )


def relative(f, sc):
    return 2 * jnp.bitwise_xor(sc[1], f // 2) + jnp.bitwise_xor(sc[2], f % 2)


TILE = 16


def eight(x):
    return jnp.sum(x.reshape(TILE // 8, 8, x.shape[1]), axis=0)


def out_kernel(
    sc, tok, r0, r1, r2, r3, w, small, valid, normed, low, low_rel, scaled, inv, mixed, stats, acc
):
    z = sc[0]
    for k, r in enumerate((r0, r1, r2, r3)):
        a = lax.rem(z + k, 4)
        mixed[:, pl.ds(pl.multiple_of(a * WIDE, WIDE), WIDE)] = r[...]
    acc[...] = dot(mixed[...], w[...].reshape(1024, 1024))
    bias, gain, shift_by = vec(small, 0, 256, 128), vec(small, 0, 384, 128), vec(small, 0, 512, 128)

    def tile(t, carry):
        rows = pl.ds(pl.multiple_of(t * TILE, TILE), TILE)
        branch = acc[rows, :] + bias
        x = tok[rows, :].astype(F32)
        n, inverse = normalise(x + branch)
        y = n * gain + shift_by
        normed[rows, :] = y
        low[rows, :] = y.astype(BF)
        scaled[rows, :] = n
        inv[rows, :] = jnp.broadcast_to(inverse, (TILE, 128))
        ok = valid[rows, 0:1]
        return carry[0] + eight(ok * x * x), carry[1] + eight(ok * branch * branch)

    zero = jnp.zeros((8, 1024), F32)
    stream, branch = lax.fori_loop(0, CHUNK // TILE, tile, (zero, zero), unroll=4)
    for f in range(SHARDS):
        at = pl.multiple_of(relative(f, sc) * ROWS, ROWS)
        low_rel[:, pl.ds(at, ROWS)] = low[:, ROWS * f : ROWS * f + ROWS]
    lane = lax.broadcasted_iota(jnp.int32, (8, 128), 1)
    stats[...] = jnp.where(
        lane == 0,
        jnp.sum(stream),
        jnp.where(
            lane == 1, jnp.sum(branch), jnp.where(lane == 3, jnp.sum(valid[:, 0:1]), 0.0)
        ),
    )


def out_project(scalars, tok, parts, pack, valid):
    shape = jax.ShapeDtypeStruct
    full = lambda *s: any_spec(s)
    return pl.pallas_call(
        out_kernel,
        name="out_project",
        grid=(1,),
        out_shape=(
            shape((CHUNK, 1024), F32),
            shape((CHUNK, 1024), BF),
            shape((CHUNK, 1024), BF),
            shape((CHUNK, 1024), F32),
            shape((CHUNK, 128), F32),
            shape((CHUNK, 1024), BF),
            shape((8, 128), F32),
        ),
        in_specs=[SMEM_SPEC, full(CHUNK, 1024)]
        + [full(CHUNK, WIDE)] * 4
        + [OUT_SPEC, SMALL_SPEC, full(CHUNK, 128)],
        out_specs=(
            full(CHUNK, 1024),
            full(CHUNK, 1024),
            full(CHUNK, 1024),
            full(CHUNK, 1024),
            full(CHUNK, 128),
            full(CHUNK, 1024),
            full(8, 128),
        ),
        scratch_shapes=[pltpu.VMEM((CHUNK, 1024), F32)],
        compiler_params=PARAMS,
    )(scalars, tok, *parts, pack, pack, valid)


UP_SPECS = [pl.BlockSpec((ROWS, 1024), lambda j: (0, j))] * SHARDS


def gate_kernel(low, low_rel, mixed, *refs):
    ups = refs[0:SHARDS]
    small, acts, slope, pre = refs[SHARDS:]
    j = pl.program_id(0)
    pre[...] = dot(low_rel[...], jnp.concatenate([u[...] for u in ups]))
    bias = jnp.concatenate(
        [small[2 * j + n, 1:2, 256:768].astype(F32) for n in range(2)], axis=1
    )
    for t in range(CHUNK // TILE):
        rows = slice(TILE * t, TILE * t + TILE)
        for n in range(2):
            cols = slice(512 * n, 512 * n + 512)
            gate = pre[rows, cols] + bias[:, cols]
            cdf = 0.5 * (1.0 + lax.erf(gate * (2.0 ** -0.5)))
            acts[j, rows, cols] = (gate * cdf).astype(BF)
            slope[rows, cols] = cdf + gate * (jnp.exp(-0.5 * gate * gate) * 0.3989422804014327)

    @pl.when(j == 0)
    def _():
        acts[4] = low[...]
        acts[5] = mixed[...]


def mlp_gate(low, low_rel, mixed, ups, pack):
    shape = jax.ShapeDtypeStruct
    full = lambda *s: any_spec(s)
    return pl.pallas_call(
        gate_kernel,
        name="mlp_gate",
        grid=(4,),
        out_shape=(shape((6, CHUNK, 1024), BF), shape((CHUNK, 4096), F32)),
        in_specs=[full(CHUNK, 1024)] * 3 + UP_SPECS + [SMALL_SPEC],
        out_specs=(full(6, CHUNK, 1024), pl.BlockSpec((CHUNK, 1024), lambda j: (0, j))),
        scratch_shapes=[pltpu.VMEM((CHUNK, 1024), F32)],
        compiler_params=PARAMS,
    )(low, low_rel, mixed, *ups, pack)


def mlp_tail_kernel(sc, acts, down_cols, down_rows, slope, small, valid, inv, *refs):
    far = refs[0 : SHARDS + 4]
    (
        out,
        grads,
        gh1,
        g0,
        g1,
        g2,
        g3,
        sums_m,
        stats,
        sums_a,
        ub,
        acc,
        gh2,
        gm,
        gg_all,
        pre,
        total,
        held,
        normed,
        cot,
        scaled,
        wout,
        sems,
    ) = refs[SHARDS + 4 :]
    s = pl.program_id(0)
    z = sc[0]
    targets = [normed, cot, scaled, wout] + [held.at[n] for n in range(SHARDS)]
    sources = [far[0], far[1], far[2], far[3].at[:, 0:ROWS, :]] + list(far[4:])
    copies = [
        pltpu.make_async_copy(src, dst, sems.at[n])
        for n, (src, dst) in enumerate(zip(sources, targets))
    ]
    zero = jnp.zeros((8, 1024), F32)

    def tiles(body, count):
        totals = lax.fori_loop(0, CHUNK // TILE, body, (zero,) * count, unroll=4)
        return [jnp.sum(t, axis=0, keepdims=True) for t in totals]

    @pl.when(s == 0)
    def _():
        for copy in copies:
            copy.start()

    @pl.when(s < 2)
    def _():
        hidden = jnp.concatenate([acts[b] for b in range(4)], axis=1)
        for n in range(2):
            cols = pl.ds(pl.multiple_of(jnp.minimum(s, 1) * 512 + 256 * n, 256), 256)
            part = down_cols[:, :, 256 * n : 256 * n + 256].reshape(4096, 256)
            acc[:, cols] = dot(hidden, part)

    @pl.when(s == 1)
    def _():
        for copy in copies[0:2]:
            copy.wait()
        bias, gain, shift_by = vec(small, 0, 640, 128), vec(small, 1, 0, 128), vec(small, 1, 128, 128)

        def tile(t, carry):
            rows = pl.ds(pl.multiple_of(t * TILE, TILE), TILE)
            branch = acc[rows, :] + bias
            unit, inverse = normalise(normed[rows, :] + branch)
            out[rows, :] = (unit * gain + shift_by).astype(BF)
            ok = valid[rows, 0:1]
            u = cot[rows, :].astype(F32) * ok
            g = norm_pullback(u, unit, inverse, gain)
            gh2[rows, :] = g
            g_low = g.astype(BF)
            gm[rows, :] = g_low
            terms = (u * unit, u, g_low.astype(F32), ok * branch * branch)
            return tuple(c + eight(v) for c, v in zip(carry, terms))

        totals = tiles(tile, 4)
        sums_m[...] = jnp.zeros_like(sums_m)
        for at in range(3):
            sums_m[at : at + 1, :] = totals[at]
        lane = lax.broadcasted_iota(jnp.int32, (8, 128), 1)
        stats[...] = jnp.where(lane == 2, jnp.sum(totals[3]), 0.0)

    @pl.when((s >= 2) & (s < 6))
    def _():
        j = jnp.clip(s - 2, 0, 3)
        pre[...] = dot(gm[...], down_rows[...].reshape(1024, 1024), ((1,), (1,)))
        for n in range(2):
            cols = slice(512 * n, 512 * n + 512)
            total_ub = jnp.zeros((8, 512), F32)
            for t in range(CHUNK // TILE):
                rows = slice(TILE * t, TILE * t + TILE)
                gg = (pre[rows, cols] * slope[rows, cols]).astype(BF)
                gg_all[j, rows, cols] = gg
                grads[0, rows, cols] = gg
                total_ub = total_ub + eight(gg.astype(F32))
            row = jnp.sum(total_ub, axis=0, keepdims=True)
            for q in range(4):
                to = pl.ds(pl.multiple_of((2 * j + n) * 128, 128), 128)
                ub[q : q + 1, to] = row[:, 128 * q : 128 * q + 128]

    @pl.when(s == 6)
    def _():
        grads[0] = gm[...]
        for copy in copies[2:]:
            copy.wait()

    @pl.when(s >= 6)
    def _():
        gg = jnp.concatenate([gg_all[b] for b in range(4)], axis=1)
        for m in range(2):
            j = jnp.clip(2 * (s - 6) + m, 0, 3)
            rows = held[pl.ds(2 * j, 2)].reshape(2 * ROWS, 4096)
            part = dot(gg, rows, ((1,), (1,)))
            pair = jnp.bitwise_xor(sc[1], j)
            for t in range(2):
                f = 2 * pair + jnp.bitwise_xor(sc[2], t)
                to = pl.ds(pl.multiple_of(f * ROWS, ROWS), ROWS)
                total[:, to] = part[:, ROWS * t : ROWS * t + ROWS]

    @pl.when(s == 7)
    def _():
        gain = vec(small, 0, 384, 128)

        def tile(t, carry):
            rows = pl.ds(pl.multiple_of(t * TILE, TILE), TILE)
            u = gh2[rows, :] + total[rows, :]
            n = scaled[rows, :]
            g = norm_pullback(u, n, inv[rows, 0:1], gain)
            gh1[rows, :] = g
            g_low = g.astype(BF)
            grads[0, rows, :] = g_low
            terms = (u * n, u, g_low.astype(F32))
            return tuple(c + eight(v) for c, v in zip(carry, terms))

        totals = tiles(tile, 3)
        sums_a[...] = jnp.zeros_like(sums_a)
        for at in range(3):
            sums_a[at : at + 1, :] = totals[at]
        g_low = grads[0]
        for k, g_out in enumerate((g0, g1, g2, g3)):
            a = lax.rem(z + k, 4)
            rows = wout[pl.ds(2 * a, 2)].reshape(WIDE, 1024)
            g_out[...] = dot(g_low, rows, ((1,), (1,))).astype(BF)


def mlp_tail(scalars, acts, slope, ups, down, normed, scaled, inv, pack, cot, valid):
    shape = jax.ShapeDtypeStruct
    full = lambda *s: any_spec(s)
    block = lambda s: jnp.clip(s - 2, 0, 3)

    def grads_at(s):
        return (jnp.where(s < 6, block(s), jnp.where(s < 7, 5, 4)), 0, 0)

    return pl.pallas_call(
        mlp_tail_kernel,
        name="mlp_tail",
        grid=(8,),
        in_specs=[
            SMEM_SPEC,
            full(4, CHUNK, 1024),
            pl.BlockSpec((SHARDS, 512, 512), lambda s: (0, 0, jnp.minimum(s, 1))),
            pl.BlockSpec((2, 512, 1024), lambda s: (block(s), 0, 0)),
            pl.BlockSpec((CHUNK, 1024), lambda s: (0, block(s))),
            SMALL_SPEC,
            full(CHUNK, 128),
            full(CHUNK, 128),
        ]
        + [pl.BlockSpec(memory_space=pl.ANY)] * (SHARDS + 4),
        out_specs=(
            full(CHUNK, 1024),
            pl.BlockSpec((1, CHUNK, 1024), grads_at),
            full(CHUNK, 1024),
        )
        + (full(CHUNK, WIDE),) * 4
        + (full(8, 1024), full(8, 128), full(8, 1024), full(4, 1024)),
        out_shape=(
            shape((CHUNK, 1024), BF),
            shape((6, CHUNK, 1024), BF),
            shape((CHUNK, 1024), F32),
        )
        + (shape((CHUNK, WIDE), BF),) * 4
        + (
            shape((8, 1024), F32),
            shape((8, 128), F32),
            shape((8, 1024), F32),
            shape((4, 1024), F32),
        ),
        scratch_shapes=[
            pltpu.VMEM((CHUNK, 1024), F32),
            pltpu.VMEM((CHUNK, 1024), F32),
            pltpu.VMEM((CHUNK, 1024), BF),
            pltpu.VMEM((4, CHUNK, 1024), BF),
            pltpu.VMEM((CHUNK, 1024), F32),
            pltpu.VMEM((CHUNK, 1024), F32),
            pltpu.VMEM((SHARDS, ROWS, 4096), BF),
            pltpu.VMEM((CHUNK, 1024), F32),
            pltpu.VMEM((CHUNK, 1024), BF),
            pltpu.VMEM((CHUNK, 1024), F32),
            pltpu.VMEM((SHARDS, ROWS, 1024), BF),
            pltpu.SemaphoreType.DMA((SHARDS + 4,)),
        ],
        compiler_params=PARAMS,
    )(scalars, acts, down, down, slope, pack, valid, inv, normed, cot, scaled, pack, *ups)


REST = 640


def step_shard(j, sc):
    rel = jnp.where(j == 0, 3, jnp.where(j >= 3, 0, j))
    return 2 * jnp.bitwise_xor(sc[1], rel) + sc[2]


def product(left, right, res):
    for n in range(4):
        cols = slice(256 * n, 256 * n + 256)
        res[:, cols] = dot(left[...], right[:, cols]).astype(BF)


def down_kernel(sc, ho, hp, go, gp, d3, d1, d2, d0, left, right, res):
    s = pl.program_id(0)

    @pl.when(s == 0)
    def _():
        right[0:CHUNK] = go[0]
        right[CHUNK:] = gp[0]

    left[:, 0:CHUNK] = jnp.transpose(ho[0])
    left[:, CHUNK:] = jnp.transpose(hp[0])
    product(left, right, res)
    for n, out in enumerate((d3, d1, d2, d0)):

        @pl.when(s == n)
        def _():
            out[...] = res[...]


def down_grads(scalars, acts, acts_p, grads, grads_p):
    shape = jax.ShapeDtypeStruct
    full = lambda *s: pl.BlockSpec(s, lambda j, sc: (0,) * len(s))

    def hid(j, sc):
        f = step_shard(j, sc)
        return (f // 2, 0, f % 2)

    hidden = pl.BlockSpec((1, CHUNK, 512), hid)
    grad = pl.BlockSpec((1, CHUNK, 1024), lambda j, sc: (5, 0, 0))
    return pl.pallas_call(
        down_kernel,
        name="down_grads",
        grid_spec=pltpu.PrefetchScalarGridSpec(
            num_scalar_prefetch=1,
            grid=(4,),
            in_specs=[hidden, hidden, grad, grad],
            out_specs=(full(512, 1024),) * 4,
            scratch_shapes=[
                pltpu.VMEM((512, 2 * CHUNK), BF),
                pltpu.VMEM((2 * CHUNK, 1024), BF),
                pltpu.VMEM((512, 1024), BF),
            ],
        ),
        out_shape=(shape((512, 1024), BF),) * 4,
        compiler_params=PARAMS,
    )(scalars, acts, acts_p, grads, grads_p)


def rest_kernel(sc, lo, lp, go, gp, r3, r1, r2, r0, low_sel, mix_sel, right, res):
    s = pl.program_id(0)
    chip, core = sc[1], sc[2]

    @pl.when(s == 0)
    def _():
        for r in range(4):
            at = pl.multiple_of((2 * jnp.bitwise_xor(chip, r) + core) * ROWS, ROWS)
            to = slice(ROWS * r, ROWS * r + ROWS)
            for n, out in enumerate((low_sel, mix_sel)):
                out[to, 0:CHUNK] = jnp.transpose(lo[n, :, pl.ds(at, ROWS)])
                out[to, CHUNK:] = jnp.transpose(lp[n, :, pl.ds(at, ROWS)])

    @pl.when(s == 4)
    def _():
        low_sel[...] = mix_sel[...]

    right[0:CHUNK] = go[0]
    right[CHUNK:] = gp[0]
    product(low_sel, right, res)
    for r, out in enumerate((r0, r1, r2, r3)):
        out[...] = res[ROWS * r : ROWS * r + ROWS, :]


def rest_grads(scalars, acts, acts_p, grads, grads_p):
    shape = jax.ShapeDtypeStruct
    full = lambda *s: pl.BlockSpec(s, lambda j, sc: (0,) * len(s))
    flat = pl.BlockSpec((pl.Element(2), pl.Element(CHUNK), pl.Element(1024)), lambda j, sc: (4, 0, 0))
    grad = pl.BlockSpec((1, CHUNK, 1024), lambda j, sc: (j, 0, 0))
    return pl.pallas_call(
        rest_kernel,
        name="rest_grads",
        grid_spec=pltpu.PrefetchScalarGridSpec(
            num_scalar_prefetch=1,
            grid=(5,),
            in_specs=[flat, flat, grad, grad],
            out_specs=(pl.BlockSpec((ROWS, 1024), lambda j, sc: (j, 0)),) * 4,
            scratch_shapes=[
                pltpu.VMEM((512, 2 * CHUNK), BF),
                pltpu.VMEM((512, 2 * CHUNK), BF),
                pltpu.VMEM((2 * CHUNK, 1024), BF),
                pltpu.VMEM((512, 1024), BF),
            ],
        ),
        out_shape=(shape((REST, 1024), BF),) * 4,
        compiler_params=PARAMS,
    )(scalars, acts, acts_p, grads, grads_p)


def attn_bwd_kernel(
    sc,
    segr,
    w,
    qm,
    kv,
    kt,
    mixt,
    lse,
    g0,
    g1,
    g2,
    g3,
    ig,
    dall,
    segc,
    ends,
    gs,
    dq,
    dqt,
    dk,
    dv,
    delta,
    scores,
    slopes,
    probs,
    pulls,
):
    z = sc[0]
    segment_setup(segr, segc, ends)
    dk[...] = jnp.zeros_like(dk)
    dv[...] = jnp.zeros_like(dv)
    for k, g in enumerate((g0, g1, g2, g3)):
        rows = pl.ds(pl.multiple_of(lax.rem(z - k + 4, 4) * CHUNK, CHUNK), CHUNK)
        turned = jnp.transpose(g[...])
        for h in range(HERE):
            head = slice(h * HEAD_DIM, (h + 1) * HEAD_DIM)
            gs[h, rows, :] = one_head(g[...], h)
            prod = turned[head, :].astype(F32) * mixt[head, rows]
            delta[h : h + 1, rows] = jnp.sum(prod, axis=0, keepdims=True)

    def q_chunk(i, carry):
        rows = pl.ds(pl.multiple_of(i * CHUNK, CHUNK), CHUNK)
        low, high = key_range(ends, i)
        row = segr[i][0:1, :]
        dqt[...] = jnp.zeros_like(dqt)

        def key_chunk(j, inner):
            keys = pl.ds(pl.multiple_of(j * CHUNK, CHUNK), CHUNK)
            col = segc[j]
            mask = jnp.concatenate([col, col], axis=1) == row
            for h in range(HERE):
                low_lane = 128 * (h // 2)
                pair = slice(low_lane, low_lane + 128)
                scores[h] = dot(kv[keys, pair], qm[h, rows, :], ((1,), (1,)))
                wide = slice(WIDE + low_lane, WIDE + low_lane + 128)
                slopes[h] = dot(kv[keys, wide], gs[h, rows, :], ((1,), (1,)))
            for h in range(HERE):
                log, shift_by = lse[h : h + 1, rows], delta[h : h + 1, rows]
                for t in range(4):
                    tile = slice(64 * t, 64 * t + 64)
                    p = jnp.where(mask[tile, :], jnp.exp(scores[h, tile, :] - log), 0.0)
                    probs[h, tile, :] = p.astype(BF)
                    pulls[h, tile, :] = (p * (slopes[h, tile, :] - shift_by)).astype(BF)
            for h in range(HERE):
                head = slice(h * HEAD_DIM, (h + 1) * HEAD_DIM)
                pair = slice(128 * (h // 2), 128 * (h // 2) + 128)
                dv[keys, pair] += dot(probs[h], gs[h, rows, :])
                dk[keys, pair] += dot(pulls[h], qm[h, rows, :])
                dqt[head, :] += dot(kt[head, keys], pulls[h])
            return inner

        lax.fori_loop(low, high, key_chunk, 0)
        dq[...] = (dqt[...] * SCALE).astype(BF)
        dall[rows, 0:WIDE] = jnp.transpose(dq[...])
        return carry

    lax.fori_loop(0, 4, q_chunk, 0)
    dall[:, WIDE : 2 * WIDE] = dk[...].astype(BF)
    dall[:, 2 * WIDE :] = dv[...].astype(BF)
    weight = w[...].reshape(SHARDS * ROWS, 3 * WIDE)
    for k in range(4):
        rows = slice(CHUNK * k, CHUNK * k + CHUNK)
        ig[rows, :] = dot(dall[rows, :], weight, ((1,), (1,))).astype(BF)


def qkv_kernel(sc, xall, dall, sums_m, sums_a, ubt, stats_a, stats_m, out, small, acc):
    z = sc[0]
    for k in range(4):
        part = dot(xall[k], dall[CHUNK * k : CHUNK * k + CHUNK, :], ((0,), (0,)))
        if k == 0:
            acc[...] = part
        else:
            acc[...] += part
    out[:, 0 : 3 * WIDE] = acc[...].astype(BF)
    here = pl.ds(pl.multiple_of(z * WIDE, WIDE), WIDE)
    small[...] = jnp.zeros_like(small)
    small[0:3, :] = sums_m[0:3, :]
    small[3:6, :] = sums_a[0:3, :]
    small[6:7, here] = jnp.sum(dall[:, 0:WIDE].astype(F32), axis=0, keepdims=True)
    small[7:8, here] = jnp.sum(dall[:, 2 * WIDE :].astype(F32), axis=0, keepdims=True)
    small[8:12, :] = ubt[...]
    every = lambda value: jnp.broadcast_to(value, (1, 1024))
    small[12:13, :] = every(stats_a[0:1, 0:1])
    small[13:14, :] = every(stats_a[0:1, 1:2])
    small[14:15, :] = every(stats_m[0:1, 2:3])
    count = stats_a[0:1, 3:4]
    high = jnp.floor(count * 0.0625)
    small[15:16, :] = every(high)
    small[16:17, :] = every(count - 16.0 * high)
    out[:, 3 * WIDE :] = jnp.transpose(small[...]).astype(BF)


def qkv_grads(scalars, xall, dall, smalls):
    return pl.pallas_call(
        qkv_kernel,
        name="qkv_grads",
        out_shape=jax.ShapeDtypeStruct((1024, 3 * WIDE + 128), BF),
        in_specs=[SMEM_SPEC] + [VMEM_SPEC] * 7,
        out_specs=VMEM_SPEC,
        scratch_shapes=[pltpu.VMEM((128, 1024), F32), pltpu.VMEM((1024, 3 * WIDE), F32)],
        compiler_params=PARAMS,
    )(scalars, xall, dall, *smalls)


def attn_bwd(scalars, segr, pack, qm, kv, kt, mixt, lse, gs):
    shape = jax.ShapeDtypeStruct
    return pl.pallas_call(
        attn_bwd_kernel,
        name="attn_bwd",
        out_shape=(shape((1024, 1024), BF), shape((1024, 3 * WIDE), BF)),
        grid=(1,),
        in_specs=[SMEM_SPEC]
        + [
            any_spec((4, 8, CHUNK)),
            QKV_SPEC,
            any_spec((HERE, 4 * CHUNK, 128)),
            any_spec((4 * CHUNK, 2 * WIDE)),
            any_spec((WIDE, 4 * CHUNK)),
            any_spec((WIDE, 4 * CHUNK)),
            any_spec((8, 4 * CHUNK)),
        ]
        + [any_spec((CHUNK, WIDE))] * 4,
        out_specs=(any_spec((1024, 1024)), any_spec((1024, 3 * WIDE))),
        scratch_shapes=[
            pltpu.VMEM((4, CHUNK, 128), F32),
            pltpu.SMEM((2, 4), jnp.int32),
            pltpu.VMEM((HERE, 4 * CHUNK, 128), BF),
            pltpu.VMEM((WIDE, CHUNK), BF),
            pltpu.VMEM((WIDE, CHUNK), F32),
            pltpu.VMEM((4 * CHUNK, WIDE), F32),
            pltpu.VMEM((4 * CHUNK, WIDE), F32),
            pltpu.VMEM((8, 4 * CHUNK), F32),
            pltpu.VMEM((HERE, CHUNK, CHUNK), F32),
            pltpu.VMEM((HERE, CHUNK, CHUNK), F32),
            pltpu.VMEM((HERE, CHUNK, CHUNK), BF),
            pltpu.VMEM((HERE, CHUNK, CHUNK), BF),
        ],
        compiler_params=PARAMS,
    )(scalars, segr, pack, qm, kv, kt, mixt, lse, *gs)


def finish_kernel(sc, *refs):
    z = sc[0]
    pieces, (gq, gk, gv), vectors, ub, rms = refs[0:4], refs[4:7], refs[7:15], refs[15], refs[16:19]
    for k, piece in enumerate(pieces):
        cols = pl.ds(pl.multiple_of(lax.rem(z - k + 4, 4) * WIDE, WIDE), WIDE)
        for n, out in enumerate((gq, gk, gv)):
            out[:, cols] = piece[:, WIDE * n : WIDE * n + WIDE].astype(F32)
    extra = pieces[0][:, 3 * WIDE :].astype(F32)
    for piece in pieces[1:]:
        extra = extra + piece[:, 3 * WIDE :].astype(F32)
    extra = jnp.transpose(extra)
    for n, out in enumerate(vectors):
        out[...] = extra[n : n + 1, :]
    ub[...] = extra[8:12, :]
    counted = (16.0 * extra[15:16, 0:1] + extra[16:17, 0:1]) * 1024.0
    for n, out in enumerate(rms):
        out[...] = jnp.sqrt(extra[12 + n : 13 + n, 0:1] / counted)


def finish(scalars, pieces):
    shape = jax.ShapeDtypeStruct
    shapes = [(ROWS, 1024)] * 3 + [(1, ROWS)] * 8 + [(4, ROWS)] + [(1, 1)] * 3
    return pl.pallas_call(
        finish_kernel,
        name="finish",
        out_shape=tuple(shape(n, F32) for n in shapes),
        in_specs=[SMEM_SPEC] + [VMEM_SPEC] * 4,
        out_specs=(VMEM_SPEC,) * len(shapes),
        compiler_params=PARAMS,
    )(scalars, *pieces)


def line_gather(x):
    right = lax.ppermute(x, "ctx", [(0, 1), (1, 2), (2, 3)])
    left = lax.ppermute(x, "ctx", [(1, 0), (2, 1), (3, 2)])
    two = lax.ppermute(x, "ctx", [(0, 2), (1, 3), (2, 0), (3, 1)])
    return [x, right, left, two]


def line_forward(two):
    return lax.ppermute(two, "ctx", [(1, 0), (2, 3)])


def shift(x, k):
    n = lax.axis_size("ctx")
    return lax.ppermute(x, "ctx", [(i, (i + k) % n) for i in range(n)])


def swap(x, bits):
    return lax.ppermute(x, "fsdp", [(i, i ^ bits) for i in range(lax.axis_size("fsdp"))])


def add(*terms):
    total = terms[0].astype(F32)
    for term in terms[1:]:
        total = total + term.astype(F32)
    return total


def neighbour(x, bits):
    return lax.ppermute(x, "ctx", [(i, i ^ bits) for i in range(4)])


def half_sum(terms, which):
    half = terms[0].shape[0] // 2
    return add(*[lax.dynamic_slice_in_dim(t, which * half, half, 0) for t in terms])


class LineSum:
    def __init__(self, *terms):
        self.terms = terms
        self.odd = lax.axis_index("ctx") % 2

    def first(self):
        return half_sum(self.terms, 1 - self.odd).astype(BF)

    def second(self, got):
        self.pair = add(half_sum(self.terms, self.odd), got).astype(BF)
        return self.pair

    def third(self, got):
        self.whole = add(self.pair, got).astype(BF)
        return self.whole

    def result(self, got):
        even = self.odd == 0
        low = jnp.where(even, self.whole, got)
        return jnp.concatenate([low, jnp.where(even, got, self.whole)]).astype(F32)


def line_sum(*terms):
    parts = LineSum(*terms)
    got = neighbour(parts.first(), 1)
    got = neighbour(parts.second(got), 2)
    return parts.result(neighbour(parts.third(got), 1))


def per_device(
    tokens,
    segment_ids,
    cotangent,
    query_weight,
    query_bias,
    key_weight,
    value_weight,
    value_bias,
    out_weight,
    out_bias,
    attn_gain,
    attn_shift,
    up_weight,
    up_bias,
    down_weight,
    down_bias,
    mlp_gain,
    mlp_shift,
):
    owners = lax.axis_size("fsdp")
    plane = owners == SHARDS
    z = lax.axis_index("ctx")
    f = lax.axis_index("fsdp")
    if plane:
        chip, core = f // 2, f % 2
    else:
        chip, core = jnp.int32(0), jnp.int32(0)
    scalars = jnp.stack([z, chip, core, z]).astype(jnp.int32)
    tok = tokens[0]
    if plane:
        weights = (query_weight, key_weight, value_weight, out_weight)
        vectors = (query_bias, value_bias, out_bias, attn_gain, attn_shift, down_bias)
        vectors += (mlp_gain, mlp_shift, up_bias)
        packed, mine_pack = pack_inputs(scalars, tok, segment_ids, weights, vectors)
        pack = lax.all_gather(mine_pack, "fsdp", axis=0)
        xs = line_gather(packed)
        xs.append(line_forward(xs[3]))
        near_x, near_y = swap(up_weight, 2), swap(up_weight, 4)
        half = up_weight.shape[1] // 2
        far = [swap(near_x[:, :half], 4), swap(near_y[:, half:], 2)]
        xs, near_x, near_y, after, pack = lax.optimization_barrier(
            (xs, near_x, near_y, down_weight, pack)
        )
        down = lax.all_gather(after, "fsdp", axis=0)
    else:
        seg_row = jnp.pad(segment_ids.astype(BF), ((0, 15), (0, 1024 - CHUNK)))
        packed = jnp.concatenate([tok, seg_row])
        xs = line_gather(packed)
        xs.append(line_forward(xs[3]))
        quarter = jnp.concatenate(
            [
                lax.dynamic_slice_in_dim(m, z * WIDE, WIDE, 1)
                for m in (query_weight, key_weight, value_weight)
            ],
            axis=1,
        )
        whole = lambda m: lax.all_gather(m, "fsdp", axis=0, tiled=True)
        split = lambda m: whole(m).reshape(SHARDS, -1)
        line0 = jnp.concatenate(
            [split(m) for m in (query_bias, value_bias, out_bias, attn_gain, attn_shift, down_bias)],
            axis=1,
        )
        line1 = jnp.concatenate([split(m) for m in (mlp_gain, mlp_shift, up_bias)], axis=1)
        lines = jnp.pad(jnp.stack([line0, line1], axis=1), ((0, 0), (0, 14), (0, 0)))
        pack = jnp.concatenate([whole(quarter).reshape(SHARDS, ROWS, 768), lines], axis=1)
        out_rows = whole(out_weight).reshape(SHARDS, ROWS, 1024)
        wide = lambda m: jnp.pad(m, ((0, 0), (0, 0), (0, 1024 - m.shape[2])))
        pack = jnp.concatenate([out_rows, wide(pack)], axis=1)
        ups = list(whole(up_weight).reshape(SHARDS, ROWS, 4096))
        down = whole(down_weight).reshape(SHARDS, 512, 1024)

    m0, m1, m2, m3, mixt, lse, qm, kv, kt, xall, segr, valid = attn_fwd(scalars, xs, pack)
    parts = [m0] + [shift(m, -k) for k, m in ((1, m1), (2, m2), (3, m3))]
    if plane:
        ups = [up_weight, swap(up_weight, 1)]
        far, _ = lax.optimization_barrier((far, m0))
        far = jnp.concatenate(far, axis=1)
        parts, near_x, near_y, far = lax.optimization_barrier((parts, near_x, near_y, far))
        for rows in (near_x, near_y, far):
            ups += [rows, swap(rows, 1)]
    normed, low, low_rel, scaled, inv, mixed, stats_a = out_project(
        scalars, tok, parts, pack, valid
    )
    acts, slope = mlp_gate(low, low_rel, mixed, ups, pack)
    acts_p = swap(acts, 1)
    result, grads, gh1, g0, g1, g2, g3, sums_m, stats_m, sums_a, ub = mlp_tail(
        scalars, acts, slope, ups, down, normed, scaled, inv, pack, cotangent[0], valid
    )
    gs = [g0] + [shift(g, k) for k, g in ((1, g1), (2, g2), (3, g3))]
    grads_p = swap(grads, 1)
    d3, d1, d2, d0 = down_grads(scalars, acts, acts_p, grads, grads_p)
    if plane:
        d_far = swap(d3, 2)
    r3, r1, r2, r0 = rest_grads(scalars, acts, acts_p, grads, grads_p)
    gs, r3, r1, r2, r0 = lax.optimization_barrier((gs, r3, r1, r2, r0))
    if plane:
        r_far = swap(r3, 4)
    if not plane:
        ub = ub.reshape(4, SHARDS, 128).swapaxes(0, 1).reshape(1024, 4).T
    smalls = (sums_m, sums_a, ub, stats_a, stats_m)
    ig, dall = attn_bwd(scalars, segr, pack, qm, kv, kt, mixt, lse, gs)
    tie = lax.optimization_barrier
    if plane:
        ig, dall, d_far, r_far = tie((ig, dall, d_far, r_far))
    ig = lax.psum_scatter(ig, "ctx", scatter_dimension=0, tiled=True)
    if plane:
        to_x = add(r1, r_far).astype(BF)
        to_x, r2, dall, d_far = tie((to_x, r2, dall, d_far))
        r_from_x, r_from_y = swap(to_x, 2), swap(r2, 4)
    gw = qkv_grads(scalars, xall, dall, smalls)
    if plane:
        to_y = add(d2, d_far).astype(BF)
        r_sum = LineSum(r0, r_from_x, r_from_y)
        r_first, gw, to_y, d1 = tie((r_sum.first(), gw, to_y, d1))
        d_from_x, d_from_y = swap(d1, 2), swap(to_y, 4)
        got_r = neighbour(r_first, 1)
        ig, gw, d_from_x, d_from_y, got_r = tie((ig, gw, d_from_x, d_from_y, got_r))
    q_own = lax.psum_scatter(gw, "fsdp", scatter_dimension=0, tiled=True)
    q_low = q_own.astype(BF)

    if plane:
        d_from_x, d_from_y, got_r = tie((d_from_x, d_from_y, got_r))
        got_r = neighbour(r_sum.second(got_r), 2)
        d_sum = LineSum(d0, d_from_x, d_from_y)
        got = neighbour(d_sum.first(), 1)
        r_third = r_sum.third(got_r)
        got_r = neighbour(r_third, 1)
        got, _ = tie((got, r_third))
        d_second = d_sum.second(got)
        got = neighbour(d_second, 2)
        q_low, _ = tie((q_low, d_second))
        q_pieces = [q_low] + [shift(q_low, k) for k in (1, 2, 3)]
        got, got_r, q_pieces = tie((got, got_r, q_pieces))
        rest = r_sum.result(got_r)
        grad_down = d_sum.result(neighbour(d_sum.third(got), 1))
        input_grad = add(gh1, ig)
        grad_up = jnp.concatenate([rest[ROWS * b : ROWS * b + ROWS] for b in range(4)], axis=1)
        grad_out = rest[4 * ROWS :]
    else:
        other = scalars.at[2].set(1)
        sums_w = (d3, d1, d2, d0, r3, r1, r2, r0)
        second = down_grads(other, acts, acts_p, grads, grads_p)
        second += rest_grads(other, acts, acts_p, grads, grads_p)
        rows_of = lambda t: ([t[3], t[1], t[2], t[0]], [t[7], t[5], t[6], t[4]])
        down_0, rest_0 = rows_of(sums_w)
        down_1, rest_1 = rows_of(second)
        down_all = 0.5 * jnp.stack([m.astype(F32) for p in zip(down_0, down_1) for m in p])
        rest_all = 0.5 * jnp.stack([m.astype(F32) for p in zip(rest_0, rest_1) for m in p])
        scatter = lambda m: lax.psum_scatter(
            m.astype(BF), "fsdp", scatter_dimension=0, tiled=True
        )
        grad_down = line_sum(scatter(down_all.reshape(4096, 1024)))
        grad_up = line_sum(
            scatter(
                rest_all[:, 0:512]
                .reshape(SHARDS, 4, ROWS, 1024)
                .swapaxes(1, 2)
                .reshape(1024, 4096)
            )
        )
        grad_out = line_sum(scatter(rest_all[:, 512:].reshape(1024, 1024)))
        q_pieces = [q_low] + [shift(q_low, k) for k in (1, 2, 3)]
        input_grad = add(gh1, ig)
    if plane:
        done = finish(scalars, q_pieces)
        grad_q, grad_k, grad_v = done[0:3]
        vectors = [v.reshape(-1) for v in done[3:11]]
        up_bias_grad = done[11].reshape(-1)
        rms = [v.reshape(()) for v in done[12:15]]
    else:
        table = jnp.take(jnp.stack(q_pieces), (z - jnp.arange(4)) % 4, axis=0)
        extra = add(*q_pieces)[:, 3 * WIDE :]
        cols = lambda n: jnp.concatenate(
            [table[a, :, n * WIDE : (n + 1) * WIDE].astype(F32) for a in range(4)], axis=1
        )
        grad_q, grad_k, grad_v = cols(0), cols(1), cols(2)
        vectors = [extra[:, n] for n in range(8)]
        up_bias_grad = extra[:, 8:12].reshape(-1)
        counted = (16.0 * extra[0, 15] + extra[0, 16]) * 1024
        rms = [jnp.sqrt(extra[0, 12 + n] / counted) for n in range(3)]
    return (
        result[None],
        input_grad[None],
        grad_q,
        vectors[6],
        grad_k,
        grad_v,
        vectors[7],
        grad_out,
        vectors[5],
        vectors[3],
        vectors[4],
        grad_up,
        up_bias_grad,
        grad_down,
        vectors[2],
        vectors[0],
        vectors[1],
        rms[0],
        rms[1],
        rms[2],
    )


def solution(mesh):
    matrix, vector = P("fsdp", None), P("fsdp")
    stream = P("fsdp", "ctx", None)
    placed = (
        stream,
        P("fsdp", "ctx"),
        stream,
        matrix,
        vector,
        matrix,
        matrix,
        vector,
        matrix,
        vector,
        vector,
        vector,
        matrix,
        vector,
        matrix,
        vector,
        vector,
        vector,
    )
    return jax.shard_map(
        per_device,
        mesh=mesh,
        in_specs=placed,
        out_specs=(
            stream,
            stream,
            matrix,
            vector,
            matrix,
            matrix,
            vector,
            matrix,
            vector,
            vector,
            vector,
            matrix,
            vector,
            matrix,
            vector,
            vector,
            vector,
            P(),
            P(),
            P(),
        ),
        check_vma=False,
    )
```

```python
from functools import partial

import jax
import jax.numpy as jnp
from jax import lax
from jax.experimental import pallas as pl
from jax.experimental.pallas import tpu as pltpu
from jax.sharding import PartitionSpec as P

HEADS = 16
HEAD_DIM = 64
SEGS = 8
EPSILON = 1e-05
MASKED = -1000000000.0
SCALE = HEAD_DIM ** (-0.5)
BF = jnp.bfloat16
F32 = jnp.float32

CHUNK = 256
HERE = 4
WIDE = HERE * HEAD_DIM
SHARDS = 8
ROWS = 128
PACK = 2 * ROWS + 16
PARAMS = pltpu.CompilerParams(vmem_limit_bytes=60 * 1024 * 1024)


SMEM_SPEC = pl.BlockSpec(memory_space=pltpu.SMEM)
VMEM_SPEC = pl.BlockSpec(memory_space=pltpu.VMEM)


def dot(a, b, dims=((1,), (0,))):
    return lax.dot_general(a, b, (dims, ((), ())), preferred_element_type=F32)


def vec(small_ref, row, start, size):
    return jnp.concatenate(
        [small_ref[f, row : row + 1, start : start + size].astype(F32) for f in range(SHARDS)],
        axis=1,
    )


def any_spec(shape):
    return pl.BlockSpec(shape, lambda *a: (0,) * len(shape))


def pack_kernel(sc, tok, seg, wq, wk, wv, wout, qb, vb, ob, ag, sh, db, mg, ms, ub, xp, pk):
    z = sc[0]
    cols = pl.ds(pl.multiple_of(z * WIDE, WIDE), WIDE)
    xp[0:CHUNK] = tok[...]
    xp[CHUNK:] = jnp.zeros((16, 1024), BF)
    xp[CHUNK : CHUNK + 1, 0:CHUNK] = seg[...].astype(F32).astype(BF)
    pk[0:ROWS] = wout[...]
    for n, w in enumerate((wq, wk, wv)):
        pk[ROWS : 2 * ROWS, WIDE * n : WIDE * n + WIDE] = w[:, cols]
    pk[ROWS : 2 * ROWS, 3 * WIDE :] = jnp.zeros((ROWS, 1024 - 3 * WIDE), BF)
    pk[2 * ROWS :] = jnp.zeros((16, 1024), BF)
    at = slice(2 * ROWS, 2 * ROWS + 1)
    for n, vector in enumerate((qb, vb, ob, ag, sh, db)):
        pk[at, 128 * n : 128 * n + 128] = vector[...]
    at = slice(2 * ROWS + 1, 2 * ROWS + 2)
    for n, vector in enumerate((mg, ms)):
        pk[at, 128 * n : 128 * n + 128] = vector[...]
    for n in range(4):
        pk[at, 256 + 128 * n : 384 + 128 * n] = ub[n : n + 1, :]


def pack_inputs(scalars, tok, seg, weights, vectors):
    shape = jax.ShapeDtypeStruct
    return pl.pallas_call(
        pack_kernel,
        name="pack_inputs",
        in_specs=[SMEM_SPEC] + [VMEM_SPEC] * 15,
        out_specs=(VMEM_SPEC,) * 2,
        out_shape=(shape((CHUNK + 16, 1024), BF), shape((PACK, 1024), BF)),
        compiler_params=PARAMS,
    )(scalars, tok, seg, *weights, *[v.reshape(-1, 128) for v in vectors])


def segment_setup(rows, segc, ends):
    for a in range(4):
        row = rows[a][0:1, :]
        segc[a] = jnp.transpose(jnp.broadcast_to(row, (128, CHUNK)))
        ends[0, a] = jnp.min(row).astype(jnp.int32)
        ends[1, a] = jnp.max(row).astype(jnp.int32)


def key_range(ends, i):
    low = jnp.int32(0)
    high = jnp.int32(4)
    for j in range(4):
        low = low + (ends[1, j] < ends[0, i]).astype(jnp.int32)
        high = high - (ends[0, j] > ends[1, i]).astype(jnp.int32)
    return low, high


def one_head(x, h):
    pair = x[:, 128 * (h // 2) : 128 * (h // 2) + 128]
    lane = lax.broadcasted_iota(jnp.int32, pair.shape, 1)
    return jnp.where((lane < HEAD_DIM) == (h % 2 == 0), pair, jnp.zeros_like(pair))


def attn_fwd_kernel(
    sc,
    x0,
    right,
    left,
    x2,
    far,
    w,
    small,
    m0,
    m1,
    m2,
    m3,
    mixt,
    lse,
    qm,
    kv,
    kt,
    xall,
    segr,
    valid,
    vt,
    acc,
    scores,
    probs,
    segc,
    ends,
):
    z = sc[0]

    def place(k, src):
        a = lax.rem(z - k + 4, 4)
        xall[a] = src[0:CHUNK, :]
        segr[a] = jnp.broadcast_to(
            src[CHUNK : CHUNK + 16, 0:CHUNK].astype(F32)[0:1, :], (8, CHUNK)
        )

    place(0, x0)
    place(2, x2)
    for k, usual, end in ((1, right, 0), (3, left, 3)):
        pl.when(z == end)(partial(place, k, far))
        pl.when(z != end)(partial(place, k, usual))
    segment_setup(segr, segc, ends)
    valid[...] = (segc[z] != SEGS - 1).astype(F32)
    weight = w[...].reshape(SHARDS * ROWS, 3 * WIDE)
    first = small[2 * z].astype(F32)
    second = small[2 * z + 1].astype(F32)
    qb = jnp.concatenate([first[0:1, 0:128], second[0:1, 0:128]], axis=1)
    vb = jnp.concatenate([first[0:1, 128:256], second[0:1, 128:256]], axis=1)
    for n in range(4):
        at = slice(n * CHUNK, (n + 1) * CHUNK)
        prod = dot(xall[n], weight)
        q = ((prod[:, 0:WIDE] + qb).astype(BF).astype(F32) * SCALE).astype(BF)
        kk = prod[:, WIDE : 2 * WIDE].astype(BF)
        v = (prod[:, 2 * WIDE :] + vb).astype(BF)
        for h in range(HERE):
            qm[h, at, :] = one_head(q, h)
        kv[at, 0:WIDE] = kk
        kv[at, WIDE:] = v
        kt[:, at] = jnp.transpose(kk)
        vt[:, at] = jnp.transpose(v)

    def q_chunk(i, carry):
        rows = pl.ds(pl.multiple_of(i * CHUNK, CHUNK), CHUNK)
        low, high = key_range(ends, i)
        row = segr[i][0:1, :]

        acc[...] = jnp.zeros_like(acc)

        def key_chunk(j, state):
            keys = pl.ds(pl.multiple_of(j * CHUNK, CHUNK), CHUNK)
            col = segc[j]
            mask = jnp.concatenate([col, col], axis=1) == row
            new, fixes = [], []
            for h in range(HERE):
                pair = slice(128 * (h // 2), 128 * (h // 2) + 128)
                s = dot(kv[keys, pair], qm[h, rows, :], ((1,), (1,)))
                s = jnp.where(mask, s, MASKED)
                scores[h] = s
                new.append(jnp.maximum(state[h][0], jnp.max(s, axis=0, keepdims=True)))
            out = []
            for h in range(HERE):
                m, l = state[h]
                total = jnp.zeros((1, CHUNK), F32)
                for t in range(4):
                    tile = slice(64 * t, 64 * t + 64)
                    p = jnp.exp(scores[h, tile, :] - new[h])
                    total = total + jnp.sum(p, axis=0, keepdims=True)
                    probs[h, tile, :] = p.astype(BF)
                fixes.append(jnp.exp(m - new[h]))
                out.append((new[h], l * fixes[h] + total))
            for h in range(HERE):
                head = slice(h * HEAD_DIM, (h + 1) * HEAD_DIM)
                acc[head, :] = acc[head, :] * fixes[h] + dot(vt[head, keys], probs[h])
            return tuple(out)

        init = tuple(
            (jnp.full((1, CHUNK), MASKED, F32), jnp.zeros((1, CHUNK), F32)) for _ in range(HERE)
        )
        state = lax.fori_loop(low, high, key_chunk, init)
        for h in range(HERE):
            m, l = state[h]
            head = slice(h * HEAD_DIM, (h + 1) * HEAD_DIM)
            mixt[head, rows] = acc[head, :] / l
            lse[h : h + 1, rows] = m + jnp.log(l)
        return carry

    lax.fori_loop(0, 4, q_chunk, 0)
    for k, out in enumerate((m0, m1, m2, m3)):
        a = pl.multiple_of(lax.rem(z - k + 4, 4) * CHUNK, CHUNK)
        out[...] = jnp.transpose(mixt[:, pl.ds(a, CHUNK)].astype(BF))


OUT_SPEC = pl.BlockSpec((SHARDS, ROWS, 1024), lambda *a: (0, 0, 0))
QKV_SPEC = pl.BlockSpec((SHARDS, ROWS, 3 * WIDE), lambda *a: (0, 1, 0))
SMALL_SPEC = pl.BlockSpec((SHARDS, 16, 3 * WIDE), lambda *a: (0, 2 * ROWS // 16, 0))


def attn_fwd(scalars, xs, pack):
    shape = jax.ShapeDtypeStruct
    return pl.pallas_call(
        attn_fwd_kernel,
        name="attn_fwd",
        out_shape=(shape((CHUNK, WIDE), BF),) * 4
        + (
            shape((WIDE, 4 * CHUNK), F32),
            shape((8, 4 * CHUNK), F32),
            shape((HERE, 4 * CHUNK, 128), BF),
            shape((4 * CHUNK, 2 * WIDE), BF),
            shape((WIDE, 4 * CHUNK), BF),
            shape((4, CHUNK, 1024), BF),
            shape((4, 8, CHUNK), F32),
            shape((CHUNK, 128), F32),
        ),
        grid=(1,),
        in_specs=[SMEM_SPEC] + [any_spec((CHUNK + 16, 1024))] * 5 + [QKV_SPEC, SMALL_SPEC],
        out_specs=(any_spec((CHUNK, WIDE)),) * 4
        + (
            any_spec((WIDE, 4 * CHUNK)),
            any_spec((8, 4 * CHUNK)),
            any_spec((HERE, 4 * CHUNK, 128)),
            any_spec((4 * CHUNK, 2 * WIDE)),
            any_spec((WIDE, 4 * CHUNK)),
            any_spec((4, CHUNK, 1024)),
            any_spec((4, 8, CHUNK)),
            any_spec((CHUNK, 128)),
        ),
        scratch_shapes=[
            pltpu.VMEM((WIDE, 4 * CHUNK), BF),
            pltpu.VMEM((WIDE, CHUNK), F32),
            pltpu.VMEM((HERE, CHUNK, CHUNK), F32),
            pltpu.VMEM((HERE, CHUNK, CHUNK), BF),
            pltpu.VMEM((4, CHUNK, 128), F32),
            pltpu.SMEM((2, 4), jnp.int32),
        ],
        compiler_params=PARAMS,
    )(scalars, *xs, pack, pack)


def normalise(h):
    centre = h - jnp.mean(h, axis=-1, keepdims=True)
    inverse = lax.rsqrt(jnp.mean(centre * centre, axis=-1, keepdims=True) + EPSILON)
    return centre * inverse, inverse


def norm_pullback(upstream, scaled, inverse, gain):
    e = upstream * gain
    return inverse * (
        e
        - jnp.mean(e, axis=-1, keepdims=True)
        - scaled * jnp.mean(e * scaled, axis=-1, keepdims=True)
    )


def relative(f, sc):
    return 2 * jnp.bitwise_xor(sc[1], f // 2) + jnp.bitwise_xor(sc[2], f % 2)


TILE = 16


def eight(x):
    return jnp.sum(x.reshape(TILE // 8, 8, x.shape[1]), axis=0)


def out_kernel(
    sc, tok, r0, r1, r2, r3, w, small, valid, normed, low, low_rel, scaled, inv, mixed, stats, acc
):
    z = sc[0]
    for k, r in enumerate((r0, r1, r2, r3)):
        a = lax.rem(z + k, 4)
        mixed[:, pl.ds(pl.multiple_of(a * WIDE, WIDE), WIDE)] = r[...]
    acc[...] = dot(mixed[...], w[...].reshape(1024, 1024))
    bias, gain, shift_by = vec(small, 0, 256, 128), vec(small, 0, 384, 128), vec(small, 0, 512, 128)

    def tile(t, carry):
        rows = pl.ds(pl.multiple_of(t * TILE, TILE), TILE)
        branch = acc[rows, :] + bias
        x = tok[rows, :].astype(F32)
        n, inverse = normalise(x + branch)
        y = n * gain + shift_by
        normed[rows, :] = y
        low[rows, :] = y.astype(BF)
        scaled[rows, :] = n
        inv[rows, :] = jnp.broadcast_to(inverse, (TILE, 128))
        ok = valid[rows, 0:1]
        return carry[0] + eight(ok * x * x), carry[1] + eight(ok * branch * branch)

    zero = jnp.zeros((8, 1024), F32)
    stream, branch = lax.fori_loop(0, CHUNK // TILE, tile, (zero, zero), unroll=4)
    for f in range(SHARDS):
        at = pl.multiple_of(relative(f, sc) * ROWS, ROWS)
        low_rel[:, pl.ds(at, ROWS)] = low[:, ROWS * f : ROWS * f + ROWS]
    lane = lax.broadcasted_iota(jnp.int32, (8, 128), 1)
    stats[...] = jnp.where(
        lane == 0,
        jnp.sum(stream),
        jnp.where(
            lane == 1, jnp.sum(branch), jnp.where(lane == 3, jnp.sum(valid[:, 0:1]), 0.0)
        ),
    )


def out_project(scalars, tok, parts, pack, valid):
    shape = jax.ShapeDtypeStruct
    full = lambda *s: any_spec(s)
    return pl.pallas_call(
        out_kernel,
        name="out_project",
        grid=(1,),
        out_shape=(
            shape((CHUNK, 1024), F32),
            shape((CHUNK, 1024), BF),
            shape((CHUNK, 1024), BF),
            shape((CHUNK, 1024), F32),
            shape((CHUNK, 128), F32),
            shape((CHUNK, 1024), BF),
            shape((8, 128), F32),
        ),
        in_specs=[SMEM_SPEC, full(CHUNK, 1024)]
        + [full(CHUNK, WIDE)] * 4
        + [OUT_SPEC, SMALL_SPEC, full(CHUNK, 128)],
        out_specs=(
            full(CHUNK, 1024),
            full(CHUNK, 1024),
            full(CHUNK, 1024),
            full(CHUNK, 1024),
            full(CHUNK, 128),
            full(CHUNK, 1024),
            full(8, 128),
        ),
        scratch_shapes=[pltpu.VMEM((CHUNK, 1024), F32)],
        compiler_params=PARAMS,
    )(scalars, tok, *parts, pack, pack, valid)


UP_SPECS = [pl.BlockSpec((ROWS, 1024), lambda j: (0, j))] * SHARDS


def gate_kernel(low, low_rel, mixed, *refs):
    ups = refs[0:SHARDS]
    small, acts, slope, pre = refs[SHARDS:]
    j = pl.program_id(0)
    pre[...] = dot(low_rel[...], jnp.concatenate([u[...] for u in ups]))
    bias = jnp.concatenate(
        [small[2 * j + n, 1:2, 256:768].astype(F32) for n in range(2)], axis=1
    )
    for t in range(CHUNK // TILE):
        rows = slice(TILE * t, TILE * t + TILE)
        for n in range(2):
            cols = slice(512 * n, 512 * n + 512)
            gate = pre[rows, cols] + bias[:, cols]
            cdf = 0.5 * (1.0 + lax.erf(gate * (2.0 ** -0.5)))
            acts[j, rows, cols] = (gate * cdf).astype(BF)
            slope[rows, cols] = cdf + gate * (jnp.exp(-0.5 * gate * gate) * 0.3989422804014327)

    @pl.when(j == 0)
    def _():
        acts[4] = low[...]
        acts[5] = mixed[...]


def mlp_gate(low, low_rel, mixed, ups, pack):
    shape = jax.ShapeDtypeStruct
    full = lambda *s: any_spec(s)
    return pl.pallas_call(
        gate_kernel,
        name="mlp_gate",
        grid=(4,),
        out_shape=(shape((6, CHUNK, 1024), BF), shape((CHUNK, 4096), F32)),
        in_specs=[full(CHUNK, 1024)] * 3 + UP_SPECS + [SMALL_SPEC],
        out_specs=(full(6, CHUNK, 1024), pl.BlockSpec((CHUNK, 1024), lambda j: (0, j))),
        scratch_shapes=[pltpu.VMEM((CHUNK, 1024), F32)],
        compiler_params=PARAMS,
    )(low, low_rel, mixed, *ups, pack)


def mlp_tail_kernel(sc, acts, down_cols, down_rows, slope, small, valid, inv, *refs):
    far = refs[0 : SHARDS + 4]
    (
        out,
        grads,
        gh1,
        g0,
        g1,
        g2,
        g3,
        sums_m,
        stats,
        sums_a,
        ub,
        acc,
        gh2,
        gm,
        gg_all,
        pre,
        total,
        held,
        normed,
        cot,
        scaled,
        wout,
        sems,
    ) = refs[SHARDS + 4 :]
    s = pl.program_id(0)
    z = sc[0]
    targets = [normed, cot, scaled, wout] + [held.at[n] for n in range(SHARDS)]
    sources = [far[0], far[1], far[2], far[3].at[:, 0:ROWS, :]] + list(far[4:])
    copies = [
        pltpu.make_async_copy(src, dst, sems.at[n])
        for n, (src, dst) in enumerate(zip(sources, targets))
    ]
    zero = jnp.zeros((8, 1024), F32)

    def tiles(body, count):
        totals = lax.fori_loop(0, CHUNK // TILE, body, (zero,) * count, unroll=4)
        return [jnp.sum(t, axis=0, keepdims=True) for t in totals]

    @pl.when(s == 0)
    def _():
        for copy in copies:
            copy.start()

    @pl.when(s < 2)
    def _():
        hidden = jnp.concatenate([acts[b] for b in range(4)], axis=1)
        for n in range(2):
            cols = pl.ds(pl.multiple_of(jnp.minimum(s, 1) * 512 + 256 * n, 256), 256)
            part = down_cols[:, :, 256 * n : 256 * n + 256].reshape(4096, 256)
            acc[:, cols] = dot(hidden, part)

    @pl.when(s == 1)
    def _():
        for copy in copies[0:2]:
            copy.wait()
        bias, gain, shift_by = vec(small, 0, 640, 128), vec(small, 1, 0, 128), vec(small, 1, 128, 128)

        def tile(t, carry):
            rows = pl.ds(pl.multiple_of(t * TILE, TILE), TILE)
            branch = acc[rows, :] + bias
            unit, inverse = normalise(normed[rows, :] + branch)
            out[rows, :] = (unit * gain + shift_by).astype(BF)
            ok = valid[rows, 0:1]
            u = cot[rows, :].astype(F32) * ok
            g = norm_pullback(u, unit, inverse, gain)
            gh2[rows, :] = g
            g_low = g.astype(BF)
            gm[rows, :] = g_low
            terms = (u * unit, u, g_low.astype(F32), ok * branch * branch)
            return tuple(c + eight(v) for c, v in zip(carry, terms))

        totals = tiles(tile, 4)
        sums_m[...] = jnp.zeros_like(sums_m)
        for at in range(3):
            sums_m[at : at + 1, :] = totals[at]
        lane = lax.broadcasted_iota(jnp.int32, (8, 128), 1)
        stats[...] = jnp.where(lane == 2, jnp.sum(totals[3]), 0.0)

    @pl.when((s >= 2) & (s < 6))
    def _():
        j = jnp.clip(s - 2, 0, 3)
        pre[...] = dot(gm[...], down_rows[...].reshape(1024, 1024), ((1,), (1,)))
        for n in range(2):
            cols = slice(512 * n, 512 * n + 512)
            total_ub = jnp.zeros((8, 512), F32)
            for t in range(CHUNK // TILE):
                rows = slice(TILE * t, TILE * t + TILE)
                gg = (pre[rows, cols] * slope[rows, cols]).astype(BF)
                gg_all[j, rows, cols] = gg
                grads[0, rows, cols] = gg
                total_ub = total_ub + eight(gg.astype(F32))
            row = jnp.sum(total_ub, axis=0, keepdims=True)
            for q in range(4):
                to = pl.ds(pl.multiple_of((2 * j + n) * 128, 128), 128)
                ub[q : q + 1, to] = row[:, 128 * q : 128 * q + 128]

    @pl.when(s == 6)
    def _():
        grads[0] = gm[...]
        for copy in copies[2:]:
            copy.wait()

    @pl.when(s >= 6)
    def _():
        gg = jnp.concatenate([gg_all[b] for b in range(4)], axis=1)
        for m in range(2):
            j = jnp.clip(2 * (s - 6) + m, 0, 3)
            rows = held[pl.ds(2 * j, 2)].reshape(2 * ROWS, 4096)
            part = dot(gg, rows, ((1,), (1,)))
            pair = jnp.bitwise_xor(sc[1], j)
            for t in range(2):
                f = 2 * pair + jnp.bitwise_xor(sc[2], t)
                to = pl.ds(pl.multiple_of(f * ROWS, ROWS), ROWS)
                total[:, to] = part[:, ROWS * t : ROWS * t + ROWS]

    @pl.when(s == 7)
    def _():
        gain = vec(small, 0, 384, 128)

        def tile(t, carry):
            rows = pl.ds(pl.multiple_of(t * TILE, TILE), TILE)
            u = gh2[rows, :] + total[rows, :]
            n = scaled[rows, :]
            g = norm_pullback(u, n, inv[rows, 0:1], gain)
            gh1[rows, :] = g
            g_low = g.astype(BF)
            grads[0, rows, :] = g_low
            terms = (u * n, u, g_low.astype(F32))
            return tuple(c + eight(v) for c, v in zip(carry, terms))

        totals = tiles(tile, 3)
        sums_a[...] = jnp.zeros_like(sums_a)
        for at in range(3):
            sums_a[at : at + 1, :] = totals[at]
        g_low = grads[0]
        for k, g_out in enumerate((g0, g1, g2, g3)):
            a = lax.rem(z + k, 4)
            rows = wout[pl.ds(2 * a, 2)].reshape(WIDE, 1024)
            g_out[...] = dot(g_low, rows, ((1,), (1,))).astype(BF)


def mlp_tail(scalars, acts, slope, ups, down, normed, scaled, inv, pack, cot, valid):
    shape = jax.ShapeDtypeStruct
    full = lambda *s: any_spec(s)
    block = lambda s: jnp.clip(s - 2, 0, 3)

    def grads_at(s):
        return (jnp.where(s < 6, block(s), jnp.where(s < 7, 5, 4)), 0, 0)

    return pl.pallas_call(
        mlp_tail_kernel,
        name="mlp_tail",
        grid=(8,),
        in_specs=[
            SMEM_SPEC,
            full(4, CHUNK, 1024),
            pl.BlockSpec((SHARDS, 512, 512), lambda s: (0, 0, jnp.minimum(s, 1))),
            pl.BlockSpec((2, 512, 1024), lambda s: (block(s), 0, 0)),
            pl.BlockSpec((CHUNK, 1024), lambda s: (0, block(s))),
            SMALL_SPEC,
            full(CHUNK, 128),
            full(CHUNK, 128),
        ]
        + [pl.BlockSpec(memory_space=pl.ANY)] * (SHARDS + 4),
        out_specs=(
            full(CHUNK, 1024),
            pl.BlockSpec((1, CHUNK, 1024), grads_at),
            full(CHUNK, 1024),
        )
        + (full(CHUNK, WIDE),) * 4
        + (full(8, 1024), full(8, 128), full(8, 1024), full(4, 1024)),
        out_shape=(
            shape((CHUNK, 1024), BF),
            shape((6, CHUNK, 1024), BF),
            shape((CHUNK, 1024), F32),
        )
        + (shape((CHUNK, WIDE), BF),) * 4
        + (
            shape((8, 1024), F32),
            shape((8, 128), F32),
            shape((8, 1024), F32),
            shape((4, 1024), F32),
        ),
        scratch_shapes=[
            pltpu.VMEM((CHUNK, 1024), F32),
            pltpu.VMEM((CHUNK, 1024), F32),
            pltpu.VMEM((CHUNK, 1024), BF),
            pltpu.VMEM((4, CHUNK, 1024), BF),
            pltpu.VMEM((CHUNK, 1024), F32),
            pltpu.VMEM((CHUNK, 1024), F32),
            pltpu.VMEM((SHARDS, ROWS, 4096), BF),
            pltpu.VMEM((CHUNK, 1024), F32),
            pltpu.VMEM((CHUNK, 1024), BF),
            pltpu.VMEM((CHUNK, 1024), F32),
            pltpu.VMEM((SHARDS, ROWS, 1024), BF),
            pltpu.SemaphoreType.DMA((SHARDS + 4,)),
        ],
        compiler_params=PARAMS,
    )(scalars, acts, down, down, slope, pack, valid, inv, normed, cot, scaled, pack, *ups)


REST = 640


def product(left, right, res):
    for n in range(4):
        cols = slice(256 * n, 256 * n + 256)
        res[:, cols] = dot(left[...], right[:, cols]).astype(BF)


def down_kernel(count, sc, ho, hp, go, gp, *refs):
    outs = refs[0:count]
    left, right, res = refs[count:]
    s = pl.program_id(0)

    @pl.when(s == 0)
    def _():
        right[0:CHUNK] = go[0]
        right[CHUNK:] = gp[0]

    left[:, 0:CHUNK] = jnp.transpose(ho[0])
    left[:, CHUNK:] = jnp.transpose(hp[0])
    product(left, right, res)
    for n, out in enumerate(outs):

        @pl.when(s == n)
        def _():
            out[...] = res[...]


def down_grads(scalars, acts, acts_p, grads, grads_p, distances):
    shape = jax.ShapeDtypeStruct
    full = lambda *s: pl.BlockSpec(s, lambda j, sc: (0,) * len(s))
    first, count = distances[0], len(distances)

    def hid(j, sc):
        f = 2 * jnp.bitwise_xor(sc[1], first + j) + sc[2]
        return (f // 2, 0, f % 2)

    hidden = pl.BlockSpec((1, CHUNK, 512), hid)
    grad = pl.BlockSpec((1, CHUNK, 1024), lambda j, sc: (5, 0, 0))
    return pl.pallas_call(
        partial(down_kernel, count),
        name="down_grads",
        grid_spec=pltpu.PrefetchScalarGridSpec(
            num_scalar_prefetch=1,
            grid=(count,),
            in_specs=[hidden, hidden, grad, grad],
            out_specs=(full(512, 1024),) * count,
            scratch_shapes=[
                pltpu.VMEM((512, 2 * CHUNK), BF),
                pltpu.VMEM((2 * CHUNK, 1024), BF),
                pltpu.VMEM((512, 1024), BF),
            ],
        ),
        out_shape=(shape((512, 1024), BF),) * count,
        compiler_params=PARAMS,
    )(scalars, acts, acts_p, grads, grads_p)


def rest_kernel(sc, lo, lp, go, gp, r3, r1, r2, r0, low_sel, mix_sel, right, res):
    s = pl.program_id(0)
    chip, core = sc[1], sc[2]

    @pl.when(s == 0)
    def _():
        for r in range(4):
            at = pl.multiple_of((2 * jnp.bitwise_xor(chip, r) + core) * ROWS, ROWS)
            to = slice(ROWS * r, ROWS * r + ROWS)
            for n, out in enumerate((low_sel, mix_sel)):
                out[to, 0:CHUNK] = jnp.transpose(lo[n, :, pl.ds(at, ROWS)])
                out[to, CHUNK:] = jnp.transpose(lp[n, :, pl.ds(at, ROWS)])

    @pl.when(s == 4)
    def _():
        low_sel[...] = mix_sel[...]

    right[0:CHUNK] = go[0]
    right[CHUNK:] = gp[0]
    product(low_sel, right, res)
    for r, out in enumerate((r0, r1, r2, r3)):
        out[...] = res[ROWS * r : ROWS * r + ROWS, :]


def rest_grads(scalars, acts, acts_p, grads, grads_p):
    shape = jax.ShapeDtypeStruct
    full = lambda *s: pl.BlockSpec(s, lambda j, sc: (0,) * len(s))
    flat = pl.BlockSpec((pl.Element(2), pl.Element(CHUNK), pl.Element(1024)), lambda j, sc: (4, 0, 0))
    grad = pl.BlockSpec((1, CHUNK, 1024), lambda j, sc: (j, 0, 0))
    return pl.pallas_call(
        rest_kernel,
        name="rest_grads",
        grid_spec=pltpu.PrefetchScalarGridSpec(
            num_scalar_prefetch=1,
            grid=(5,),
            in_specs=[flat, flat, grad, grad],
            out_specs=(pl.BlockSpec((ROWS, 1024), lambda j, sc: (j, 0)),) * 4,
            scratch_shapes=[
                pltpu.VMEM((512, 2 * CHUNK), BF),
                pltpu.VMEM((512, 2 * CHUNK), BF),
                pltpu.VMEM((2 * CHUNK, 1024), BF),
                pltpu.VMEM((512, 1024), BF),
            ],
        ),
        out_shape=(shape((REST, 1024), BF),) * 4,
        compiler_params=PARAMS,
    )(scalars, acts, acts_p, grads, grads_p)


def attn_bwd_kernel(
    sc,
    segr,
    w,
    qm,
    kv,
    kt,
    mixt,
    lse,
    g0,
    g1,
    g2,
    g3,
    ig,
    dall,
    segc,
    ends,
    gs,
    dq,
    dqt,
    dk,
    dv,
    delta,
    scores,
    slopes,
    probs,
    pulls,
):
    z = sc[0]
    segment_setup(segr, segc, ends)
    dk[...] = jnp.zeros_like(dk)
    dv[...] = jnp.zeros_like(dv)
    for k, g in enumerate((g0, g1, g2, g3)):
        rows = pl.ds(pl.multiple_of(lax.rem(z - k + 4, 4) * CHUNK, CHUNK), CHUNK)
        turned = jnp.transpose(g[...])
        for h in range(HERE):
            head = slice(h * HEAD_DIM, (h + 1) * HEAD_DIM)
            gs[h, rows, :] = one_head(g[...], h)
            prod = turned[head, :].astype(F32) * mixt[head, rows]
            delta[h : h + 1, rows] = jnp.sum(prod, axis=0, keepdims=True)

    def q_chunk(i, carry):
        rows = pl.ds(pl.multiple_of(i * CHUNK, CHUNK), CHUNK)
        low, high = key_range(ends, i)
        row = segr[i][0:1, :]
        dqt[...] = jnp.zeros_like(dqt)

        def key_chunk(j, inner):
            keys = pl.ds(pl.multiple_of(j * CHUNK, CHUNK), CHUNK)
            col = segc[j]
            mask = jnp.concatenate([col, col], axis=1) == row
            for h in range(HERE):
                low_lane = 128 * (h // 2)
                pair = slice(low_lane, low_lane + 128)
                scores[h] = dot(kv[keys, pair], qm[h, rows, :], ((1,), (1,)))
                wide = slice(WIDE + low_lane, WIDE + low_lane + 128)
                slopes[h] = dot(kv[keys, wide], gs[h, rows, :], ((1,), (1,)))
            for h in range(HERE):
                log, shift_by = lse[h : h + 1, rows], delta[h : h + 1, rows]
                for t in range(4):
                    tile = slice(64 * t, 64 * t + 64)
                    p = jnp.where(mask[tile, :], jnp.exp(scores[h, tile, :] - log), 0.0)
                    probs[h, tile, :] = p.astype(BF)
                    pulls[h, tile, :] = (p * (slopes[h, tile, :] - shift_by)).astype(BF)
            for h in range(HERE):
                head = slice(h * HEAD_DIM, (h + 1) * HEAD_DIM)
                pair = slice(128 * (h // 2), 128 * (h // 2) + 128)
                dv[keys, pair] += dot(probs[h], gs[h, rows, :])
                dk[keys, pair] += dot(pulls[h], qm[h, rows, :])
                dqt[head, :] += dot(kt[head, keys], pulls[h])
            return inner

        lax.fori_loop(low, high, key_chunk, 0)
        dq[...] = (dqt[...] * SCALE).astype(BF)
        dall[rows, 0:WIDE] = jnp.transpose(dq[...])
        return carry

    lax.fori_loop(0, 4, q_chunk, 0)
    dall[:, WIDE : 2 * WIDE] = dk[...].astype(BF)
    dall[:, 2 * WIDE :] = dv[...].astype(BF)
    weight = w[...].reshape(SHARDS * ROWS, 3 * WIDE)
    for k in range(4):
        rows = slice(CHUNK * k, CHUNK * k + CHUNK)
        ig[rows, :] = dot(dall[rows, :], weight, ((1,), (1,))).astype(BF)


def qkv_kernel(sc, xall, dall, sums_m, sums_a, ubt, stats_a, stats_m, out, small, acc):
    z = sc[0]
    for k in range(4):
        part = dot(xall[k], dall[CHUNK * k : CHUNK * k + CHUNK, :], ((0,), (0,)))
        if k == 0:
            acc[...] = part
        else:
            acc[...] += part
    out[:, 0 : 3 * WIDE] = acc[...].astype(BF)
    here = pl.ds(pl.multiple_of(z * WIDE, WIDE), WIDE)
    small[...] = jnp.zeros_like(small)
    small[0:3, :] = sums_m[0:3, :]
    small[3:6, :] = sums_a[0:3, :]
    small[6:7, here] = jnp.sum(dall[:, 0:WIDE].astype(F32), axis=0, keepdims=True)
    small[7:8, here] = jnp.sum(dall[:, 2 * WIDE :].astype(F32), axis=0, keepdims=True)
    small[8:12, :] = ubt[...]
    every = lambda value: jnp.broadcast_to(value, (1, 1024))
    small[12:13, :] = every(stats_a[0:1, 0:1])
    small[13:14, :] = every(stats_a[0:1, 1:2])
    small[14:15, :] = every(stats_m[0:1, 2:3])
    count = stats_a[0:1, 3:4]
    high = jnp.floor(count * 0.0625)
    small[15:16, :] = every(high)
    small[16:17, :] = every(count - 16.0 * high)
    out[:, 3 * WIDE :] = jnp.transpose(small[...]).astype(BF)


def qkv_grads(scalars, xall, dall, smalls):
    return pl.pallas_call(
        qkv_kernel,
        name="qkv_grads",
        out_shape=jax.ShapeDtypeStruct((1024, 3 * WIDE + 128), BF),
        in_specs=[SMEM_SPEC] + [VMEM_SPEC] * 7,
        out_specs=VMEM_SPEC,
        scratch_shapes=[pltpu.VMEM((128, 1024), F32), pltpu.VMEM((1024, 3 * WIDE), F32)],
        compiler_params=PARAMS,
    )(scalars, xall, dall, *smalls)


def attn_bwd(scalars, segr, pack, qm, kv, kt, mixt, lse, gs):
    shape = jax.ShapeDtypeStruct
    return pl.pallas_call(
        attn_bwd_kernel,
        name="attn_bwd",
        out_shape=(shape((1024, 1024), BF), shape((1024, 3 * WIDE), BF)),
        grid=(1,),
        in_specs=[SMEM_SPEC]
        + [
            any_spec((4, 8, CHUNK)),
            QKV_SPEC,
            any_spec((HERE, 4 * CHUNK, 128)),
            any_spec((4 * CHUNK, 2 * WIDE)),
            any_spec((WIDE, 4 * CHUNK)),
            any_spec((WIDE, 4 * CHUNK)),
            any_spec((8, 4 * CHUNK)),
        ]
        + [any_spec((CHUNK, WIDE))] * 4,
        out_specs=(any_spec((1024, 1024)), any_spec((1024, 3 * WIDE))),
        scratch_shapes=[
            pltpu.VMEM((4, CHUNK, 128), F32),
            pltpu.SMEM((2, 4), jnp.int32),
            pltpu.VMEM((HERE, 4 * CHUNK, 128), BF),
            pltpu.VMEM((WIDE, CHUNK), BF),
            pltpu.VMEM((WIDE, CHUNK), F32),
            pltpu.VMEM((4 * CHUNK, WIDE), F32),
            pltpu.VMEM((4 * CHUNK, WIDE), F32),
            pltpu.VMEM((8, 4 * CHUNK), F32),
            pltpu.VMEM((HERE, CHUNK, CHUNK), F32),
            pltpu.VMEM((HERE, CHUNK, CHUNK), F32),
            pltpu.VMEM((HERE, CHUNK, CHUNK), BF),
            pltpu.VMEM((HERE, CHUNK, CHUNK), BF),
        ],
        compiler_params=PARAMS,
    )(scalars, segr, pack, qm, kv, kt, mixt, lse, *gs)


def finish_kernel(sc, *refs):
    z = sc[0]
    pieces, (gq, gk, gv), vectors, ub, rms = refs[0:4], refs[4:7], refs[7:15], refs[15], refs[16:19]
    for k, piece in enumerate(pieces):
        cols = pl.ds(pl.multiple_of(lax.rem(z - k + 4, 4) * WIDE, WIDE), WIDE)
        for n, out in enumerate((gq, gk, gv)):
            out[:, cols] = piece[:, WIDE * n : WIDE * n + WIDE].astype(F32)
    extra = pieces[0][:, 3 * WIDE :].astype(F32)
    for piece in pieces[1:]:
        extra = extra + piece[:, 3 * WIDE :].astype(F32)
    extra = jnp.transpose(extra)
    for n, out in enumerate(vectors):
        out[...] = extra[n : n + 1, :]
    ub[...] = extra[8:12, :]
    counted = (16.0 * extra[15:16, 0:1] + extra[16:17, 0:1]) * 1024.0
    for n, out in enumerate(rms):
        out[...] = jnp.sqrt(extra[12 + n : 13 + n, 0:1] / counted)


def finish(scalars, pieces):
    shape = jax.ShapeDtypeStruct
    shapes = [(ROWS, 1024)] * 3 + [(1, ROWS)] * 8 + [(4, ROWS)] + [(1, 1)] * 3
    return pl.pallas_call(
        finish_kernel,
        name="finish",
        out_shape=tuple(shape(n, F32) for n in shapes),
        in_specs=[SMEM_SPEC] + [VMEM_SPEC] * 4,
        out_specs=(VMEM_SPEC,) * len(shapes),
        compiler_params=PARAMS,
    )(scalars, *pieces)


def line_gather(x):
    right = lax.ppermute(x, "ctx", [(0, 1), (1, 2), (2, 3)])
    left = lax.ppermute(x, "ctx", [(1, 0), (2, 1), (3, 2)])
    two = lax.ppermute(x, "ctx", [(0, 2), (1, 3), (2, 0), (3, 1)])
    return [x, right, left, two]


def line_forward(two):
    return lax.ppermute(two, "ctx", [(1, 0), (2, 3)])


def shift(x, k):
    n = lax.axis_size("ctx")
    return lax.ppermute(x, "ctx", [(i, (i + k) % n) for i in range(n)])


def swap(x, bits):
    return lax.ppermute(x, "fsdp", [(i, i ^ bits) for i in range(lax.axis_size("fsdp"))])


def add(*terms):
    total = terms[0].astype(F32)
    for term in terms[1:]:
        total = total + term.astype(F32)
    return total


def neighbour(x, bits):
    return lax.ppermute(x, "ctx", [(i, i ^ bits) for i in range(4)])


def half_sum(terms, which):
    half = terms[0].shape[0] // 2
    return add(*[lax.dynamic_slice_in_dim(t, which * half, half, 0) for t in terms])


class LineSum:
    def __init__(self, *terms):
        self.terms = terms
        self.odd = lax.axis_index("ctx") % 2

    def first(self):
        return half_sum(self.terms, 1 - self.odd).astype(BF)

    def second(self, got):
        self.pair = add(half_sum(self.terms, self.odd), got).astype(BF)
        return self.pair

    def third(self, got):
        self.whole = add(self.pair, got).astype(BF)
        return self.whole

    def result(self, got):
        even = self.odd == 0
        low = jnp.where(even, self.whole, got)
        return jnp.concatenate([low, jnp.where(even, got, self.whole)]).astype(F32)


def line_sum(*terms):
    parts = LineSum(*terms)
    got = neighbour(parts.first(), 1)
    got = neighbour(parts.second(got), 2)
    return parts.result(neighbour(parts.third(got), 1))


def per_device(
    tokens,
    segment_ids,
    cotangent,
    query_weight,
    query_bias,
    key_weight,
    value_weight,
    value_bias,
    out_weight,
    out_bias,
    attn_gain,
    attn_shift,
    up_weight,
    up_bias,
    down_weight,
    down_bias,
    mlp_gain,
    mlp_shift,
):
    owners = lax.axis_size("fsdp")
    plane = owners == SHARDS
    z = lax.axis_index("ctx")
    f = lax.axis_index("fsdp")
    if plane:
        chip, core = f // 2, f % 2
    else:
        chip, core = jnp.int32(0), jnp.int32(0)
    scalars = jnp.stack([z, chip, core, z]).astype(jnp.int32)
    tok = tokens[0]
    if plane:
        weights = (query_weight, key_weight, value_weight, out_weight)
        vectors = (query_bias, value_bias, out_bias, attn_gain, attn_shift, down_bias)
        vectors += (mlp_gain, mlp_shift, up_bias)
        packed, mine_pack = pack_inputs(scalars, tok, segment_ids, weights, vectors)
        pack = lax.all_gather(mine_pack, "fsdp", axis=0)
        xs = line_gather(packed)
        xs.append(line_forward(xs[3]))
        near_x, near_y = swap(up_weight, 2), swap(up_weight, 4)
        half = up_weight.shape[1] // 2
        far = [swap(near_x[:, :half], 4), swap(near_y[:, half:], 2)]
        xs, near_x, near_y, after, pack = lax.optimization_barrier(
            (xs, near_x, near_y, down_weight, pack)
        )
        down = lax.all_gather(after, "fsdp", axis=0)
    else:
        seg_row = jnp.pad(segment_ids.astype(BF), ((0, 15), (0, 1024 - CHUNK)))
        packed = jnp.concatenate([tok, seg_row])
        xs = line_gather(packed)
        xs.append(line_forward(xs[3]))
        quarter = jnp.concatenate(
            [
                lax.dynamic_slice_in_dim(m, z * WIDE, WIDE, 1)
                for m in (query_weight, key_weight, value_weight)
            ],
            axis=1,
        )
        whole = lambda m: lax.all_gather(m, "fsdp", axis=0, tiled=True)
        split = lambda m: whole(m).reshape(SHARDS, -1)
        line0 = jnp.concatenate(
            [split(m) for m in (query_bias, value_bias, out_bias, attn_gain, attn_shift, down_bias)],
            axis=1,
        )
        line1 = jnp.concatenate([split(m) for m in (mlp_gain, mlp_shift, up_bias)], axis=1)
        lines = jnp.pad(jnp.stack([line0, line1], axis=1), ((0, 0), (0, 14), (0, 0)))
        pack = jnp.concatenate([whole(quarter).reshape(SHARDS, ROWS, 768), lines], axis=1)
        out_rows = whole(out_weight).reshape(SHARDS, ROWS, 1024)
        wide = lambda m: jnp.pad(m, ((0, 0), (0, 0), (0, 1024 - m.shape[2])))
        pack = jnp.concatenate([out_rows, wide(pack)], axis=1)
        ups = list(whole(up_weight).reshape(SHARDS, ROWS, 4096))
        down = whole(down_weight).reshape(SHARDS, 512, 1024)

    m0, m1, m2, m3, mixt, lse, qm, kv, kt, xall, segr, valid = attn_fwd(scalars, xs, pack)
    parts = [m0] + [shift(m, -k) for k, m in ((1, m1), (2, m2), (3, m3))]
    if plane:
        ups = [up_weight, swap(up_weight, 1)]
        far, _ = lax.optimization_barrier((far, m0))
        far = jnp.concatenate(far, axis=1)
        parts, near_x, near_y, far = lax.optimization_barrier((parts, near_x, near_y, far))
        for rows in (near_x, near_y, far):
            ups += [rows, swap(rows, 1)]
    normed, low, low_rel, scaled, inv, mixed, stats_a = out_project(
        scalars, tok, parts, pack, valid
    )
    acts, slope = mlp_gate(low, low_rel, mixed, ups, pack)
    acts_p = swap(acts, 1)
    result, grads, gh1, g0, g1, g2, g3, sums_m, stats_m, sums_a, ub = mlp_tail(
        scalars, acts, slope, ups, down, normed, scaled, inv, pack, cotangent[0], valid
    )
    gs = [g0] + [shift(g, k) for k, g in ((1, g1), (2, g2), (3, g3))]
    grads_p = swap(grads, 1)
    (d3,) = down_grads(scalars, acts, acts_p, grads, grads_p, (3,))
    d0, d1, d2 = down_grads(scalars, acts, acts_p, grads, grads_p, (0, 1, 2))
    if plane:
        d_far = swap(d3, 2)
    r3, r1, r2, r0 = rest_grads(scalars, acts, acts_p, grads, grads_p)
    gs, r3, r1, r2, r0 = lax.optimization_barrier((gs, r3, r1, r2, r0))
    if plane:
        r_far = swap(r3, 4)
    if not plane:
        ub = ub.reshape(4, SHARDS, 128).swapaxes(0, 1).reshape(1024, 4).T
    smalls = (sums_m, sums_a, ub, stats_a, stats_m)
    ig, dall = attn_bwd(scalars, segr, pack, qm, kv, kt, mixt, lse, gs)
    tie = lax.optimization_barrier
    if plane:
        ig, dall, d_far, r_far = tie((ig, dall, d_far, r_far))
    ig = lax.psum_scatter(ig, "ctx", scatter_dimension=0, tiled=True)
    if plane:
        to_x = add(r1, r_far).astype(BF)
        to_x, r2, dall, d_far = tie((to_x, r2, dall, d_far))
        r_from_x, r_from_y = swap(to_x, 2), swap(r2, 4)
    gw = qkv_grads(scalars, xall, dall, smalls)
    if plane:
        to_y = add(d2, d_far).astype(BF)
        r_sum = LineSum(r0, r_from_x, r_from_y)
        r_first, gw, to_y, d1 = tie((r_sum.first(), gw, to_y, d1))
        d_from_x, d_from_y = swap(d1, 2), swap(to_y, 4)
        got_r = neighbour(r_first, 1)
        ig, gw, d_from_x, d_from_y, got_r = tie((ig, gw, d_from_x, d_from_y, got_r))
    q_own = lax.psum_scatter(gw, "fsdp", scatter_dimension=0, tiled=True)
    q_low = q_own.astype(BF)

    if plane:
        d_from_x, d_from_y, got_r = tie((d_from_x, d_from_y, got_r))
        got_r = neighbour(r_sum.second(got_r), 2)
        d_sum = LineSum(d0, d_from_x, d_from_y)
        got = neighbour(d_sum.first(), 1)
        r_third = r_sum.third(got_r)
        got_r = neighbour(r_third, 1)
        got, _ = tie((got, r_third))
        d_second = d_sum.second(got)
        got = neighbour(d_second, 2)
        q_low, _ = tie((q_low, d_second))
        q_pieces = [q_low] + [shift(q_low, k) for k in (1, 2, 3)]
        got, got_r, q_pieces = tie((got, got_r, q_pieces))
        rest = r_sum.result(got_r)
        grad_down = d_sum.result(neighbour(d_sum.third(got), 1))
        input_grad = add(gh1, ig)
        grad_up = jnp.concatenate([rest[ROWS * b : ROWS * b + ROWS] for b in range(4)], axis=1)
        grad_out = rest[4 * ROWS :]
    else:
        other = scalars.at[2].set(1)
        sums_w = (d3, d1, d2, d0, r3, r1, r2, r0)
        e0, e1, e2, e3 = down_grads(other, acts, acts_p, grads, grads_p, (0, 1, 2, 3))
        second = (e3, e1, e2, e0)
        second += rest_grads(other, acts, acts_p, grads, grads_p)
        rows_of = lambda t: ([t[3], t[1], t[2], t[0]], [t[7], t[5], t[6], t[4]])
        down_0, rest_0 = rows_of(sums_w)
        down_1, rest_1 = rows_of(second)
        down_all = 0.5 * jnp.stack([m.astype(F32) for p in zip(down_0, down_1) for m in p])
        rest_all = 0.5 * jnp.stack([m.astype(F32) for p in zip(rest_0, rest_1) for m in p])
        scatter = lambda m: lax.psum_scatter(
            m.astype(BF), "fsdp", scatter_dimension=0, tiled=True
        )
        grad_down = line_sum(scatter(down_all.reshape(4096, 1024)))
        grad_up = line_sum(
            scatter(
                rest_all[:, 0:512]
                .reshape(SHARDS, 4, ROWS, 1024)
                .swapaxes(1, 2)
                .reshape(1024, 4096)
            )
        )
        grad_out = line_sum(scatter(rest_all[:, 512:].reshape(1024, 1024)))
        q_pieces = [q_low] + [shift(q_low, k) for k in (1, 2, 3)]
        input_grad = add(gh1, ig)
    if plane:
        done = finish(scalars, q_pieces)
        grad_q, grad_k, grad_v = done[0:3]
        vectors = [v.reshape(-1) for v in done[3:11]]
        up_bias_grad = done[11].reshape(-1)
        rms = [v.reshape(()) for v in done[12:15]]
    else:
        table = jnp.take(jnp.stack(q_pieces), (z - jnp.arange(4)) % 4, axis=0)
        extra = add(*q_pieces)[:, 3 * WIDE :]
        cols = lambda n: jnp.concatenate(
            [table[a, :, n * WIDE : (n + 1) * WIDE].astype(F32) for a in range(4)], axis=1
        )
        grad_q, grad_k, grad_v = cols(0), cols(1), cols(2)
        vectors = [extra[:, n] for n in range(8)]
        up_bias_grad = extra[:, 8:12].reshape(-1)
        counted = (16.0 * extra[0, 15] + extra[0, 16]) * 1024
        rms = [jnp.sqrt(extra[0, 12 + n] / counted) for n in range(3)]
    return (
        result[None],
        input_grad[None],
        grad_q,
        vectors[6],
        grad_k,
        grad_v,
        vectors[7],
        grad_out,
        vectors[5],
        vectors[3],
        vectors[4],
        grad_up,
        up_bias_grad,
        grad_down,
        vectors[2],
        vectors[0],
        vectors[1],
        rms[0],
        rms[1],
        rms[2],
    )


def solution(mesh):
    matrix, vector = P("fsdp", None), P("fsdp")
    stream = P("fsdp", "ctx", None)
    placed = (
        stream,
        P("fsdp", "ctx"),
        stream,
        matrix,
        vector,
        matrix,
        matrix,
        vector,
        matrix,
        vector,
        vector,
        vector,
        matrix,
        vector,
        matrix,
        vector,
        vector,
        vector,
    )
    return jax.shard_map(
        per_device,
        mesh=mesh,
        in_specs=placed,
        out_specs=(
            stream,
            stream,
            matrix,
            vector,
            matrix,
            matrix,
            vector,
            matrix,
            vector,
            vector,
            vector,
            matrix,
            vector,
            matrix,
            vector,
            vector,
            vector,
            P(),
            P(),
            P(),
        ),
        check_vma=False,
    )
```

```python
from functools import partial

import jax
import jax.numpy as jnp
from jax import lax
from jax.experimental import pallas as pl
from jax.experimental.pallas import tpu as pltpu
from jax.sharding import PartitionSpec as P

HEADS = 16
HEAD_DIM = 64
SEGS = 8
EPSILON = 1e-05
MASKED = -1000000000.0
SCALE = HEAD_DIM ** (-0.5)
BF = jnp.bfloat16
F32 = jnp.float32

CHUNK = 256
HERE = 4
WIDE = HERE * HEAD_DIM
SHARDS = 8
ROWS = 128
PACK = 2 * ROWS + 16
PARAMS = pltpu.CompilerParams(vmem_limit_bytes=60 * 1024 * 1024)


SMEM_SPEC = pl.BlockSpec(memory_space=pltpu.SMEM)
VMEM_SPEC = pl.BlockSpec(memory_space=pltpu.VMEM)


def dot(a, b, dims=((1,), (0,))):
    return lax.dot_general(a, b, (dims, ((), ())), preferred_element_type=F32)


def vec(small_ref, row, start, size):
    return jnp.concatenate(
        [small_ref[f, row : row + 1, start : start + size].astype(F32) for f in range(SHARDS)],
        axis=1,
    )


def any_spec(shape):
    return pl.BlockSpec(shape, lambda *a: (0,) * len(shape))


def pack_kernel(sc, tok, seg, wq, wk, wv, wout, qb, vb, ob, ag, sh, db, mg, ms, ub, xp, pk):
    z = sc[0]
    cols = pl.ds(pl.multiple_of(z * WIDE, WIDE), WIDE)
    xp[0:CHUNK] = tok[...]
    xp[CHUNK:] = jnp.zeros((16, 1024), BF)
    xp[CHUNK : CHUNK + 1, 0:CHUNK] = seg[...].astype(F32).astype(BF)
    pk[0:ROWS] = wout[...]
    for n, w in enumerate((wq, wk, wv)):
        pk[ROWS : 2 * ROWS, WIDE * n : WIDE * n + WIDE] = w[:, cols]
    pk[ROWS : 2 * ROWS, 3 * WIDE :] = jnp.zeros((ROWS, 1024 - 3 * WIDE), BF)
    pk[2 * ROWS :] = jnp.zeros((16, 1024), BF)
    at = slice(2 * ROWS, 2 * ROWS + 1)
    for n, vector in enumerate((qb, vb, ob, ag, sh, db)):
        pk[at, 128 * n : 128 * n + 128] = vector[...]
    at = slice(2 * ROWS + 1, 2 * ROWS + 2)
    for n, vector in enumerate((mg, ms)):
        pk[at, 128 * n : 128 * n + 128] = vector[...]
    for n in range(4):
        pk[at, 256 + 128 * n : 384 + 128 * n] = ub[n : n + 1, :]


def pack_inputs(scalars, tok, seg, weights, vectors):
    shape = jax.ShapeDtypeStruct
    return pl.pallas_call(
        pack_kernel,
        name="pack_inputs",
        in_specs=[SMEM_SPEC] + [VMEM_SPEC] * 15,
        out_specs=(VMEM_SPEC,) * 2,
        out_shape=(shape((CHUNK + 16, 1024), BF), shape((PACK, 1024), BF)),
        compiler_params=PARAMS,
    )(scalars, tok, seg, *weights, *[v.reshape(-1, 128) for v in vectors])


def segment_setup(rows, segc, ends):
    for a in range(4):
        row = rows[a][0:1, :]
        segc[a] = jnp.transpose(jnp.broadcast_to(row, (128, CHUNK)))
        ends[0, a] = jnp.min(row).astype(jnp.int32)
        ends[1, a] = jnp.max(row).astype(jnp.int32)


def key_range(ends, i):
    low = jnp.int32(0)
    high = jnp.int32(4)
    for j in range(4):
        low = low + (ends[1, j] < ends[0, i]).astype(jnp.int32)
        high = high - (ends[0, j] > ends[1, i]).astype(jnp.int32)
    return low, high


def one_head(x, h):
    pair = x[:, 128 * (h // 2) : 128 * (h // 2) + 128]
    lane = lax.broadcasted_iota(jnp.int32, pair.shape, 1)
    return jnp.where((lane < HEAD_DIM) == (h % 2 == 0), pair, jnp.zeros_like(pair))


def attn_fwd_kernel(
    sc,
    x0,
    right,
    left,
    x2,
    far,
    w,
    small,
    m0,
    m1,
    m2,
    m3,
    mixt,
    lse,
    qm,
    kv,
    kt,
    xall,
    segr,
    valid,
    vt,
    acc,
    scores,
    probs,
    segc,
    ends,
):
    z = sc[0]

    def place(k, src):
        a = lax.rem(z - k + 4, 4)
        xall[a] = src[0:CHUNK, :]
        segr[a] = jnp.broadcast_to(
            src[CHUNK : CHUNK + 16, 0:CHUNK].astype(F32)[0:1, :], (8, CHUNK)
        )

    place(0, x0)
    place(2, x2)
    for k, usual, end in ((1, right, 0), (3, left, 3)):
        pl.when(z == end)(partial(place, k, far))
        pl.when(z != end)(partial(place, k, usual))
    segment_setup(segr, segc, ends)
    valid[...] = (segc[z] != SEGS - 1).astype(F32)
    weight = w[...].reshape(SHARDS * ROWS, 3 * WIDE)
    first = small[2 * z].astype(F32)
    second = small[2 * z + 1].astype(F32)
    qb = jnp.concatenate([first[0:1, 0:128], second[0:1, 0:128]], axis=1)
    vb = jnp.concatenate([first[0:1, 128:256], second[0:1, 128:256]], axis=1)
    for n in range(4):
        at = slice(n * CHUNK, (n + 1) * CHUNK)
        prod = dot(xall[n], weight)
        q = ((prod[:, 0:WIDE] + qb).astype(BF).astype(F32) * SCALE).astype(BF)
        kk = prod[:, WIDE : 2 * WIDE].astype(BF)
        v = (prod[:, 2 * WIDE :] + vb).astype(BF)
        for h in range(HERE):
            qm[h, at, :] = one_head(q, h)
        kv[at, 0:WIDE] = kk
        kv[at, WIDE:] = v
        kt[:, at] = jnp.transpose(kk)
        vt[:, at] = jnp.transpose(v)

    def q_chunk(i, carry):
        rows = pl.ds(pl.multiple_of(i * CHUNK, CHUNK), CHUNK)
        low, high = key_range(ends, i)
        row = segr[i][0:1, :]

        acc[...] = jnp.zeros_like(acc)

        def key_chunk(j, state):
            keys = pl.ds(pl.multiple_of(j * CHUNK, CHUNK), CHUNK)
            col = segc[j]
            mask = jnp.concatenate([col, col], axis=1) == row
            new, fixes = [], []
            for h in range(HERE):
                pair = slice(128 * (h // 2), 128 * (h // 2) + 128)
                s = dot(kv[keys, pair], qm[h, rows, :], ((1,), (1,)))
                s = jnp.where(mask, s, MASKED)
                scores[h] = s
                new.append(jnp.maximum(state[h][0], jnp.max(s, axis=0, keepdims=True)))
            out = []
            for h in range(HERE):
                m, l = state[h]
                total = jnp.zeros((1, CHUNK), F32)
                for t in range(4):
                    tile = slice(64 * t, 64 * t + 64)
                    p = jnp.exp(scores[h, tile, :] - new[h])
                    total = total + jnp.sum(p, axis=0, keepdims=True)
                    probs[h, tile, :] = p.astype(BF)
                fixes.append(jnp.exp(m - new[h]))
                out.append((new[h], l * fixes[h] + total))
            for h in range(HERE):
                head = slice(h * HEAD_DIM, (h + 1) * HEAD_DIM)
                acc[head, :] = acc[head, :] * fixes[h] + dot(vt[head, keys], probs[h])
            return tuple(out)

        init = tuple(
            (jnp.full((1, CHUNK), MASKED, F32), jnp.zeros((1, CHUNK), F32)) for _ in range(HERE)
        )
        state = lax.fori_loop(low, high, key_chunk, init)
        for h in range(HERE):
            m, l = state[h]
            head = slice(h * HEAD_DIM, (h + 1) * HEAD_DIM)
            mixt[head, rows] = acc[head, :] / l
            lse[h : h + 1, rows] = m + jnp.log(l)
        return carry

    lax.fori_loop(0, 4, q_chunk, 0)
    for k, out in enumerate((m0, m1, m2, m3)):
        a = pl.multiple_of(lax.rem(z - k + 4, 4) * CHUNK, CHUNK)
        out[...] = jnp.transpose(mixt[:, pl.ds(a, CHUNK)].astype(BF))


OUT_SPEC = pl.BlockSpec((SHARDS, ROWS, 1024), lambda *a: (0, 0, 0))
QKV_SPEC = pl.BlockSpec((SHARDS, ROWS, 3 * WIDE), lambda *a: (0, 1, 0))
SMALL_SPEC = pl.BlockSpec((SHARDS, 16, 3 * WIDE), lambda *a: (0, 2 * ROWS // 16, 0))


def attn_fwd(scalars, xs, pack):
    shape = jax.ShapeDtypeStruct
    return pl.pallas_call(
        attn_fwd_kernel,
        name="attn_fwd",
        out_shape=(shape((CHUNK, WIDE), BF),) * 4
        + (
            shape((WIDE, 4 * CHUNK), F32),
            shape((8, 4 * CHUNK), F32),
            shape((HERE, 4 * CHUNK, 128), BF),
            shape((4 * CHUNK, 2 * WIDE), BF),
            shape((WIDE, 4 * CHUNK), BF),
            shape((4, CHUNK, 1024), BF),
            shape((4, 8, CHUNK), F32),
            shape((CHUNK, 128), F32),
        ),
        grid=(1,),
        in_specs=[SMEM_SPEC] + [any_spec((CHUNK + 16, 1024))] * 5 + [QKV_SPEC, SMALL_SPEC],
        out_specs=(any_spec((CHUNK, WIDE)),) * 4
        + (
            any_spec((WIDE, 4 * CHUNK)),
            any_spec((8, 4 * CHUNK)),
            any_spec((HERE, 4 * CHUNK, 128)),
            any_spec((4 * CHUNK, 2 * WIDE)),
            any_spec((WIDE, 4 * CHUNK)),
            any_spec((4, CHUNK, 1024)),
            any_spec((4, 8, CHUNK)),
            any_spec((CHUNK, 128)),
        ),
        scratch_shapes=[
            pltpu.VMEM((WIDE, 4 * CHUNK), BF),
            pltpu.VMEM((WIDE, CHUNK), F32),
            pltpu.VMEM((HERE, CHUNK, CHUNK), F32),
            pltpu.VMEM((HERE, CHUNK, CHUNK), BF),
            pltpu.VMEM((4, CHUNK, 128), F32),
            pltpu.SMEM((2, 4), jnp.int32),
        ],
        compiler_params=PARAMS,
    )(scalars, *xs, pack, pack)


def normalise(h):
    centre = h - jnp.mean(h, axis=-1, keepdims=True)
    inverse = lax.rsqrt(jnp.mean(centre * centre, axis=-1, keepdims=True) + EPSILON)
    return centre * inverse, inverse


def norm_pullback(upstream, scaled, inverse, gain):
    e = upstream * gain
    return inverse * (
        e
        - jnp.mean(e, axis=-1, keepdims=True)
        - scaled * jnp.mean(e * scaled, axis=-1, keepdims=True)
    )


def relative(f, sc):
    return 2 * jnp.bitwise_xor(sc[1], f // 2) + jnp.bitwise_xor(sc[2], f % 2)


TILE = 16


def eight(x):
    return jnp.sum(x.reshape(TILE // 8, 8, x.shape[1]), axis=0)


def out_kernel(
    sc, tok, r0, r1, r2, r3, w, small, valid, normed, low, low_rel, scaled, inv, mixed, stats, acc
):
    z = sc[0]
    for k, r in enumerate((r0, r1, r2, r3)):
        a = lax.rem(z + k, 4)
        mixed[:, pl.ds(pl.multiple_of(a * WIDE, WIDE), WIDE)] = r[...]
    acc[...] = dot(mixed[...], w[...].reshape(1024, 1024))
    bias, gain, shift_by = vec(small, 0, 256, 128), vec(small, 0, 384, 128), vec(small, 0, 512, 128)

    def tile(t, carry):
        rows = pl.ds(pl.multiple_of(t * TILE, TILE), TILE)
        branch = acc[rows, :] + bias
        x = tok[rows, :].astype(F32)
        n, inverse = normalise(x + branch)
        y = n * gain + shift_by
        normed[rows, :] = y
        low[rows, :] = y.astype(BF)
        scaled[rows, :] = n
        inv[rows, :] = jnp.broadcast_to(inverse, (TILE, 128))
        ok = valid[rows, 0:1]
        return carry[0] + eight(ok * x * x), carry[1] + eight(ok * branch * branch)

    zero = jnp.zeros((8, 1024), F32)
    stream, branch = lax.fori_loop(0, CHUNK // TILE, tile, (zero, zero), unroll=4)
    for f in range(SHARDS):
        at = pl.multiple_of(relative(f, sc) * ROWS, ROWS)
        low_rel[:, pl.ds(at, ROWS)] = low[:, ROWS * f : ROWS * f + ROWS]
    lane = lax.broadcasted_iota(jnp.int32, (8, 128), 1)
    stats[...] = jnp.where(
        lane == 0,
        jnp.sum(stream),
        jnp.where(
            lane == 1, jnp.sum(branch), jnp.where(lane == 3, jnp.sum(valid[:, 0:1]), 0.0)
        ),
    )


def out_project(scalars, tok, parts, pack, valid):
    shape = jax.ShapeDtypeStruct
    full = lambda *s: any_spec(s)
    return pl.pallas_call(
        out_kernel,
        name="out_project",
        grid=(1,),
        out_shape=(
            shape((CHUNK, 1024), F32),
            shape((CHUNK, 1024), BF),
            shape((CHUNK, 1024), BF),
            shape((CHUNK, 1024), F32),
            shape((CHUNK, 128), F32),
            shape((CHUNK, 1024), BF),
            shape((8, 128), F32),
        ),
        in_specs=[SMEM_SPEC, full(CHUNK, 1024)]
        + [full(CHUNK, WIDE)] * 4
        + [OUT_SPEC, SMALL_SPEC, full(CHUNK, 128)],
        out_specs=(
            full(CHUNK, 1024),
            full(CHUNK, 1024),
            full(CHUNK, 1024),
            full(CHUNK, 1024),
            full(CHUNK, 128),
            full(CHUNK, 1024),
            full(8, 128),
        ),
        scratch_shapes=[pltpu.VMEM((CHUNK, 1024), F32)],
        compiler_params=PARAMS,
    )(scalars, tok, *parts, pack, pack, valid)


UP_SPECS = [pl.BlockSpec((ROWS, 1024), lambda j: (0, j))] * SHARDS


def gate_kernel(low, low_rel, mixed, *refs):
    ups = refs[0:SHARDS]
    small, acts, slope, pre = refs[SHARDS:]
    j = pl.program_id(0)
    pre[...] = dot(low_rel[...], jnp.concatenate([u[...] for u in ups]))
    bias = jnp.concatenate(
        [small[2 * j + n, 1:2, 256:768].astype(F32) for n in range(2)], axis=1
    )
    for t in range(CHUNK // TILE):
        rows = slice(TILE * t, TILE * t + TILE)
        for n in range(2):
            cols = slice(512 * n, 512 * n + 512)
            gate = pre[rows, cols] + bias[:, cols]
            cdf = 0.5 * (1.0 + lax.erf(gate * (2.0 ** -0.5)))
            acts[j, rows, cols] = (gate * cdf).astype(BF)
            slope[rows, cols] = cdf + gate * (jnp.exp(-0.5 * gate * gate) * 0.3989422804014327)

    @pl.when(j == 0)
    def _():
        acts[4] = low[...]
        acts[5] = mixed[...]


def mlp_gate(low, low_rel, mixed, ups, pack):
    shape = jax.ShapeDtypeStruct
    full = lambda *s: any_spec(s)
    return pl.pallas_call(
        gate_kernel,
        name="mlp_gate",
        grid=(4,),
        out_shape=(shape((6, CHUNK, 1024), BF), shape((CHUNK, 4096), F32)),
        in_specs=[full(CHUNK, 1024)] * 3 + UP_SPECS + [SMALL_SPEC],
        out_specs=(full(6, CHUNK, 1024), pl.BlockSpec((CHUNK, 1024), lambda j: (0, j))),
        scratch_shapes=[pltpu.VMEM((CHUNK, 1024), F32)],
        compiler_params=PARAMS,
    )(low, low_rel, mixed, *ups, pack)


def mlp_tail_kernel(sc, acts, slope, small, valid, inv, *refs):
    far = refs[0 : SHARDS + 5]
    (
        out,
        grads,
        gh1,
        g0,
        g1,
        g2,
        g3,
        sums_m,
        stats,
        sums_a,
        ub,
        acc,
        gh2,
        gm,
        gg_all,
        pre,
        total,
        held,
        normed,
        cot,
        scaled,
        wout,
        rows_d,
        sems,
    ) = refs[SHARDS + 5 :]
    s = pl.program_id(0)
    z = sc[0]
    halves = [(slice(None), slice(None), slice(512 * n, 512 * n + 512)) for n in range(2)]
    targets = [rows_d.at[h] for h in halves] + [normed, cot, scaled, wout]
    targets += [held.at[n] for n in range(SHARDS)]
    sources = [far[0].at[h] for h in halves]
    sources += [far[1], far[2], far[3], far[4].at[:, 0:ROWS, :]] + list(far[5:])
    copies = [
        pltpu.make_async_copy(src, dst, sems.at[n])
        for n, (src, dst) in enumerate(zip(sources, targets))
    ]
    zero = jnp.zeros((8, 1024), F32)

    def tiles(body, count):
        totals = lax.fori_loop(0, CHUNK // TILE, body, (zero,) * count, unroll=4)
        return [jnp.sum(t, axis=0, keepdims=True) for t in totals]

    @pl.when(s == 0)
    def _():
        for copy in copies:
            copy.start()

    for n in range(2):
        pl.when(s == n)(copies[n].wait)

    @pl.when(s < 2)
    def _():
        hidden = jnp.concatenate([acts[b] for b in range(4)], axis=1)
        for n in range(2):
            cols = pl.ds(pl.multiple_of(jnp.minimum(s, 1) * 512 + 256 * n, 256), 256)
            acc[:, cols] = dot(hidden, rows_d[:, :, cols].reshape(4096, 256))

    @pl.when(s == 1)
    def _():
        for copy in copies[2:4]:
            copy.wait()
        bias, gain, shift_by = vec(small, 0, 640, 128), vec(small, 1, 0, 128), vec(small, 1, 128, 128)

        def tile(t, carry):
            rows = pl.ds(pl.multiple_of(t * TILE, TILE), TILE)
            branch = acc[rows, :] + bias
            unit, inverse = normalise(normed[rows, :] + branch)
            out[rows, :] = (unit * gain + shift_by).astype(BF)
            ok = valid[rows, 0:1]
            u = cot[rows, :].astype(F32) * ok
            g = norm_pullback(u, unit, inverse, gain)
            gh2[rows, :] = g
            g_low = g.astype(BF)
            gm[rows, :] = g_low
            terms = (u * unit, u, g_low.astype(F32), ok * branch * branch)
            return tuple(c + eight(v) for c, v in zip(carry, terms))

        totals = tiles(tile, 4)
        sums_m[...] = jnp.zeros_like(sums_m)
        for at in range(3):
            sums_m[at : at + 1, :] = totals[at]
        lane = lax.broadcasted_iota(jnp.int32, (8, 128), 1)
        stats[...] = jnp.where(lane == 2, jnp.sum(totals[3]), 0.0)

    @pl.when((s >= 2) & (s < 6))
    def _():
        j = jnp.clip(s - 2, 0, 3)
        pre[...] = dot(gm[...], rows_d[pl.ds(2 * j, 2)].reshape(1024, 1024), ((1,), (1,)))
        for n in range(2):
            cols = slice(512 * n, 512 * n + 512)
            total_ub = jnp.zeros((8, 512), F32)
            for t in range(CHUNK // TILE):
                rows = slice(TILE * t, TILE * t + TILE)
                gg = (pre[rows, cols] * slope[rows, cols]).astype(BF)
                gg_all[j, rows, cols] = gg
                grads[0, rows, cols] = gg
                total_ub = total_ub + eight(gg.astype(F32))
            row = jnp.sum(total_ub, axis=0, keepdims=True)
            for q in range(4):
                to = pl.ds(pl.multiple_of((2 * j + n) * 128, 128), 128)
                ub[q : q + 1, to] = row[:, 128 * q : 128 * q + 128]

    @pl.when(s == 6)
    def _():
        grads[0] = gm[...]
        for copy in copies[4:]:
            copy.wait()

    @pl.when(s >= 6)
    def _():
        gg = jnp.concatenate([gg_all[b] for b in range(4)], axis=1)
        for m in range(2):
            j = jnp.clip(2 * (s - 6) + m, 0, 3)
            rows = held[pl.ds(2 * j, 2)].reshape(2 * ROWS, 4096)
            part = dot(gg, rows, ((1,), (1,)))
            pair = jnp.bitwise_xor(sc[1], j)
            for t in range(2):
                f = 2 * pair + jnp.bitwise_xor(sc[2], t)
                to = pl.ds(pl.multiple_of(f * ROWS, ROWS), ROWS)
                total[:, to] = part[:, ROWS * t : ROWS * t + ROWS]

    @pl.when(s == 7)
    def _():
        gain = vec(small, 0, 384, 128)

        def tile(t, carry):
            rows = pl.ds(pl.multiple_of(t * TILE, TILE), TILE)
            u = gh2[rows, :] + total[rows, :]
            n = scaled[rows, :]
            g = norm_pullback(u, n, inv[rows, 0:1], gain)
            gh1[rows, :] = g
            g_low = g.astype(BF)
            grads[0, rows, :] = g_low
            terms = (u * n, u, g_low.astype(F32))
            return tuple(c + eight(v) for c, v in zip(carry, terms))

        totals = tiles(tile, 3)
        sums_a[...] = jnp.zeros_like(sums_a)
        for at in range(3):
            sums_a[at : at + 1, :] = totals[at]
        g_low = grads[0]
        for k, g_out in enumerate((g0, g1, g2, g3)):
            a = lax.rem(z + k, 4)
            rows = wout[pl.ds(2 * a, 2)].reshape(WIDE, 1024)
            g_out[...] = dot(g_low, rows, ((1,), (1,))).astype(BF)


def mlp_tail(scalars, acts, slope, ups, down, normed, scaled, inv, pack, cot, valid):
    shape = jax.ShapeDtypeStruct
    full = lambda *s: any_spec(s)
    block = lambda s: jnp.clip(s - 2, 0, 3)

    def grads_at(s):
        return (jnp.where(s < 6, block(s), jnp.where(s < 7, 5, 4)), 0, 0)

    return pl.pallas_call(
        mlp_tail_kernel,
        name="mlp_tail",
        grid=(8,),
        in_specs=[
            SMEM_SPEC,
            full(4, CHUNK, 1024),
            pl.BlockSpec((CHUNK, 1024), lambda s: (0, block(s))),
            SMALL_SPEC,
            full(CHUNK, 128),
            full(CHUNK, 128),
        ]
        + [pl.BlockSpec(memory_space=pl.ANY)] * (SHARDS + 5),
        out_specs=(
            full(CHUNK, 1024),
            pl.BlockSpec((1, CHUNK, 1024), grads_at),
            full(CHUNK, 1024),
        )
        + (full(CHUNK, WIDE),) * 4
        + (full(8, 1024), full(8, 128), full(8, 1024), full(4, 1024)),
        out_shape=(
            shape((CHUNK, 1024), BF),
            shape((6, CHUNK, 1024), BF),
            shape((CHUNK, 1024), F32),
        )
        + (shape((CHUNK, WIDE), BF),) * 4
        + (
            shape((8, 1024), F32),
            shape((8, 128), F32),
            shape((8, 1024), F32),
            shape((4, 1024), F32),
        ),
        scratch_shapes=[
            pltpu.VMEM((CHUNK, 1024), F32),
            pltpu.VMEM((CHUNK, 1024), F32),
            pltpu.VMEM((CHUNK, 1024), BF),
            pltpu.VMEM((4, CHUNK, 1024), BF),
            pltpu.VMEM((CHUNK, 1024), F32),
            pltpu.VMEM((CHUNK, 1024), F32),
            pltpu.VMEM((SHARDS, ROWS, 4096), BF),
            pltpu.VMEM((CHUNK, 1024), F32),
            pltpu.VMEM((CHUNK, 1024), BF),
            pltpu.VMEM((CHUNK, 1024), F32),
            pltpu.VMEM((SHARDS, ROWS, 1024), BF),
            pltpu.VMEM((SHARDS, 512, 1024), BF),
            pltpu.SemaphoreType.DMA((SHARDS + 6,)),
        ],
        compiler_params=PARAMS,
    )(scalars, acts, slope, pack, valid, inv, down, normed, cot, scaled, pack, *ups)


REST = 640


def product(left, right, res):
    for n in range(4):
        cols = slice(256 * n, 256 * n + 256)
        res[:, cols] = dot(left[...], right[:, cols]).astype(BF)


def down_kernel(count, sc, ho, hp, go, gp, *refs):
    outs = refs[0:count]
    left, right, res = refs[count:]
    s = pl.program_id(0)

    @pl.when(s == 0)
    def _():
        right[0:CHUNK] = go[0]
        right[CHUNK:] = gp[0]

    left[:, 0:CHUNK] = jnp.transpose(ho[0])
    left[:, CHUNK:] = jnp.transpose(hp[0])
    product(left, right, res)
    for n, out in enumerate(outs):

        @pl.when(s == n)
        def _():
            out[...] = res[...]


def down_grads(scalars, acts, acts_p, grads, grads_p, distances):
    shape = jax.ShapeDtypeStruct
    full = lambda *s: pl.BlockSpec(s, lambda j, sc: (0,) * len(s))
    first, count = distances[0], len(distances)

    def hid(j, sc):
        f = 2 * jnp.bitwise_xor(sc[1], first + j) + sc[2]
        return (f // 2, 0, f % 2)

    hidden = pl.BlockSpec((1, CHUNK, 512), hid)
    grad = pl.BlockSpec((1, CHUNK, 1024), lambda j, sc: (5, 0, 0))
    return pl.pallas_call(
        partial(down_kernel, count),
        name="down_grads",
        grid_spec=pltpu.PrefetchScalarGridSpec(
            num_scalar_prefetch=1,
            grid=(count,),
            in_specs=[hidden, hidden, grad, grad],
            out_specs=(full(512, 1024),) * count,
            scratch_shapes=[
                pltpu.VMEM((512, 2 * CHUNK), BF),
                pltpu.VMEM((2 * CHUNK, 1024), BF),
                pltpu.VMEM((512, 1024), BF),
            ],
        ),
        out_shape=(shape((512, 1024), BF),) * count,
        compiler_params=PARAMS,
    )(scalars, acts, acts_p, grads, grads_p)


def rest_kernel(sc, lo, lp, go, gp, r3, r1, r2, r0, low_sel, mix_sel, right, res):
    s = pl.program_id(0)
    chip, core = sc[1], sc[2]

    @pl.when(s == 0)
    def _():
        for r in range(4):
            at = pl.multiple_of((2 * jnp.bitwise_xor(chip, r) + core) * ROWS, ROWS)
            to = slice(ROWS * r, ROWS * r + ROWS)
            for n, out in enumerate((low_sel, mix_sel)):
                out[to, 0:CHUNK] = jnp.transpose(lo[n, :, pl.ds(at, ROWS)])
                out[to, CHUNK:] = jnp.transpose(lp[n, :, pl.ds(at, ROWS)])

    @pl.when(s == 4)
    def _():
        low_sel[...] = mix_sel[...]

    right[0:CHUNK] = go[0]
    right[CHUNK:] = gp[0]
    product(low_sel, right, res)
    for r, out in enumerate((r0, r1, r2, r3)):
        out[...] = res[ROWS * r : ROWS * r + ROWS, :]


def rest_grads(scalars, acts, acts_p, grads, grads_p):
    shape = jax.ShapeDtypeStruct
    full = lambda *s: pl.BlockSpec(s, lambda j, sc: (0,) * len(s))
    flat = pl.BlockSpec((pl.Element(2), pl.Element(CHUNK), pl.Element(1024)), lambda j, sc: (4, 0, 0))
    grad = pl.BlockSpec((1, CHUNK, 1024), lambda j, sc: (j, 0, 0))
    return pl.pallas_call(
        rest_kernel,
        name="rest_grads",
        grid_spec=pltpu.PrefetchScalarGridSpec(
            num_scalar_prefetch=1,
            grid=(5,),
            in_specs=[flat, flat, grad, grad],
            out_specs=(pl.BlockSpec((ROWS, 1024), lambda j, sc: (j, 0)),) * 4,
            scratch_shapes=[
                pltpu.VMEM((512, 2 * CHUNK), BF),
                pltpu.VMEM((512, 2 * CHUNK), BF),
                pltpu.VMEM((2 * CHUNK, 1024), BF),
                pltpu.VMEM((512, 1024), BF),
            ],
        ),
        out_shape=(shape((REST, 1024), BF),) * 4,
        compiler_params=PARAMS,
    )(scalars, acts, acts_p, grads, grads_p)


def attn_bwd_kernel(
    sc,
    segr,
    w,
    qm,
    kv,
    kt,
    mixt,
    lse,
    g0,
    g1,
    g2,
    g3,
    ig,
    dall,
    segc,
    ends,
    gs,
    dq,
    dqt,
    dk,
    dv,
    delta,
    scores,
    slopes,
    probs,
    pulls,
):
    z = sc[0]
    segment_setup(segr, segc, ends)
    dk[...] = jnp.zeros_like(dk)
    dv[...] = jnp.zeros_like(dv)
    for k, g in enumerate((g0, g1, g2, g3)):
        rows = pl.ds(pl.multiple_of(lax.rem(z - k + 4, 4) * CHUNK, CHUNK), CHUNK)
        turned = jnp.transpose(g[...])
        for h in range(HERE):
            head = slice(h * HEAD_DIM, (h + 1) * HEAD_DIM)
            gs[h, rows, :] = one_head(g[...], h)
            prod = turned[head, :].astype(F32) * mixt[head, rows]
            delta[h : h + 1, rows] = jnp.sum(prod, axis=0, keepdims=True)

    def q_chunk(i, carry):
        rows = pl.ds(pl.multiple_of(i * CHUNK, CHUNK), CHUNK)
        low, high = key_range(ends, i)
        row = segr[i][0:1, :]
        dqt[...] = jnp.zeros_like(dqt)

        def key_chunk(j, inner):
            keys = pl.ds(pl.multiple_of(j * CHUNK, CHUNK), CHUNK)
            col = segc[j]
            mask = jnp.concatenate([col, col], axis=1) == row
            for h in range(HERE):
                low_lane = 128 * (h // 2)
                pair = slice(low_lane, low_lane + 128)
                scores[h] = dot(kv[keys, pair], qm[h, rows, :], ((1,), (1,)))
                wide = slice(WIDE + low_lane, WIDE + low_lane + 128)
                slopes[h] = dot(kv[keys, wide], gs[h, rows, :], ((1,), (1,)))
            for h in range(HERE):
                log, shift_by = lse[h : h + 1, rows], delta[h : h + 1, rows]
                for t in range(4):
                    tile = slice(64 * t, 64 * t + 64)
                    p = jnp.where(mask[tile, :], jnp.exp(scores[h, tile, :] - log), 0.0)
                    probs[h, tile, :] = p.astype(BF)
                    pulls[h, tile, :] = (p * (slopes[h, tile, :] - shift_by)).astype(BF)
            for h in range(HERE):
                head = slice(h * HEAD_DIM, (h + 1) * HEAD_DIM)
                pair = slice(128 * (h // 2), 128 * (h // 2) + 128)
                dv[keys, pair] += dot(probs[h], gs[h, rows, :])
                dk[keys, pair] += dot(pulls[h], qm[h, rows, :])
                dqt[head, :] += dot(kt[head, keys], pulls[h])
            return inner

        lax.fori_loop(low, high, key_chunk, 0)
        dq[...] = (dqt[...] * SCALE).astype(BF)
        dall[rows, 0:WIDE] = jnp.transpose(dq[...])
        return carry

    lax.fori_loop(0, 4, q_chunk, 0)
    dall[:, WIDE : 2 * WIDE] = dk[...].astype(BF)
    dall[:, 2 * WIDE :] = dv[...].astype(BF)
    weight = w[...].reshape(SHARDS * ROWS, 3 * WIDE)
    for k in range(4):
        rows = slice(CHUNK * k, CHUNK * k + CHUNK)
        ig[rows, :] = dot(dall[rows, :], weight, ((1,), (1,))).astype(BF)


def qkv_kernel(sc, xall, dall, sums_m, sums_a, ubt, stats_a, stats_m, out, small, acc):
    z = sc[0]
    for k in range(4):
        part = dot(xall[k], dall[CHUNK * k : CHUNK * k + CHUNK, :], ((0,), (0,)))
        if k == 0:
            acc[...] = part
        else:
            acc[...] += part
    out[:, 0 : 3 * WIDE] = acc[...].astype(BF)
    here = pl.ds(pl.multiple_of(z * WIDE, WIDE), WIDE)
    small[...] = jnp.zeros_like(small)
    small[0:3, :] = sums_m[0:3, :]
    small[3:6, :] = sums_a[0:3, :]
    small[6:7, here] = jnp.sum(dall[:, 0:WIDE].astype(F32), axis=0, keepdims=True)
    small[7:8, here] = jnp.sum(dall[:, 2 * WIDE :].astype(F32), axis=0, keepdims=True)
    small[8:12, :] = ubt[...]
    every = lambda value: jnp.broadcast_to(value, (1, 1024))
    small[12:13, :] = every(stats_a[0:1, 0:1])
    small[13:14, :] = every(stats_a[0:1, 1:2])
    small[14:15, :] = every(stats_m[0:1, 2:3])
    count = stats_a[0:1, 3:4]
    high = jnp.floor(count * 0.0625)
    small[15:16, :] = every(high)
    small[16:17, :] = every(count - 16.0 * high)
    out[:, 3 * WIDE :] = jnp.transpose(small[...]).astype(BF)


def qkv_grads(scalars, xall, dall, smalls):
    return pl.pallas_call(
        qkv_kernel,
        name="qkv_grads",
        out_shape=jax.ShapeDtypeStruct((1024, 3 * WIDE + 128), BF),
        in_specs=[SMEM_SPEC] + [VMEM_SPEC] * 7,
        out_specs=VMEM_SPEC,
        scratch_shapes=[pltpu.VMEM((128, 1024), F32), pltpu.VMEM((1024, 3 * WIDE), F32)],
        compiler_params=PARAMS,
    )(scalars, xall, dall, *smalls)


def attn_bwd(scalars, segr, pack, qm, kv, kt, mixt, lse, gs):
    shape = jax.ShapeDtypeStruct
    return pl.pallas_call(
        attn_bwd_kernel,
        name="attn_bwd",
        out_shape=(shape((1024, 1024), BF), shape((1024, 3 * WIDE), BF)),
        grid=(1,),
        in_specs=[SMEM_SPEC]
        + [
            any_spec((4, 8, CHUNK)),
            QKV_SPEC,
            any_spec((HERE, 4 * CHUNK, 128)),
            any_spec((4 * CHUNK, 2 * WIDE)),
            any_spec((WIDE, 4 * CHUNK)),
            any_spec((WIDE, 4 * CHUNK)),
            any_spec((8, 4 * CHUNK)),
        ]
        + [any_spec((CHUNK, WIDE))] * 4,
        out_specs=(any_spec((1024, 1024)), any_spec((1024, 3 * WIDE))),
        scratch_shapes=[
            pltpu.VMEM((4, CHUNK, 128), F32),
            pltpu.SMEM((2, 4), jnp.int32),
            pltpu.VMEM((HERE, 4 * CHUNK, 128), BF),
            pltpu.VMEM((WIDE, CHUNK), BF),
            pltpu.VMEM((WIDE, CHUNK), F32),
            pltpu.VMEM((4 * CHUNK, WIDE), F32),
            pltpu.VMEM((4 * CHUNK, WIDE), F32),
            pltpu.VMEM((8, 4 * CHUNK), F32),
            pltpu.VMEM((HERE, CHUNK, CHUNK), F32),
            pltpu.VMEM((HERE, CHUNK, CHUNK), F32),
            pltpu.VMEM((HERE, CHUNK, CHUNK), BF),
            pltpu.VMEM((HERE, CHUNK, CHUNK), BF),
        ],
        compiler_params=PARAMS,
    )(scalars, segr, pack, qm, kv, kt, mixt, lse, *gs)


def finish_kernel(sc, *refs):
    z = sc[0]
    pieces, (gq, gk, gv), vectors, ub, rms = refs[0:4], refs[4:7], refs[7:15], refs[15], refs[16:19]
    for k, piece in enumerate(pieces):
        cols = pl.ds(pl.multiple_of(lax.rem(z - k + 4, 4) * WIDE, WIDE), WIDE)
        for n, out in enumerate((gq, gk, gv)):
            out[:, cols] = piece[:, WIDE * n : WIDE * n + WIDE].astype(F32)
    extra = pieces[0][:, 3 * WIDE :].astype(F32)
    for piece in pieces[1:]:
        extra = extra + piece[:, 3 * WIDE :].astype(F32)
    extra = jnp.transpose(extra)
    for n, out in enumerate(vectors):
        out[...] = extra[n : n + 1, :]
    ub[...] = extra[8:12, :]
    counted = (16.0 * extra[15:16, 0:1] + extra[16:17, 0:1]) * 1024.0
    for n, out in enumerate(rms):
        out[...] = jnp.sqrt(extra[12 + n : 13 + n, 0:1] / counted)


def finish(scalars, pieces):
    shape = jax.ShapeDtypeStruct
    shapes = [(ROWS, 1024)] * 3 + [(1, ROWS)] * 8 + [(4, ROWS)] + [(1, 1)] * 3
    return pl.pallas_call(
        finish_kernel,
        name="finish",
        out_shape=tuple(shape(n, F32) for n in shapes),
        in_specs=[SMEM_SPEC] + [VMEM_SPEC] * 4,
        out_specs=(VMEM_SPEC,) * len(shapes),
        compiler_params=PARAMS,
    )(scalars, *pieces)


def line_gather(x):
    right = lax.ppermute(x, "ctx", [(0, 1), (1, 2), (2, 3)])
    left = lax.ppermute(x, "ctx", [(1, 0), (2, 1), (3, 2)])
    two = lax.ppermute(x, "ctx", [(0, 2), (1, 3), (2, 0), (3, 1)])
    return [x, right, left, two]


def line_forward(two):
    return lax.ppermute(two, "ctx", [(1, 0), (2, 3)])


def shift(x, k):
    n = lax.axis_size("ctx")
    return lax.ppermute(x, "ctx", [(i, (i + k) % n) for i in range(n)])


def swap(x, bits):
    return lax.ppermute(x, "fsdp", [(i, i ^ bits) for i in range(lax.axis_size("fsdp"))])


def add(*terms):
    total = terms[0].astype(F32)
    for term in terms[1:]:
        total = total + term.astype(F32)
    return total


def neighbour(x, bits):
    return lax.ppermute(x, "ctx", [(i, i ^ bits) for i in range(4)])


def half_sum(terms, which):
    half = terms[0].shape[0] // 2
    return add(*[lax.dynamic_slice_in_dim(t, which * half, half, 0) for t in terms])


class LineSum:
    def __init__(self, *terms):
        self.terms = terms
        self.odd = lax.axis_index("ctx") % 2

    def first(self):
        return half_sum(self.terms, 1 - self.odd).astype(BF)

    def second(self, got):
        self.pair = add(half_sum(self.terms, self.odd), got).astype(BF)
        return self.pair

    def third(self, got):
        self.whole = add(self.pair, got).astype(BF)
        return self.whole

    def result(self, got):
        even = self.odd == 0
        low = jnp.where(even, self.whole, got)
        return jnp.concatenate([low, jnp.where(even, got, self.whole)]).astype(F32)


def line_sum(*terms):
    parts = LineSum(*terms)
    got = neighbour(parts.first(), 1)
    got = neighbour(parts.second(got), 2)
    return parts.result(neighbour(parts.third(got), 1))


def per_device(
    tokens,
    segment_ids,
    cotangent,
    query_weight,
    query_bias,
    key_weight,
    value_weight,
    value_bias,
    out_weight,
    out_bias,
    attn_gain,
    attn_shift,
    up_weight,
    up_bias,
    down_weight,
    down_bias,
    mlp_gain,
    mlp_shift,
):
    owners = lax.axis_size("fsdp")
    plane = owners == SHARDS
    z = lax.axis_index("ctx")
    f = lax.axis_index("fsdp")
    if plane:
        chip, core = f // 2, f % 2
    else:
        chip, core = jnp.int32(0), jnp.int32(0)
    scalars = jnp.stack([z, chip, core, z]).astype(jnp.int32)
    tok = tokens[0]
    if plane:
        weights = (query_weight, key_weight, value_weight, out_weight)
        vectors = (query_bias, value_bias, out_bias, attn_gain, attn_shift, down_bias)
        vectors += (mlp_gain, mlp_shift, up_bias)
        packed, mine_pack = pack_inputs(scalars, tok, segment_ids, weights, vectors)
        pack = lax.all_gather(mine_pack, "fsdp", axis=0)
        xs = line_gather(packed)
        xs.append(line_forward(xs[3]))
        near_x, near_y = swap(up_weight, 2), swap(up_weight, 4)
        half = up_weight.shape[1] // 2
        far = [swap(near_x[:, :half], 4), swap(near_y[:, half:], 2)]
        xs, near_x, near_y, after, pack = lax.optimization_barrier(
            (xs, near_x, near_y, down_weight, pack)
        )
        down = lax.all_gather(after, "fsdp", axis=0)
    else:
        seg_row = jnp.pad(segment_ids.astype(BF), ((0, 15), (0, 1024 - CHUNK)))
        packed = jnp.concatenate([tok, seg_row])
        xs = line_gather(packed)
        xs.append(line_forward(xs[3]))
        quarter = jnp.concatenate(
            [
                lax.dynamic_slice_in_dim(m, z * WIDE, WIDE, 1)
                for m in (query_weight, key_weight, value_weight)
            ],
            axis=1,
        )
        whole = lambda m: lax.all_gather(m, "fsdp", axis=0, tiled=True)
        split = lambda m: whole(m).reshape(SHARDS, -1)
        line0 = jnp.concatenate(
            [split(m) for m in (query_bias, value_bias, out_bias, attn_gain, attn_shift, down_bias)],
            axis=1,
        )
        line1 = jnp.concatenate([split(m) for m in (mlp_gain, mlp_shift, up_bias)], axis=1)
        lines = jnp.pad(jnp.stack([line0, line1], axis=1), ((0, 0), (0, 14), (0, 0)))
        pack = jnp.concatenate([whole(quarter).reshape(SHARDS, ROWS, 768), lines], axis=1)
        out_rows = whole(out_weight).reshape(SHARDS, ROWS, 1024)
        wide = lambda m: jnp.pad(m, ((0, 0), (0, 0), (0, 1024 - m.shape[2])))
        pack = jnp.concatenate([out_rows, wide(pack)], axis=1)
        ups = list(whole(up_weight).reshape(SHARDS, ROWS, 4096))
        down = whole(down_weight).reshape(SHARDS, 512, 1024)

    m0, m1, m2, m3, mixt, lse, qm, kv, kt, xall, segr, valid = attn_fwd(scalars, xs, pack)
    parts = [m0] + [shift(m, -k) for k, m in ((1, m1), (2, m2), (3, m3))]
    if plane:
        ups = [up_weight, swap(up_weight, 1)]
        far, _ = lax.optimization_barrier((far, m0))
        far = jnp.concatenate(far, axis=1)
        parts, near_x, near_y, far = lax.optimization_barrier((parts, near_x, near_y, far))
        for rows in (near_x, near_y, far):
            ups += [rows, swap(rows, 1)]
    normed, low, low_rel, scaled, inv, mixed, stats_a = out_project(
        scalars, tok, parts, pack, valid
    )
    acts, slope = mlp_gate(low, low_rel, mixed, ups, pack)
    acts_p = swap(acts, 1)
    result, grads, gh1, g0, g1, g2, g3, sums_m, stats_m, sums_a, ub = mlp_tail(
        scalars, acts, slope, ups, down, normed, scaled, inv, pack, cotangent[0], valid
    )
    gs = [g0] + [shift(g, k) for k, g in ((1, g1), (2, g2), (3, g3))]
    grads_p = swap(grads, 1)
    (d3,) = down_grads(scalars, acts, acts_p, grads, grads_p, (3,))
    d0, d1, d2 = down_grads(scalars, acts, acts_p, grads, grads_p, (0, 1, 2))
    if plane:
        d_far = swap(d3, 2)
    r3, r1, r2, r0 = rest_grads(scalars, acts, acts_p, grads, grads_p)
    gs, r3, r1, r2, r0 = lax.optimization_barrier((gs, r3, r1, r2, r0))
    if plane:
        r_far = swap(r3, 4)
    if not plane:
        ub = ub.reshape(4, SHARDS, 128).swapaxes(0, 1).reshape(1024, 4).T
    smalls = (sums_m, sums_a, ub, stats_a, stats_m)
    ig, dall = attn_bwd(scalars, segr, pack, qm, kv, kt, mixt, lse, gs)
    tie = lax.optimization_barrier
    if plane:
        ig, dall, d_far, r_far = tie((ig, dall, d_far, r_far))
    ig = lax.psum_scatter(ig, "ctx", scatter_dimension=0, tiled=True)
    if plane:
        to_x = add(r1, r_far).astype(BF)
        to_x, r2, dall, d_far = tie((to_x, r2, dall, d_far))
        r_from_x, r_from_y = swap(to_x, 2), swap(r2, 4)
    gw = qkv_grads(scalars, xall, dall, smalls)
    if plane:
        to_y = add(d2, d_far).astype(BF)
        r_sum = LineSum(r0, r_from_x, r_from_y)
        r_first, gw, to_y, d1 = tie((r_sum.first(), gw, to_y, d1))
        d_from_x, d_from_y = swap(d1, 2), swap(to_y, 4)
        got_r = neighbour(r_first, 1)
        ig, gw, d_from_x, d_from_y, got_r = tie((ig, gw, d_from_x, d_from_y, got_r))
    q_own = lax.psum_scatter(gw, "fsdp", scatter_dimension=0, tiled=True)
    q_low = q_own.astype(BF)

    if plane:
        d_from_x, d_from_y, got_r = tie((d_from_x, d_from_y, got_r))
        got_r = neighbour(r_sum.second(got_r), 2)
        d_sum = LineSum(d0, d_from_x, d_from_y)
        got = neighbour(d_sum.first(), 1)
        r_third = r_sum.third(got_r)
        got_r = neighbour(r_third, 1)
        got, _ = tie((got, r_third))
        d_second = d_sum.second(got)
        got = neighbour(d_second, 2)
        q_low, _ = tie((q_low, d_second))
        q_pieces = [q_low] + [shift(q_low, k) for k in (1, 2, 3)]
        got, got_r, q_pieces = tie((got, got_r, q_pieces))
        rest = r_sum.result(got_r)
        grad_down = d_sum.result(neighbour(d_sum.third(got), 1))
        input_grad = add(gh1, ig)
        grad_up = jnp.concatenate([rest[ROWS * b : ROWS * b + ROWS] for b in range(4)], axis=1)
        grad_out = rest[4 * ROWS :]
    else:
        other = scalars.at[2].set(1)
        sums_w = (d3, d1, d2, d0, r3, r1, r2, r0)
        e0, e1, e2, e3 = down_grads(other, acts, acts_p, grads, grads_p, (0, 1, 2, 3))
        second = (e3, e1, e2, e0)
        second += rest_grads(other, acts, acts_p, grads, grads_p)
        rows_of = lambda t: ([t[3], t[1], t[2], t[0]], [t[7], t[5], t[6], t[4]])
        down_0, rest_0 = rows_of(sums_w)
        down_1, rest_1 = rows_of(second)
        down_all = 0.5 * jnp.stack([m.astype(F32) for p in zip(down_0, down_1) for m in p])
        rest_all = 0.5 * jnp.stack([m.astype(F32) for p in zip(rest_0, rest_1) for m in p])
        scatter = lambda m: lax.psum_scatter(
            m.astype(BF), "fsdp", scatter_dimension=0, tiled=True
        )
        grad_down = line_sum(scatter(down_all.reshape(4096, 1024)))
        grad_up = line_sum(
            scatter(
                rest_all[:, 0:512]
                .reshape(SHARDS, 4, ROWS, 1024)
                .swapaxes(1, 2)
                .reshape(1024, 4096)
            )
        )
        grad_out = line_sum(scatter(rest_all[:, 512:].reshape(1024, 1024)))
        q_pieces = [q_low] + [shift(q_low, k) for k in (1, 2, 3)]
        input_grad = add(gh1, ig)
    if plane:
        done = finish(scalars, q_pieces)
        grad_q, grad_k, grad_v = done[0:3]
        vectors = [v.reshape(-1) for v in done[3:11]]
        up_bias_grad = done[11].reshape(-1)
        rms = [v.reshape(()) for v in done[12:15]]
    else:
        table = jnp.take(jnp.stack(q_pieces), (z - jnp.arange(4)) % 4, axis=0)
        extra = add(*q_pieces)[:, 3 * WIDE :]
        cols = lambda n: jnp.concatenate(
            [table[a, :, n * WIDE : (n + 1) * WIDE].astype(F32) for a in range(4)], axis=1
        )
        grad_q, grad_k, grad_v = cols(0), cols(1), cols(2)
        vectors = [extra[:, n] for n in range(8)]
        up_bias_grad = extra[:, 8:12].reshape(-1)
        counted = (16.0 * extra[0, 15] + extra[0, 16]) * 1024
        rms = [jnp.sqrt(extra[0, 12 + n] / counted) for n in range(3)]
    return (
        result[None],
        input_grad[None],
        grad_q,
        vectors[6],
        grad_k,
        grad_v,
        vectors[7],
        grad_out,
        vectors[5],
        vectors[3],
        vectors[4],
        grad_up,
        up_bias_grad,
        grad_down,
        vectors[2],
        vectors[0],
        vectors[1],
        rms[0],
        rms[1],
        rms[2],
    )


def solution(mesh):
    matrix, vector = P("fsdp", None), P("fsdp")
    stream = P("fsdp", "ctx", None)
    placed = (
        stream,
        P("fsdp", "ctx"),
        stream,
        matrix,
        vector,
        matrix,
        matrix,
        vector,
        matrix,
        vector,
        vector,
        vector,
        matrix,
        vector,
        matrix,
        vector,
        vector,
        vector,
    )
    return jax.shard_map(
        per_device,
        mesh=mesh,
        in_specs=placed,
        out_specs=(
            stream,
            stream,
            matrix,
            vector,
            matrix,
            matrix,
            vector,
            matrix,
            vector,
            vector,
            vector,
            matrix,
            vector,
            matrix,
            vector,
            vector,
            vector,
            P(),
            P(),
            P(),
        ),
        check_vma=False,
    )
```
